512 devices in a mesh: ens: 16 (over x, y_hi, core), pix: 32 (over y_lo, z).
Axes of the slice: x: 4, y: 4 (y_hi: 2, y_lo: 2; y = y_hi * 2 + y_lo), z: 16, core: 2. Of those that a mesh axis runs over, the one named last changes fastest.
Arguments:
- sample_layer_feed: bfloat16 [16, 4096, 1024], P('ens', 'pix'), may hold values from -54 to 54
- gain: float32 [1024], replicated, may hold values from 0.1 to 1.9
- w_query: bfloat16 [1024, 512], P('ens'), may hold values from -15 to 15
- w_key: bfloat16 [1024, 512], P('ens'), may hold values from -0.1875 to 0.1875
- w_value: bfloat16 [1024, 512], P('ens'), may hold values from -0.1875 to 0.1875
- w_out: bfloat16 [512, 1024], P(None, 'ens'), may hold values from -0.25 to 0.25
- readout_matrix: bfloat16 [1024, 128], replicated, may hold values from -0.1875 to 0.1875
- target: float32 [4096, 128], P('pix'), may hold values from -6 to 6
- pixel_weight: float32 [4096], P('pix'), may hold values from 0.25 to 6
- pix_mask: int32 [4096], replicated, may hold values from 0 to 1, as said below
- neighbours: int32 [32, 9], P('pix'), may hold values from 0 to 31, as said below
- neighbour_mask: int32 [32, 9], P('pix'), may hold values from 0 to 1, as said below
Outputs:
- loss: float32 [], replicated
- grad_w_out: float32 [512, 1024], P(None, 'ens')
- grad_w_value: float32 [1024, 512], P('ens')
The draws below stay inside these ranges and needn't reach their ends.
Inputs may be any that keep to these rules, and one draw needn't show every extreme that they name: `neighbours`: slot 0 of tile t names t itself; every slot names tile t, t - 1 or t + 1 (the tiles of the same and the neighbouring pix devices). `neighbour_mask`: slot 0 is live in every tile. `pix_mask`: in every tile the real pixels come first, and they are half of the tile or more.
All inputs are finite; a program needn't handle non-finite values.
Results may differ from the reference program's by a relative error of at most 0.025.
The reference program's roundings to bfloat16 on the way count: a program that leaves them out, or rounds other values in their place, can miss the bound.
Values may be sent and summed in bfloat16 or wider, within the bound.
A program may use at most 64 MiB of HBM per device.

```python
import math
import jax
import jax.numpy as jnp
from jax import lax

D = 1024
HEADS = 8
HD = 64
VARS = 128
TILE = 128
NB = 9
PIX_DEV = 128
INNER = 512
MEMBERS = 16
PIX = 4096
TILES = 32


def neighbour_table(key):
    blocks = PIX_DEV // TILE
    span_tiles = 3 * blocks
    tile_ids = jnp.arange(TILES, dtype=jnp.int32)
    block_ids = tile_ids // blocks
    offsets = jnp.arange(span_tiles, dtype=jnp.int32)
    candidate = (block_ids[:, None] - 1) * blocks + offsets[None, :]
    usable_all = (candidate >= 0) & (candidate < TILES) & (candidate != tile_ids[:, None])
    ranking = jax.random.randint(key, (TILES, span_tiles), 0, 4096, dtype=jnp.int32) * span_tiles + offsets[None, :]
    ranking = jnp.where(usable_all, ranking, 4096 * span_tiles + offsets[None, :])
    order = jnp.argsort(ranking, axis=1)
    taken = min(NB - 1, span_tiles)
    picked = jnp.take_along_axis(candidate, order[:, :taken], axis=1)
    usable = jnp.take_along_axis(usable_all, order[:, :taken], axis=1)
    if taken < NB - 1:
        picked = jnp.concatenate([picked, jnp.broadcast_to(tile_ids[:, None], (TILES, NB - 1 - taken))], axis=1)
        usable = jnp.concatenate([usable, jnp.zeros((TILES, NB - 1 - taken), dtype=bool)], axis=1)
    picked = jnp.where(usable, picked, tile_ids[:, None])
    extra = jax.random.randint(jax.random.fold_in(key, 3), (TILES, NB - 1), 0, 8, dtype=jnp.int32) > 0
    live_slots = (usable & extra).astype(jnp.int32)
    table = jnp.concatenate([tile_ids[:, None], picked], axis=1).astype(jnp.int32)
    slot_mask = jnp.concatenate([jnp.ones((TILES, 1), jnp.int32), live_slots], axis=1)
    return (table, slot_mask)


def draw_neighbours(key, part):
    return neighbour_table(jax.random.fold_in(key, 11))[0]


def draw_neighbour_mask(key, part):
    return neighbour_table(jax.random.fold_in(key, 11))[1]


def draw_pix_mask(key, part):
    live_count = jax.random.randint(jax.random.fold_in(key, 5), (TILES,), TILE // 2, TILE + 1, dtype=jnp.int32)
    position = jnp.arange(TILE, dtype=jnp.int32)
    return (position[None, :] < live_count[:, None]).astype(jnp.int32).reshape(PIX)


def draw_pixel_weight(key, part):
    position = jnp.arange(PIX, dtype=jnp.float32)
    ramp = 1.0 + 2.0 * position / (PIX - 1)
    factor = jax.random.uniform(jax.random.fold_in(key, 2), (PIX,), jnp.float32, 0.5, 1.5)
    return (ramp * factor).astype(jnp.float32)


def draw_w_query(key, part):
    base = jnp.clip(jax.random.normal(jax.random.fold_in(key, 1), (D, INNER), jnp.float32), -4.0, 4.0) * D ** (-0.5)
    return base.astype(jnp.bfloat16)


def draw_sample_layer_feed(key, part):
    member_pos = jnp.arange(MEMBERS, dtype=jnp.float32) / (MEMBERS - 1)
    entries = jnp.clip(jax.random.normal(jax.random.fold_in(key, 21), (MEMBERS, PIX, D), jnp.float32), -3.0, 3.0)
    member_scale = jnp.exp(member_pos * math.log(6.0))
    pairing = jax.random.permutation(jax.random.fold_in(key, 23), MEMBERS).astype(jnp.int32)
    feature_block = jnp.arange(D, dtype=jnp.int32) // (D // MEMBERS)
    spike = jnp.where(feature_block[None, :] == pairing[:, None], 3.0, 1.0).astype(jnp.float32)
    values = entries * member_scale[:, None, None] * spike[:, None, :]
    return values.astype(jnp.bfloat16)


def level_of(own_key, extent, pieces, smallest, high):
    def one(dim, shards_of):
        steps = jax.random.uniform(jax.random.fold_in(jax.random.fold_in(own_key, 6), dim), (shards_of,), jnp.float32, smallest / len(pieces), high / len(pieces))
        return jnp.repeat(jnp.exp(steps), extent[dim] // shards_of).reshape((-1,) + (1,) * (len(extent) - dim - 1))

    factor_of = one(*pieces[0])
    for cut in pieces[1:]:
        factor_of = factor_of * one(*cut)
    return factor_of


def scatter_about(stream_key, extent, spread, limit, split=(), kind=jnp.bfloat16):
    array = jax.random.normal(stream_key, extent, jnp.float32) * spread
    if len(split) > 0:
        array = level_of(stream_key, extent, split, -0.22, 0.18) * array
    return jnp.clip(array, min=-limit, max=limit).astype(kind)


def setup_inputs(seed: int = 0) -> dict:
    arg_keys = jax.random.split(jax.random.key(seed), 13)
    sample_layer_feed = draw_sample_layer_feed(jax.random.fold_in(arg_keys[12], 71), 0)
    gain = jnp.clip(1.0 + 0.18 * jax.random.normal(arg_keys[1], (D,), jnp.float32), 0.1, 1.9)
    w_query = draw_w_query(jax.random.fold_in(arg_keys[12], 71), 0)
    w_key = scatter_about(arg_keys[3], (D, INNER), D ** -0.5, 0.1875, ((0, 16),))
    w_value = scatter_about(arg_keys[4], (D, INNER), D ** -0.5, 0.1875, ((0, 16),))
    w_out = scatter_about(arg_keys[5], (INNER, D), INNER ** -0.5, 0.25, ((1, 16),))
    readout_matrix = scatter_about(arg_keys[6], (D, VARS), D ** -0.5, 0.1875)
    target = scatter_about(arg_keys[7], (PIX, VARS), 1.0, 6.0, ((0, 32),), jnp.float32)
    pixel_weight = draw_pixel_weight(jax.random.fold_in(arg_keys[12], 71), 0)
    pix_mask = draw_pix_mask(jax.random.fold_in(arg_keys[12], 71), 0)
    neighbours = draw_neighbours(jax.random.fold_in(arg_keys[12], 71), 0)
    neighbour_mask = draw_neighbour_mask(jax.random.fold_in(arg_keys[12], 71), 0)
    return dict(sample_layer_feed=sample_layer_feed, gain=gain, w_query=w_query, w_key=w_key, w_value=w_value, w_out=w_out, readout_matrix=readout_matrix, target=target, pixel_weight=pixel_weight, pix_mask=pix_mask, neighbours=neighbours, neighbour_mask=neighbour_mask)


eps_norm = 1e-06
easing_breadth = 0.1

def rms_scaled(member_rows, gain):
    values_f = member_rows.astype(jnp.float32)
    inverse = lax.rsqrt(lax.optimization_barrier(jnp.mean(values_f * values_f, axis=-1, keepdims=True)) + eps_norm)
    return (values_f * inverse * gain.astype(jnp.float32)).astype(jnp.bfloat16)

def eased_magnitude(sample_dispersion):
    return easing_breadth * (jax.nn.softplus(sample_dispersion / easing_breadth) + jax.nn.softplus(-sample_dispersion / easing_breadth))

def reference(sample_layer_feed, gain, w_query, w_key, w_value, w_out, readout_matrix, target, pixel_weight, pix_mask, neighbours, neighbour_mask):
    sample_sequence = sample_layer_feed.shape[0]
    normed = rms_scaled(sample_layer_feed, gain)

    def project(weights):
        return lax.map(lambda present_tile_piece: jnp.dot(present_tile_piece, weights, preferred_element_type=jnp.float32).astype(jnp.bfloat16), normed)
    queries = project(w_query)
    key_rows = project(w_key)
    value_rows = project(w_value)
    key_tiles = key_rows.reshape(sample_sequence, TILES, TILE, INNER)
    value_tiles = value_rows.reshape(sample_sequence, TILES, TILE, INNER)
    query_tiles = queries.reshape(sample_sequence, TILES, TILE, INNER)
    live_tiles = pix_mask.reshape(TILES, TILE) > 0

    def tile_weights(tile):
        slots = neighbours[tile]
        live_keys = (live_tiles[slots] & (neighbour_mask[tile][:, None] > 0)).reshape(NB * TILE)
        near_keys = key_tiles[:, slots].reshape(sample_sequence, NB * TILE, HEADS, HD).astype(jnp.float32)
        query_tile = query_tiles[:, tile].reshape(sample_sequence, TILE, HEADS, HD).astype(jnp.float32)
        scores = jnp.einsum('mqhd,mkhd->mhqk', query_tile, near_keys) * HD ** (-0.5)
        scores = jnp.where(live_keys[None, None, None, :], scores, -1e+30)
        row_max = lax.optimization_barrier(jnp.max(scores, axis=-1, keepdims=True))
        expos = jnp.exp(scores - row_max)
        return ((expos / lax.optimization_barrier(jnp.sum(expos, axis=-1, keepdims=True))).astype(jnp.bfloat16), slots)

    def attend(tile):
        weights, slots = tile_weights(tile)
        near_values = value_tiles[:, slots].reshape(sample_sequence, NB * TILE, HEADS, HD).astype(jnp.float32)
        mixture = jnp.einsum('mhqk,mkhd->mqhd', weights.astype(jnp.float32), near_values)
        return mixture.reshape(sample_sequence, TILE, INNER).astype(jnp.bfloat16)
    neighbour_mixing_vector = lax.map(attend, jnp.arange(TILES, dtype=jnp.int32))
    neighbour_mixing_vector = jnp.transpose(neighbour_mixing_vector, (1, 0, 2, 3)).reshape(sample_sequence, PIX, INNER)

    def later_layers_pass(inputs):
        member_rows, mixed_rows = inputs
        projected = jnp.dot(mixed_rows, w_out, preferred_element_type=jnp.float32)
        hidden_state = (member_rows.astype(jnp.float32) + projected).astype(jnp.bfloat16)
        return jnp.dot(hidden_state, readout_matrix, preferred_element_type=jnp.float32).astype(jnp.bfloat16)
    sample_prediction = lax.map(later_layers_pass, (sample_layer_feed, neighbour_mixing_vector))
    lone_prediction = sample_prediction.astype(jnp.float32)
    observed_entries = target[None]
    matrix_vertical_vector = (pixel_weight * pix_mask.astype(jnp.float32))[None, :, None]

    def extend_sample_entries(totals, sample_ordinal):
        eased_aggregate, accrued_tangent_amount = totals
        sample_dispersion = lone_prediction - sample_ordinal.astype(jnp.float32)[None]
        return ((eased_aggregate + eased_magnitude(sample_dispersion), accrued_tangent_amount + jnp.tanh(sample_dispersion / (2.0 * easing_breadth))), None)
    blank_tile_filler = jnp.zeros_like(lone_prediction)
    (eased_aggregate, accrued_tangent_amount), discarded_yield = lax.scan(extend_sample_entries, (blank_tile_filler, blank_tile_filler), sample_prediction)
    null_discrepancy = eased_magnitude(jnp.zeros((), jnp.float32))
    penalty_term_series = matrix_vertical_vector * (eased_magnitude(lone_prediction - observed_entries) - (eased_aggregate - null_discrepancy) / (2.0 * (sample_sequence - 1)))
    loss = jnp.sum(penalty_term_series) / (sample_sequence * PIX * VARS)
    derivative_factor = 1.0 / math.sqrt(sample_sequence * PIX)
    prediction_derivative = (matrix_vertical_vector * (jnp.tanh((lone_prediction - observed_entries) / (2.0 * easing_breadth)) - accrued_tangent_amount / (sample_sequence - 1)) * derivative_factor).astype(jnp.bfloat16)
    latent_derivative = lax.map(lambda present_tile_piece: jnp.dot(present_tile_piece, readout_matrix.T, preferred_element_type=jnp.float32).astype(jnp.bfloat16), prediction_derivative)
    grad_attended = lax.map(lambda present_tile_piece: jnp.dot(present_tile_piece, w_out.T, preferred_element_type=jnp.float32).astype(jnp.bfloat16), latent_derivative)
    grad_tiles = grad_attended.reshape(sample_sequence, TILES, TILE, HEADS, HD)

    def collect(accumulated, tile):
        weights, slots = tile_weights(tile)
        grad_tile = grad_tiles[:, tile].astype(jnp.float32)
        contrib = jnp.einsum('mhqk,mqhd->mkhd', weights.astype(jnp.float32), grad_tile).reshape(sample_sequence, NB, TILE, INNER)
        return (accumulated.at[:, slots].add(contrib), None)
    start_acc = jnp.zeros((sample_sequence, TILES, TILE, INNER), jnp.float32)
    accumulated, discarded_yield = lax.scan(collect, start_acc, jnp.arange(TILES, dtype=jnp.int32))
    grad_values = accumulated.reshape(sample_sequence, PIX, INNER).astype(jnp.bfloat16)

    def add_grads(totals, inputs):
        normed_rows, value_grads, mixed_rows, hidden_grads = inputs
        value_sum, output_sum = totals
        value_sum = value_sum + jnp.dot(normed_rows.T, value_grads, preferred_element_type=jnp.float32)
        output_sum = output_sum + jnp.dot(mixed_rows.T, hidden_grads, preferred_element_type=jnp.float32)
        return ((value_sum, output_sum), None)
    start_grads = (jnp.zeros((D, INNER), jnp.float32), jnp.zeros((INNER, D), jnp.float32))
    (grad_w_value, grad_w_out), discarded_yield = lax.scan(add_grads, start_grads, (normed, grad_values, neighbour_mixing_vector, latent_derivative))
    return (loss, grad_w_out, grad_w_value)
```

```python
import math

import jax
import jax.numpy as jnp
from jax import lax
from jax.experimental import pallas as pl
from jax.experimental.pallas import tpu as pltpu
from jax.sharding import PartitionSpec as P

HEADS = 8
HD = 64
TILE = 128
NB = 9
D = 1024
INNER = 512
VARS = 128
MEMBERS = 16
PATCHES = 32
EPS = 1e-06
MESH = pl.DeviceIdType.MESH
F32 = jnp.float32
BF16 = jnp.bfloat16

GROUPS = ((0, 2), (2, 1), (3, 1))
NSEM = 20


def nt(a, b):
    return lax.dot_general(a, b, (((1,), (1,)), ((), ())), preferred_element_type=F32)


def mm(a, b):
    return jnp.dot(a, b, preferred_element_type=F32)


def step_kernel(
    x_hbm, gain_ref, wq_hbm, wk_hbm, wv_hbm, wo_hbm, r_hbm, tgt_ref, pw_ref, pm_ref, nbr_ref, nbm_ref,
    loss_ref, gv_ref, go_ref,
    W, xw, R, nrm, nT, qs, ks, vs, wT, att, dV,
    fcs, fcr, gs, gr, lwc, lt, l2, lp, lr, lz1, lz2, ls,
    G, Gp, H, Rr, acc, z1s, z1r, z2s, z2b, fin,
    loc, xs, xr, ws, wr, fs, fr, bs, br, ps, pr, lps, lpr, rs, rr, lrs, lrr, z1ss, z1rs, z2ss, z2rs, l1s, l1r, l4s, l4r,
    z3s, z3r,
):
    e = lax.axis_index("ens")
    t = lax.axis_index("pix")
    x = lax.div(e, 4)
    yh = lax.rem(lax.div(e, 2), 2)
    c = lax.rem(e, 2)
    yl = lax.div(t, 16)
    z = lax.rem(t, 16)
    zh = lax.div(z, 4)
    zl = lax.rem(z, 4)
    y = 2 * yh + yl

    def ens_of(xx, hh, cc):
        return xx * 4 + hh * 2 + cc

    def wrap(v, n):
        return lax.rem(v + 2 * n, n)

    pending = []

    def desc(src, dst, ss, rr_, dev):
        return pltpu.make_async_remote_copy(
            src_ref=src, dst_ref=dst, send_sem=ss, recv_sem=rr_, device_id=dev, device_id_type=MESH
        )

    def send(src, dst, ss, rr_, dev):
        cp = desc(src, dst, ss, rr_, dev)
        cp.start()
        pending.append(cp)

    def chip(dx, dy):
        xx = wrap(x + dx, 4)
        yy = wrap(y + dy, 4)
        return xx, lax.div(yy, 2), lax.rem(yy, 2)

    def chip_dev(dx, dy):
        xx, hh, ll = chip(dx, dy)
        return (ens_of(xx, hh, c), ll * 16 + z)

    partner = (ens_of(x, yh, 1 - c), t)
    far = (ens_of(x, 1 - yh, c), (1 - yl) * 16 + z)
    near = (e, (1 - yl) * 16 + z)
    up = (e, wrap(t + 1, 32))
    down = (e, wrap(t - 1, 32))
    xplus = (ens_of(wrap(x + 1, 4), yh, c), t)
    xminus = (ens_of(wrap(x - 1, 4), yh, c), t)

    def ens_dev(dx, dh, dc):
        return (ens_of(wrap(x + dx, 4), wrap(yh + dh, 2), wrap(c + dc, 2)), t)

    def zl_dev(k, other=0):
        ll = wrap(yl + other, 2)
        return (e, ll * 16 + zh * 4 + wrap(zl + k, 4))

    def zh_dev(k):
        return (e, yl * 16 + wrap(zh + k, 4) * 4 + zl)

    ens_offsets = [(a, b, d) for a in range(4) for b in range(2) for d in range(2) if (a, b, d) != (0, 0, 0)]
    chip_offsets = [(a, b) for a in range(4) for b in range(4) if (a, b) != (0, 0)]

    rows = pl.ds(pl.multiple_of(64 * e, 64), 64)
    loads = [
        pltpu.make_async_copy(x_hbm, xw.at[1], loc.at[0]),
        pltpu.make_async_copy(wk_hbm, W.at[0, rows, :], loc.at[1]),
        pltpu.make_async_copy(wv_hbm, W.at[1, rows, :], loc.at[2]),
        pltpu.make_async_copy(wq_hbm, W.at[2, rows, :], loc.at[3]),
        pltpu.make_async_copy(wo_hbm, W.at[3, rows, :], loc.at[4]),
        pltpu.make_async_copy(r_hbm, R, loc.at[5]),
    ]
    for cp in loads:
        cp.start()

    peers = [ens_dev(*o) for o in ens_offsets]
    peers += [chip_dev(*o) for o in chip_offsets if o[1] % 2 == 1]
    peers += [up, down]
    peers += [zl_dev(k) for k in (1, 2, 3)] + [zh_dev(k) for k in (1, 2, 3)]
    peers += [zl_dev(k, 1) for k in (1, 2, 3)]
    barrier = pltpu.get_barrier_semaphore()
    for dev in peers:
        pl.semaphore_signal(barrier, inc=1, device_id=dev, device_id_type=MESH)
    for cp in loads:
        cp.wait()
    pl.semaphore_wait(barrier, len(peers))

    send(xw.at[1], xw.at[0], xs.at[0], xr.at[0], up)
    send(xw.at[1], xw.at[2], xs.at[1], xr.at[1], down)

    def shard(g, ee, r0=0, n=64):
        w0, nw = GROUPS[g]
        return W.at[pl.ds(w0, nw), pl.ds(pl.multiple_of(64 * ee + r0, 32), n), :]

    def wsend(g, k, ref, dev):
        send(ref, ref, ws.at[g, k], wr.at[g, k], dev)

    def wwait(g, k, ref):
        desc(ref, ref, ws.at[g, k], wr.at[g, k], partner).wait_recv()

    mine = 32 * yl
    theirs = 32 * (1 - yl)
    cols = [x, wrap(x - 1, 4), wrap(x + 1, 4), wrap(x + 2, 4)]
    own_e = [ens_of(xx, yh, c) for xx in cols]
    far_e = [ens_of(xx, 1 - yh, c) for xx in cols]
    par_e = [ens_of(xx, hh, 1 - c) for hh in (yh, 1 - yh) for xx in cols]

    def issue0(g):
        own = shard(g, own_e[0])
        wsend(g, 0, own, xplus)
        wsend(g, 1, own, xminus)
        wsend(g, 4, shard(g, own_e[0], mine, 32), far)
        wsend(g, 12, own, partner)

    def step1(g):
        wwait(g, 0, shard(g, own_e[1]))
        wsend(g, 2, shard(g, own_e[1], 0, 32), xplus)
        wsend(g, 5, shard(g, own_e[1], mine, 32), far)
        wsend(g, 13, shard(g, own_e[1]), partner)
        wwait(g, 1, shard(g, own_e[2]))
        wsend(g, 3, shard(g, own_e[2], 32, 32), xminus)
        wsend(g, 6, shard(g, own_e[2], mine, 32), far)
        wsend(g, 14, shard(g, own_e[2]), partner)

    def step2(g):
        wwait(g, 4, shard(g, far_e[0], theirs, 32))
        wsend(g, 8, shard(g, far_e[0], theirs, 32), near)
        wwait(g, 2, shard(g, own_e[3], 0, 32))
        wwait(g, 3, shard(g, own_e[3], 32, 32))
        wsend(g, 7, shard(g, own_e[3], mine, 32), far)
        wsend(g, 15, shard(g, own_e[3]), partner)

    def step3(g):
        for i in (1, 2):
            wwait(g, 4 + i, shard(g, far_e[i], theirs, 32))
            wsend(g, 8 + i, shard(g, far_e[i], theirs, 32), near)
        wwait(g, 8, shard(g, far_e[0], mine, 32))
        wsend(g, 16, shard(g, far_e[0]), partner)

    def step4(g):
        wwait(g, 7, shard(g, far_e[3], theirs, 32))
        wsend(g, 11, shard(g, far_e[3], theirs, 32), near)
        for i in (1, 2, 3):
            wwait(g, 8 + i, shard(g, far_e[i], mine, 32))
            wsend(g, 16 + i, shard(g, far_e[i]), partner)

    def step5(g):
        for i in range(8):
            wwait(g, 12 + i, shard(g, par_e[i]))

    gain = gain_ref[...]

    def normalise(j):
        v = xw[j].astype(F32)
        inv = lax.rsqrt(jnp.mean(v * v, axis=-1, keepdims=True) + EPS)
        n = v * inv * gain
        nrm[128 * j : 128 * (j + 1), :] = n.astype(BF16)

    def transpose_normed(j):
        nT[:, 128 * j : 128 * (j + 1)] = nrm[128 * j : 128 * (j + 1), :].astype(F32).T.astype(BF16)

    issue0(0)
    issue0(1)
    normalise(1)
    step1(0)
    issue0(2)
    step2(0)
    step1(1)
    step3(0)
    step2(1)
    step4(0)
    desc(xw.at[1], xw.at[0], xs.at[0], xr.at[0], up).wait_recv()
    normalise(0)
    desc(xw.at[1], xw.at[2], xs.at[1], xr.at[1], down).wait_recv()
    normalise(2)
    step3(1)
    step1(2)
    step4(1)
    step2(2)
    step5(0)
    ks[...] = mm(nrm[...], W[0]).astype(BF16)
    step3(2)
    vs[...] = mm(nrm[...], W[1]).astype(BF16)
    step4(2)
    step5(1)
    qs[...] = mm(nrm[128:256, :], W[2]).astype(BF16)

    counts = []
    live = []
    for j in range(3):
        n = jnp.int32(0)
        for s in range(NB):
            hit = (nbr_ref[0, s] == t - 1 + j) & (nbm_ref[0, s] > 0)
            n = n + jnp.where(hit, 1, 0)
        counts.append(n.astype(F32))
        row = jnp.clip(t - 1 + j, 0, PATCHES - 1)
        live.append((pm_ref[pl.ds(row, 1), :] > 0) & (n > 0))
    bias = jnp.concatenate([jnp.where(m, 0.0, -1e30) for m in live], axis=1)
    scale = jnp.concatenate([jnp.broadcast_to(n, (1, 128)) for n in counts], axis=1)
    alive = bias == 0.0
    own_mask = jnp.where(pm_ref[pl.ds(t, 1), :] > 0, 1.0, 0.0)
    lwc[...] = jnp.broadcast_to(pw_ref[...] * own_mask, (128, 128)).T

    lane = lax.broadcasted_iota(jnp.int32, (1, 128), 1)
    for pair in range(HEADS // 2):
        cs = slice(128 * pair, 128 * (pair + 1))
        q2 = qs[:, cs]
        k2 = ks[:, cs]
        mixed = []
        for half in range(2):
            inside = (lane >= 64) if half else (lane < 64)
            qh = jnp.where(inside, q2, jnp.zeros_like(q2))
            sc = nt(qh, k2) * HD ** (-0.5)
            sc = jnp.where(alive, sc, -1e30)
            ex = jnp.exp(sc - jnp.max(sc, axis=-1, keepdims=True))
            w = ex / jnp.sum(ex * scale, axis=-1, keepdims=True)
            wb = w.astype(BF16)
            out = jnp.zeros((128, 128), F32)
            for j in range(3):
                out = out + counts[j] * mm(wb[:, 128 * j : 128 * (j + 1)], vs[128 * j : 128 * (j + 1), cs])
            mixed.append(out)
            wT[2 * pair + half] = w.T.astype(BF16)
        att[:, cs] = jnp.where(lane < 64, mixed[0], mixed[1]).astype(BF16)

    step5(2)
    hidden = (xw[1].astype(F32) + nt(att[...], W[3])).astype(BF16)
    fc = mm(hidden, R[...]).astype(BF16).astype(F32)
    fcs[...] = fc.reshape(16, 8, 128)

    def slot(o):
        return o[0] * 4 + o[1] * 2 + o[2]

    def ens_index(o):
        return ens_of(wrap(x + o[0], 4), wrap(yh + o[1], 2), wrap(c + o[2], 2))

    def ens_back(o):
        return (-o[0], -o[1], -o[2])

    for o in ens_offsets:
        k = slot(o)
        send(fcs.at[ens_index(o)], fcr.at[k], fs.at[k], fr.at[k], ens_dev(*o))
    transpose_normed(0)
    fcr[0] = fcs[e]
    for o in ens_offsets:
        k = slot(o)
        desc(fcs.at[ens_index(o)], fcr.at[k], fs.at[k], fr.at[k], ens_dev(*o)).wait_recv()

    F = fcr[...]
    pix = pl.ds(pl.multiple_of(8 * e, 8), 8)
    lw = lwc[pix, :]
    dt = F - tgt_ref[pix, :][None]
    grad = jnp.tanh(dt * 5.0)
    mag = jnp.sum(jnp.abs(dt), axis=0)
    prod = jnp.ones((8, 128), F32)
    ext = 1.0 + jnp.exp(-10.0 * jnp.abs(dt))
    for i in range(16):
        prod = prod * ext[i]
    term = mag + 0.2 * jnp.log(prod)
    tot = jnp.zeros_like(F)
    pmag = jnp.zeros((8, 128), F32)
    prod = jnp.ones((8, 128), F32)
    for r in range(1, 9):
        other = jnp.concatenate([F[r:], F[:r]], axis=0)
        d = F - other
        if r == 8:
            d = d[:8]
        th = jnp.tanh(d * 5.0)
        ab = jnp.abs(d)
        pmag = pmag + jnp.sum(ab, axis=0)
        ext = 1.0 + jnp.exp(-10.0 * ab)
        for i in range(ext.shape[0]):
            prod = prod * ext[i]
        if r == 8:
            tot = tot + jnp.concatenate([th, -th], axis=0)
        else:
            tot = tot + th - jnp.concatenate([th[16 - r :], th[: 16 - r]], axis=0)
    pterm = pmag + 0.2 * jnp.log(prod)
    lt[...] = lw * (term - pterm / (MEMBERS - 1))
    factor = 1.0 / math.sqrt(MEMBERS * PATCHES * TILE)
    gs[...] = (lw[None] * (grad - tot / (MEMBERS - 1)) * factor).astype(BF16).astype(F32)

    for o in ens_offsets:
        k = slot(o)
        send(gs.at[k], gr.at[e], bs.at[k], br.at[k], ens_dev(*ens_back(o)))
    send(lt, lp, lps.at[0], lpr.at[0], partner)
    gr[e] = gs[0]
    transpose_normed(1)
    transpose_normed(2)
    desc(lt, lp, lps.at[0], lpr.at[0], partner).wait_recv()
    l2[...] = lt[...] + lp[...]
    here = x * 4 + y
    for o in chip_offsets:
        k = o[0] * 4 + o[1]
        send(l2, lr.at[here], lrs.at[k], lrr.at[k], chip_dev(*o))
    for o in ens_offsets:
        k = slot(o)
        desc(gs.at[k], gr.at[ens_index(o)], bs.at[k], br.at[k], ens_dev(*ens_back(o))).wait_recv()

    gf = gr[...].reshape(128, 128)
    gfb = gf.astype(BF16)
    gh = nt(gfb, R[...]).astype(BF16)
    ga = mm(gh, W[3]).astype(BF16)
    gfT = gf.T.astype(BF16)
    hT = mm(R[...], gfT).astype(BF16)
    for pair in range(HEADS // 2):
        cs = slice(128 * pair, 128 * (pair + 1))
        g2 = ga[:, cs]
        a = mm(wT[2 * pair], g2)
        b = mm(wT[2 * pair + 1], g2)
        both = jnp.where(lane < 64, a, b)
        for j in range(3):
            dV[128 * j : 128 * (j + 1), cs] = (both[128 * j : 128 * (j + 1)] * counts[j]).astype(BF16)
    G[1] = mm(hT, att[...]).astype(BF16).reshape(8, 2, 64, 512)
    G[0] = mm(nT[...], dV[...]).astype(BF16).reshape(8, 2, 64, 512)

    send(G.at[:, :, 1 - c], Gp, ps.at[0], pr.at[0], partner)
    desc(G.at[:, :, 1 - c], Gp, ps.at[0], pr.at[0], partner).wait_recv()
    for k in range(2):
        for b in range(8):
            H[k, b] = (G[k, b, c].astype(F32) + Gp[k, b].astype(F32)).astype(BF16)

    for o in chip_offsets:
        k = o[0] * 4 + o[1]
        xx, hh, ll = chip(*o)
        send(H.at[ll, xx * 2 + hh], Rr.at[k], rs.at[k], rr.at[k], chip_dev(*o))
    total = H[yl, x * 2 + yh].astype(F32)
    for o in chip_offsets:
        k = o[0] * 4 + o[1]
        desc(l2, lr.at[here], lrs.at[k], lrr.at[k], chip_dev(*o)).wait_recv()
    lr[here] = l2[...]
    l3 = lr[0]
    for i in range(1, 16):
        l3 = l3 + lr[i]
    ls[0] = l3
    for k in (1, 2, 3):
        send(ls.at[0], lz1.at[zl], l1s.at[k], l1r.at[k], zl_dev(k))
    lz1[zl] = l3
    for o in chip_offsets:
        k = o[0] * 4 + o[1]
        xx, hh, ll = chip(*o)
        desc(H.at[ll, xx * 2 + hh], Rr.at[k], rs.at[k], rr.at[k], chip_dev(*o)).wait_recv()
        total = total + Rr[k].astype(F32)
    acc[...] = total.reshape(4, 16, 512)

    z1s[...] = acc[...].astype(BF16)
    for k in (1, 2, 3):
        send(z1s.at[wrap(zl + k, 4)], z1r.at[k], z1ss.at[k], z1rs.at[k], zl_dev(k))
    for k in (1, 2, 3):
        desc(ls.at[0], lz1.at[zl], l1s.at[k], l1r.at[k], zl_dev(k)).wait_recv()
    l4 = ((lz1[0] + lz1[1]) + lz1[2]) + lz1[3]
    ls[1] = l4
    for k in (1, 2, 3):
        send(ls.at[1], lz2.at[zh], l4s.at[k], l4r.at[k], zh_dev(k))
    lz2[zh] = l4
    part = acc[zl]
    for k in (1, 2, 3):
        desc(z1s.at[wrap(zl + k, 4)], z1r.at[k], z1ss.at[k], z1rs.at[k], zl_dev(k)).wait_recv()
        part = part + z1r[k].astype(F32)
    z2s[...] = part.astype(BF16)
    for k in (1, 2, 3):
        send(z2s, z2b.at[zh], z2ss.at[k], z2rs.at[k], zh_dev(k))
    z2b[zh] = z2s[...]
    for k in (1, 2, 3):
        desc(ls.at[1], lz2.at[zh], l4s.at[k], l4r.at[k], zh_dev(k)).wait_recv()
    l5 = ((lz2[0] + lz2[1]) + lz2[2]) + lz2[3]
    norm = 1.0 / (MEMBERS * PATCHES * TILE * VARS)
    loss_ref[...] = jnp.sum(jnp.sum(l5, axis=0, keepdims=True), axis=1, keepdims=True) * norm
    for k in (1, 2, 3):
        desc(z2s, z2b.at[zh], z2ss.at[k], z2rs.at[k], zh_dev(k)).wait_recv()
    whole = ((z2b[0].astype(F32) + z2b[1].astype(F32)) + z2b[2].astype(F32)) + z2b[3].astype(F32)
    fin[yl, zl] = whole.astype(BF16)
    last = [(0, k) for k in (1, 2, 3)] + [(1, k) for k in range(4)]
    for i, (other, k) in enumerate(last):
        send(fin.at[yl, zl], fin.at[yl, zl], z3s.at[i], z3r.at[i], zl_dev(k, other))
    for i, (other, k) in enumerate(last):
        desc(fin.at[yl, zl], fin.at[yl, zl], z3s.at[i], z3r.at[i], zl_dev(k, other)).wait_recv()
    gv_ref[...] = fin[0].astype(F32).reshape(64, 512)
    go_ref[...] = fin[1].astype(F32).reshape(64, 512)

    for cp in pending:
        cp.wait_send()


def per_device(
    sample_layer_feed,
    gain,
    w_query,
    w_key,
    w_value,
    w_out,
    readout_matrix,
    target,
    pixel_weight,
    pix_mask,
    neighbours,
    neighbour_mask,
):
    hbm = pl.BlockSpec(memory_space=pl.ANY)
    vmem = pl.BlockSpec(memory_space=pltpu.VMEM)
    smem = pl.BlockSpec(memory_space=pltpu.SMEM)
    dma = lambda *n: pltpu.SemaphoreType.DMA(n)
    scratch = [
        pltpu.VMEM((4, D, INNER), BF16),
        pltpu.VMEM((3, TILE, D), BF16),
        pltpu.VMEM((D, VARS), BF16),
        pltpu.VMEM((3 * TILE, D), BF16),
        pltpu.VMEM((D, 3 * TILE), BF16),
        pltpu.VMEM((TILE, INNER), BF16),
        pltpu.VMEM((3 * TILE, INNER), BF16),
        pltpu.VMEM((3 * TILE, INNER), BF16),
        pltpu.VMEM((HEADS, 3 * TILE, TILE), BF16),
        pltpu.VMEM((TILE, INNER), BF16),
        pltpu.VMEM((3 * TILE, INNER), BF16),
        pltpu.VMEM((16, 8, 128), F32),
        pltpu.VMEM((16, 8, 128), F32),
        pltpu.VMEM((16, 8, 128), F32),
        pltpu.VMEM((16, 8, 128), F32),
        pltpu.VMEM((128, 128), F32),
        pltpu.VMEM((8, 128), F32),
        pltpu.VMEM((8, 128), F32),
        pltpu.VMEM((8, 128), F32),
        pltpu.VMEM((16, 8, 128), F32),
        pltpu.VMEM((4, 8, 128), F32),
        pltpu.VMEM((4, 8, 128), F32),
        pltpu.VMEM((2, 8, 128), F32),
        pltpu.VMEM((2, 8, 2, 64, INNER), BF16),
        pltpu.VMEM((2, 8, 64, INNER), BF16),
        pltpu.VMEM((2, 8, 64, INNER), BF16),
        pltpu.VMEM((16, 64, INNER), BF16),
        pltpu.VMEM((4, 16, INNER), F32),
        pltpu.VMEM((4, 16, INNER), BF16),
        pltpu.VMEM((4, 16, INNER), BF16),
        pltpu.VMEM((16, INNER), BF16),
        pltpu.VMEM((4, 16, INNER), BF16),
        pltpu.VMEM((2, 4, 16, INNER), BF16),
        dma(6), dma(2), dma(2), dma(len(GROUPS), NSEM), dma(len(GROUPS), NSEM),
        dma(16), dma(16), dma(16), dma(16), dma(1), dma(1), dma(1), dma(1),
        dma(16), dma(16), dma(16), dma(16), dma(4), dma(4), dma(4), dma(4), dma(4), dma(4), dma(4), dma(4),
        dma(7), dma(7),
    ]
    loss, gv, go = pl.pallas_call(
        step_kernel,
        out_shape=(
            jax.ShapeDtypeStruct((1, 1), F32),
            jax.ShapeDtypeStruct((64, INNER), F32),
            jax.ShapeDtypeStruct((64, INNER), F32),
        ),
        in_specs=[hbm, vmem, hbm, hbm, hbm, hbm, hbm, vmem, vmem, vmem, smem, smem],
        out_specs=(vmem, vmem, vmem),
        scratch_shapes=scratch,
        compiler_params=pltpu.CompilerParams(
            collective_id=0, has_side_effects=True, vmem_limit_bytes=48 * 1024 * 1024
        ),
        name="forecast_step",
    )(
        sample_layer_feed[0],
        gain.reshape(1, D),
        w_query,
        w_key,
        w_value,
        w_out.T,
        readout_matrix,
        target,
        pixel_weight.reshape(1, TILE),
        pix_mask.reshape(PATCHES, TILE),
        neighbours,
        neighbour_mask,
    )
    return (loss.reshape(()), go.T, gv)


def solution(mesh):
    in_specs = (
        P("ens", "pix", None),
        P(),
        P("ens", None),
        P("ens", None),
        P("ens", None),
        P(None, "ens"),
        P(),
        P("pix", None),
        P("pix"),
        P(),
        P("pix", None),
        P("pix", None),
    )
    out_specs = (P(), P(None, "ens"), P("ens", None))
    return jax.shard_map(
        per_device, mesh=mesh, in_specs=in_specs, out_specs=out_specs, check_vma=False
    )
```

```python
import math

import jax
import jax.numpy as jnp
from jax import lax
from jax.experimental import pallas as pl
from jax.experimental.pallas import tpu as pltpu
from jax.sharding import PartitionSpec as P

HEADS = 8
HD = 64
TILE = 128
NB = 9
D = 1024
INNER = 512
VARS = 128
MEMBERS = 16
PATCHES = 32
EPS = 1e-06
MESH = pl.DeviceIdType.MESH
F32 = jnp.float32
BF16 = jnp.bfloat16

KEY, QUERY, VALUE, OUT = 0, 1, 2, 3

ORDER_A = (
    ("f0", 0), ("f0", 1), ("xm", 0), ("xp", 0), ("f0", 2), ("n0", 0), ("f0", 3), ("xm", 1), ("xp", 1),
    ("n0", 1), ("f1", 0), ("n0", 2), ("f2", 0), ("xm", 2), ("xp", 2), ("n0", 3), ("f1", 1),
)
ORDER_B = (
    ("n1", 0), ("f2", 1), ("xm", 3), ("xp", 3), ("n2", 0), ("f1", 2), ("h", 0), ("n1", 1), ("f2", 2), ("h", 1),
    ("n2", 1), ("f1", 3), ("h", 2), ("n1", 2), ("f2", 3), ("h", 3), ("n2", 2), ("f3", 0), ("n1", 3), ("f3", 1),
    ("n2", 3), ("f3", 2), ("n3", 0), ("f3", 3), ("n3", 1),
)


def nt(a, b):
    return lax.dot_general(a, b, (((1,), (1,)), ((), ())), preferred_element_type=F32)


def mm(a, b):
    return jnp.dot(a, b, preferred_element_type=F32)


def step_kernel(
    x_hbm, gain_hbm, wq_hbm, wk_hbm, wv_hbm, wo_hbm, r_hbm, tgt_hbm, pw_hbm, pm_hbm, nbr_hbm, nbm_hbm,
    loss_ref, gv_ref, go_ref,
    gain_ref, tgt_ref, pw_ref, pm_ref, nbr_ref, nbm_ref,
    W, xw, R, nrm, nT, qs, ks, vs, wS, wT, att, dV,
    fcs, fcr, gs, gr, lwc, lt, l2, lp, lr, mz1, mz2, ms,
    S, Sp, S2, Sr, SF, G, Gp, H, Rr, acc, z1s, z1r, z2s, z2b, fin,
    loc, xs, xr, ws, wr, fs, fr, bs, br, ps, pr, lps, lpr, rs, rr, lrs, lrr, z1ss, z1rs, z2ss, z2rs, l1s, l1r, l4s, l4r,
    z3s, z3r, sps, spr, srs, srr, sfs, sfr,
):
    e = lax.axis_index("ens")
    t = lax.axis_index("pix")
    x = lax.div(e, 4)
    yh = lax.rem(lax.div(e, 2), 2)
    c = lax.rem(e, 2)
    yl = lax.div(t, 16)
    z = lax.rem(t, 16)
    zh = lax.div(z, 4)
    zl = lax.rem(z, 4)
    y = 2 * yh + yl

    def ens_of(xx, hh, cc):
        return xx * 4 + hh * 2 + cc

    def wrap(v, n):
        return lax.rem(v + 2 * n, n)

    def desc(src, dst, ss, rr_, dev):
        return pltpu.make_async_remote_copy(
            src_ref=src, dst_ref=dst, send_sem=ss, recv_sem=rr_, device_id=dev, device_id_type=MESH
        )

    def send(src, dst, ss, rr_, dev):
        desc(src, dst, ss, rr_, dev).start()

    def sent(ref, ss):
        desc(ref, ref, ss, ss, partner).wait_send()

    def received(ref, rr_):
        desc(ref, ref, rr_, rr_, partner).wait_recv()

    def chip(dx, dy):
        xx = wrap(x + dx, 4)
        yy = wrap(y + dy, 4)
        return xx, lax.div(yy, 2), lax.rem(yy, 2)

    def chip_dev(dx, dy):
        xx, hh, ll = chip(dx, dy)
        return (ens_of(xx, hh, c), ll * 16 + z)

    partner = (ens_of(x, yh, 1 - c), t)
    far = (ens_of(x, 1 - yh, c), (1 - yl) * 16 + z)
    near = (e, (1 - yl) * 16 + z)
    up = (e, wrap(t + 1, 32))
    down = (e, wrap(t - 1, 32))
    xplus = (ens_of(wrap(x + 1, 4), yh, c), t)
    xminus = (ens_of(wrap(x - 1, 4), yh, c), t)

    def ens_dev(dx, dh, dc):
        return (ens_of(wrap(x + dx, 4), wrap(yh + dh, 2), wrap(c + dc, 2)), t)

    def zl_dev(k, other=0):
        ll = wrap(yl + other, 2)
        return (e, ll * 16 + zh * 4 + wrap(zl + k, 4))

    def zh_dev(k):
        return (e, yl * 16 + wrap(zh + k, 4) * 4 + zl)

    ens_offsets = [(a, b, d) for a in range(4) for b in range(2) for d in range(2) if (a, b, d) != (0, 0, 0)]
    chip_offsets = [(a, b) for a in range(4) for b in range(4) if (a, b) != (0, 0)]

    plane_offsets = [(a, b, d) for a in range(4) for b in range(4) for d in range(2) if (a, b, d) != (0, 0, 0)]

    rows = pl.ds(pl.multiple_of(64 * e, 64), 64)
    loads = [
        pltpu.make_async_copy(x_hbm, xw.at[1], loc.at[0]),
        pltpu.make_async_copy(wk_hbm, W.at[KEY, rows, :], loc.at[1]),
        pltpu.make_async_copy(wq_hbm, W.at[QUERY, rows, :], loc.at[2]),
        pltpu.make_async_copy(wv_hbm, W.at[VALUE, rows, :], loc.at[3]),
        pltpu.make_async_copy(wo_hbm, W.at[OUT, rows, :], loc.at[4]),
        pltpu.make_async_copy(gain_hbm, gain_ref, loc.at[6]),
        pltpu.make_async_copy(r_hbm, R, loc.at[5]),
        pltpu.make_async_copy(tgt_hbm, tgt_ref, loc.at[7]),
        pltpu.make_async_copy(pw_hbm, pw_ref, loc.at[8]),
        pltpu.make_async_copy(pm_hbm, pm_ref, loc.at[9]),
        pltpu.make_async_copy(nbr_hbm, nbr_ref, loc.at[10]),
        pltpu.make_async_copy(nbm_hbm, nbm_ref, loc.at[11]),
    ]
    for cp in loads:
        cp.start()

    peers = []
    for dx, dy, dc in plane_offsets:
        xx, hh, ll = chip(dx, dy)
        peers.append((ens_of(xx, hh, wrap(c + dc, 2)), ll * 16 + z))
    peers += [up, down]
    peers += [zl_dev(k) for k in (1, 2, 3)] + [zh_dev(k) for k in (1, 2, 3)]
    peers += [zl_dev(k, 1) for k in (1, 2, 3)]
    barrier = pltpu.get_barrier_semaphore()
    for dev in peers:
        pl.semaphore_signal(barrier, inc=1, device_id=dev, device_id_type=MESH)
    for cp in loads[:5]:
        cp.wait()
    pl.semaphore_wait(barrier, len(peers))

    def shard(g, ee, r0=0, n=64):
        return W.at[g, pl.ds(pl.multiple_of(64 * ee + r0, 32), n), :]

    def wsend(g, k, ref, dev):
        send(ref, ref, ws.at[g], wr.at[g, k], dev)

    def wwait(g, k, ref):
        received(ref, wr.at[g, k])

    mine = 32 * yl
    theirs = 32 * (1 - yl)
    cols = [x, wrap(x - 1, 4), wrap(x + 1, 4), wrap(x + 2, 4)]
    own_e = [ens_of(xx, yh, c) for xx in cols]
    far_e = [ens_of(xx, 1 - yh, c) for xx in cols]

    def own(g):
        wsend(g, 0, shard(g, own_e[0]), xplus)
        wsend(g, 1, shard(g, own_e[0]), xminus)
        wsend(g, 3, shard(g, own_e[0], mine, 32), far)

    def take(kind, g):
        if kind == "xm":
            wwait(g, 0, shard(g, own_e[1]))
            wsend(g, 2, shard(g, own_e[1], 0, 32), xplus)
            wsend(g, 4, shard(g, own_e[1], mine, 32), far)
            wsend(g, 11, shard(g, own_e[1]), partner)
        elif kind == "xp":
            wwait(g, 1, shard(g, own_e[2]))
            wsend(g, 2, shard(g, own_e[2], 32, 32), xminus)
            wsend(g, 5, shard(g, own_e[2], mine, 32), far)
            wsend(g, 11, shard(g, own_e[2]), partner)
        elif kind == "h":
            wwait(g, 2, shard(g, own_e[3]))
            wsend(g, 6, shard(g, own_e[3], mine, 32), far)
            wsend(g, 11, shard(g, own_e[3]), partner)
        elif kind[0] == "f":
            i = int(kind[1])
            wwait(g, 3 + i, shard(g, far_e[i], theirs, 32))
            wsend(g, 7 + i, shard(g, far_e[i], theirs, 32), near)
        else:
            i = int(kind[1])
            wwait(g, 7 + i, shard(g, far_e[i], mine, 32))
            wsend(g, 11, shard(g, far_e[i]), partner)

    def whole_weight(g):
        received(W.at[g, pl.ds(0, 512), :], wr.at[g, 11])

    for g in range(4):
        own(g)
    send(xw.at[1], xw.at[0], xs.at[0], xr.at[0], up)
    send(xw.at[1], xw.at[2], xs.at[0], xr.at[1], down)
    for g in range(4):
        wsend(g, 11, shard(g, own_e[0]), partner)
    for cp in loads[5:]:
        cp.wait()

    gain = gain_ref[...]

    def normalise(j):
        v = xw[j].astype(F32)
        inv = lax.rsqrt(jnp.mean(v * v, axis=-1, keepdims=True) + EPS)
        n = v * inv * gain
        nrm[128 * j : 128 * (j + 1), :] = n.astype(BF16)

    def transpose_normed(j):
        nT[:, 128 * j : 128 * (j + 1)] = nrm[128 * j : 128 * (j + 1), :].astype(F32).T.astype(BF16)

    normalise(1)
    for kind, g in ORDER_A:
        take(kind, g)
    received(xw.at[0], xr.at[0])
    normalise(0)
    received(xw.at[2], xr.at[1])
    normalise(2)
    for kind, g in ORDER_B:
        take(kind, g)
    whole_weight(KEY)
    ks[...] = mm(nrm[...], W[KEY]).astype(BF16)
    take("n3", 2)
    whole_weight(QUERY)
    qs[...] = mm(nrm[128:256, :], W[QUERY]).astype(BF16)
    take("n3", 3)

    counts = []
    live = []
    for j in range(3):
        n = jnp.int32(0)
        for s in range(NB):
            hit = (nbr_ref[0, s] == t - 1 + j) & (nbm_ref[0, s] > 0)
            n = n + jnp.where(hit, 1, 0)
        counts.append(n.astype(F32))
        row = jnp.clip(t - 1 + j, 0, PATCHES - 1)
        live.append((pm_ref[pl.ds(row, 1), :] > 0) & (n > 0))
    bias = jnp.concatenate([jnp.where(m, 0.0, -1e30) for m in live], axis=1)
    scale = jnp.concatenate([jnp.broadcast_to(n, (1, 128)) for n in counts], axis=1)
    own_mask = jnp.where(pm_ref[pl.ds(t, 1), :] > 0, 1.0, 0.0)
    lwc[...] = jnp.broadcast_to(pw_ref[...] * own_mask, (128, 128)).T

    lane = lax.broadcasted_iota(jnp.int32, (1, 128), 1)
    for h in range(HEADS):
        cs = slice(128 * (h // 2), 128 * (h // 2 + 1))
        q2 = qs[:, cs]
        inside = (lane >= 64) if h % 2 else (lane < 64)
        qh = jnp.where(inside, q2, jnp.zeros_like(q2))
        sc = nt(qh, ks[:, cs]) * HD ** (-0.5) + bias
        ex = jnp.exp(sc - jnp.max(sc, axis=-1, keepdims=True))
        wS[h] = (ex * (1.0 / jnp.sum(ex * scale, axis=-1, keepdims=True))).astype(BF16)

    whole_weight(VALUE)
    vs[...] = mm(nrm[...], W[VALUE]).astype(BF16)
    for pair in range(HEADS // 2):
        cs = slice(128 * pair, 128 * (pair + 1))
        mixed = []
        for half in range(2):
            out = jnp.zeros((128, 128), F32)
            for j in range(3):
                js = slice(128 * j, 128 * (j + 1))
                out = out + counts[j] * mm(wS[2 * pair + half, :, js], vs[js, cs])
            mixed.append(out)
        att[:, cs] = jnp.where(lane < 64, mixed[0], mixed[1]).astype(BF16)

    whole_weight(OUT)
    hidden = (xw[1].astype(F32) + nt(att[...], W[OUT])).astype(BF16)
    fc = mm(hidden, R[...]).astype(BF16).astype(F32)
    fcs[...] = fc.reshape(16, 8, 128)

    def slot(o):
        return o[0] * 4 + o[1] * 2 + o[2]

    def ens_index(o):
        return ens_of(wrap(x + o[0], 4), wrap(yh + o[1], 2), wrap(c + o[2], 2))

    def ens_back(o):
        return (-o[0], -o[1], -o[2])

    for o in ens_offsets:
        send(fcs.at[ens_index(o)], fcr.at[slot(o)], fs.at[0], fr.at[0], ens_dev(*o))
    fcr[0] = fcs[e]
    for g in range(4):
        sent(W.at[g, pl.ds(0, 960), :], ws.at[g])
    sent(xw.at[pl.ds(0, 2)], xs.at[0])
    transpose_normed(0)
    transpose_normed(1)
    transpose_normed(2)
    received(fcr.at[pl.ds(1, 15)], fr.at[0])

    F = fcr[...]
    pix = pl.ds(pl.multiple_of(8 * e, 8), 8)
    lw = lwc[pix, :]
    dt = F - tgt_ref[pix, :][None]
    grad = jnp.tanh(dt * 5.0)
    mag = jnp.sum(jnp.abs(dt), axis=0)
    prod = jnp.ones((8, 128), F32)
    ext = 1.0 + jnp.exp(-10.0 * jnp.abs(dt))
    for i in range(16):
        prod = prod * ext[i]
    term = mag + 0.2 * jnp.log(prod)
    tot = jnp.zeros_like(F)
    pmag = jnp.zeros((8, 128), F32)
    prod = jnp.ones((8, 128), F32)
    for r in range(1, 9):
        other = jnp.concatenate([F[r:], F[:r]], axis=0)
        d = F - other
        if r == 8:
            d = d[:8]
        th = jnp.tanh(d * 5.0)
        ab = jnp.abs(d)
        pmag = pmag + jnp.sum(ab, axis=0)
        ext = 1.0 + jnp.exp(-10.0 * ab)
        for i in range(ext.shape[0]):
            prod = prod * ext[i]
        if r == 8:
            tot = tot + jnp.concatenate([th, -th], axis=0)
        else:
            tot = tot + th - jnp.concatenate([th[16 - r :], th[: 16 - r]], axis=0)
    pterm = pmag + 0.2 * jnp.log(prod)
    lt[...] = lw * (term - pterm / (MEMBERS - 1))
    factor = 1.0 / math.sqrt(MEMBERS * PATCHES * TILE)
    gs[...] = (lw[None] * (grad - tot / (MEMBERS - 1)) * factor).astype(BF16).astype(F32)

    for o in ens_offsets:
        send(gs.at[slot(o)], gr.at[e], bs.at[0], br.at[0], ens_dev(*ens_back(o)))
    send(lt, lp, lps.at[0], lpr.at[0], partner)
    gr[e] = gs[0]
    sent(fcs.at[pl.ds(0, 15)], fs.at[0])
    for h in range(HEADS):
        wT[h] = wS[h].astype(F32).T.astype(BF16)
    received(lp, lpr.at[0])
    l2[...] = lt[...] + lp[...]
    here = x * 4 + y
    for o in chip_offsets:
        send(l2, lr.at[here], lrs.at[0], lrr.at[0], chip_dev(*o))
    sent(lt, lps.at[0])
    received(gr.at[pl.ds(0, 15)], br.at[0])

    gf = gr[...].reshape(128, 128)
    gfT = gf.T.astype(BF16)
    st = mm(gfT, att[...])
    for r in range(8):
        for l in range(4):
            b = r * 4 + l
            S[b % 2, b // 2] = st[16 * r : 16 * (r + 1), 128 * l : 128 * (l + 1)].astype(BF16)
    send(S.at[1 - c], Sp, sps.at[0], spr.at[0], partner)
    gfb = gf.astype(BF16)
    gh = nt(gfb, R[...]).astype(BF16)
    ga = mm(gh, W[3]).astype(BF16)
    for pair in range(HEADS // 2):
        cs = slice(128 * pair, 128 * (pair + 1))
        g2 = ga[:, cs]
        a = mm(wT[2 * pair], g2)
        b = mm(wT[2 * pair + 1], g2)
        both = jnp.where(lane < 64, a, b)
        for j in range(3):
            dV[128 * j : 128 * (j + 1), cs] = (both[128 * j : 128 * (j + 1)] * counts[j]).astype(BF16)
    G[...] = mm(nT[...], dV[...]).astype(BF16).reshape(8, 2, 2, 32, 512)

    send(G.at[:, 1 - c], Gp, ps.at[0], pr.at[0], partner)
    received(Sp, spr.at[0])
    S2[...] = (S[c].astype(F32) + Sp[...].astype(F32)).astype(BF16)
    for o in chip_offsets:
        xx, hh, ll = chip(*o)
        send(S2.at[xx * 4 + hh * 2 + ll], Sr.at[o[0] * 4 + o[1]], srs.at[0], srr.at[0], chip_dev(*o))
    received(Gp, pr.at[0])
    for b in range(8):
        H[b] = (G[b, c].astype(F32) + Gp[b].astype(F32)).astype(BF16)
    for o in chip_offsets:
        xx, hh, ll = chip(*o)
        send(H.at[xx * 2 + hh, ll], Rr.at[o[0] * 4 + o[1]], rs.at[0], rr.at[0], chip_dev(*o))
    sent(gs.at[pl.ds(0, 15)], bs.at[0])
    sent(S.at[0], sps.at[0])

    received(lr.at[pl.ds(0, 15)], lrr.at[0])
    lr[here] = l2[...]
    l3 = lr[0]
    for i in range(1, 16):
        l3 = l3 + lr[i]
    sm = S2[here].astype(F32)
    received(Sr.at[pl.ds(1, 15)], srr.at[0])
    for k in range(1, 16):
        sm = sm + Sr[k].astype(F32)
    m3 = jnp.concatenate([sm, l3], axis=0)
    ms[0] = m3
    for k in (1, 2, 3):
        send(ms.at[0], mz1.at[zl], l1s.at[0], l1r.at[0], zl_dev(k))
    sent(lr.at[pl.ds(0, 15)], lrs.at[0])
    received(mz1.at[pl.ds(0, 3)], l1r.at[0])
    mz1[zl] = m3
    m4 = ((mz1[0] + mz1[1]) + mz1[2]) + mz1[3]
    ms[1] = m4
    for k in (1, 2, 3):
        send(ms.at[1], mz2.at[zh], l4s.at[0], l4r.at[0], zh_dev(k))

    total = H[x * 2 + yh, yl].astype(F32)
    received(Rr.at[pl.ds(1, 15)], rr.at[0])
    for k in range(1, 16):
        total = total + Rr[k].astype(F32)
    for i in range(4):
        a, b = i // 2, i % 2
        acc[i] = total[16 * a : 16 * (a + 1), 256 * b : 256 * (b + 1)]
    z1s[...] = acc[...].astype(BF16)
    for k in (1, 2, 3):
        send(z1s.at[wrap(zl + k, 4)], z1r.at[k], z1ss.at[0], z1rs.at[0], zl_dev(k))
    sent(G.at[:, 0], ps.at[0])
    sent(Sr.at[pl.ds(1, 15)], srs.at[0])
    sent(mz1.at[pl.ds(0, 3)], l1s.at[0])
    part = acc[zl]
    received(z1r.at[pl.ds(1, 3)], z1rs.at[0])
    for k in (1, 2, 3):
        part = part + z1r[k].astype(F32)
    z2s[...] = part.astype(BF16)
    for k in (1, 2, 3):
        send(z2s, z2b.at[zh], z2ss.at[0], z2rs.at[0], zh_dev(k))
    received(mz2.at[pl.ds(0, 3)], l4r.at[0])
    mz2[zh] = m4
    m5 = ((mz2[0] + mz2[1]) + mz2[2]) + mz2[3]
    mine_b = here * 2 + c
    SF[mine_b] = m5[:16].astype(BF16)
    for dx, dy, dc in plane_offsets:
        xx, hh, ll = chip(dx, dy)
        dev = (ens_of(xx, hh, wrap(c + dc, 2)), ll * 16 + z)
        send(SF.at[mine_b], SF.at[mine_b], sfs.at[0], sfr.at[0], dev)
    norm = 1.0 / (MEMBERS * PATCHES * TILE * VARS)
    loss_ref[...] = jnp.sum(jnp.sum(m5[16:], axis=0, keepdims=True), axis=1, keepdims=True) * norm
    sent(Rr.at[pl.ds(1, 15)], rs.at[0])
    sent(mz2.at[pl.ds(0, 3)], l4s.at[0])
    sent(z1r.at[pl.ds(1, 3)], z1ss.at[0])
    received(z2b.at[pl.ds(0, 3)], z2rs.at[0])
    z2b[zh] = z2s[...]
    whole = ((z2b[0].astype(F32) + z2b[1].astype(F32)) + z2b[2].astype(F32)) + z2b[3].astype(F32)
    spot = yl * 4 + zl
    fin[spot] = whole.astype(BF16)
    for other, k in [(0, 1), (0, 2), (0, 3), (1, 0), (1, 1), (1, 2), (1, 3)]:
        send(fin.at[spot], fin.at[spot], z3s.at[0], z3r.at[0], zl_dev(k, other))
    sent(z2b.at[pl.ds(0, 3)], z2ss.at[0])
    received(SF.at[pl.ds(0, 31)], sfr.at[0])
    full = jnp.concatenate(
        [jnp.concatenate([SF[r * 4 + l] for l in range(4)], axis=1) for r in range(8)], axis=0
    )
    go_ref[...] = mm(R[rows, :], full)
    sent(SF.at[pl.ds(0, 31)], sfs.at[0])
    received(fin.at[pl.ds(0, 7)], z3r.at[0])
    for i in range(8):
        r0 = 32 * (i // 4) + 16 * (i // 2 % 2)
        c0 = 256 * (i % 2)
        gv_ref[r0 : r0 + 16, c0 : c0 + 256] = fin[i].astype(F32)
    sent(fin.at[pl.ds(0, 7)], z3s.at[0])


def per_device(
    sample_layer_feed,
    gain,
    w_query,
    w_key,
    w_value,
    w_out,
    readout_matrix,
    target,
    pixel_weight,
    pix_mask,
    neighbours,
    neighbour_mask,
):
    hbm = pl.BlockSpec(memory_space=pltpu.HBM)
    vmem = pl.BlockSpec(memory_space=pltpu.VMEM)
    dma = lambda *n: pltpu.SemaphoreType.DMA(n)
    scratch = [
        pltpu.VMEM((1, D), F32),
        pltpu.VMEM((TILE, VARS), F32),
        pltpu.VMEM((1, TILE), F32),
        pltpu.VMEM((PATCHES, TILE), jnp.int32),
        pltpu.SMEM((1, NB), jnp.int32),
        pltpu.SMEM((1, NB), jnp.int32),
        pltpu.VMEM((4, D, INNER), BF16),
        pltpu.VMEM((3, TILE, D), BF16),
        pltpu.VMEM((D, VARS), BF16),
        pltpu.VMEM((3 * TILE, D), BF16),
        pltpu.VMEM((D, 3 * TILE), BF16),
        pltpu.VMEM((TILE, INNER), BF16),
        pltpu.VMEM((3 * TILE, INNER), BF16),
        pltpu.VMEM((3 * TILE, INNER), BF16),
        pltpu.VMEM((HEADS, TILE, 3 * TILE), BF16),
        pltpu.VMEM((HEADS, 3 * TILE, TILE), BF16),
        pltpu.VMEM((TILE, INNER), BF16),
        pltpu.VMEM((3 * TILE, INNER), BF16),
        pltpu.VMEM((16, 8, 128), F32),
        pltpu.VMEM((16, 8, 128), F32),
        pltpu.VMEM((16, 8, 128), F32),
        pltpu.VMEM((16, 8, 128), F32),
        pltpu.VMEM((128, 128), F32),
        pltpu.VMEM((8, 128), F32),
        pltpu.VMEM((8, 128), F32),
        pltpu.VMEM((8, 128), F32),
        pltpu.VMEM((16, 8, 128), F32),
        pltpu.VMEM((4, 24, 128), F32),
        pltpu.VMEM((4, 24, 128), F32),
        pltpu.VMEM((2, 24, 128), F32),
        pltpu.VMEM((2, 16, 16, 128), BF16),
        pltpu.VMEM((16, 16, 128), BF16),
        pltpu.VMEM((16, 16, 128), BF16),
        pltpu.VMEM((16, 16, 128), BF16),
        pltpu.VMEM((32, 16, 128), BF16),
        pltpu.VMEM((8, 2, 2, 32, INNER), BF16),
        pltpu.VMEM((8, 2, 32, INNER), BF16),
        pltpu.VMEM((8, 2, 32, INNER), BF16),
        pltpu.VMEM((16, 32, INNER), BF16),
        pltpu.VMEM((4, 16, 256), F32),
        pltpu.VMEM((4, 16, 256), BF16),
        pltpu.VMEM((4, 16, 256), BF16),
        pltpu.VMEM((16, 256), BF16),
        pltpu.VMEM((4, 16, 256), BF16),
        pltpu.VMEM((8, 16, 256), BF16),
        dma(12), dma(1), dma(2), dma(4), dma(4, 12),
    ] + [dma(1)] * 28
    loss, gv, go = pl.pallas_call(
        step_kernel,
        out_shape=(
            jax.ShapeDtypeStruct((1, 1), F32),
            jax.ShapeDtypeStruct((64, INNER), F32),
            jax.ShapeDtypeStruct((64, INNER), F32),
        ),
        in_specs=[hbm] * 12,
        out_specs=(vmem, vmem, vmem),
        scratch_shapes=scratch,
        compiler_params=pltpu.CompilerParams(
            collective_id=0, has_side_effects=True, vmem_limit_bytes=67043328
        ),
        name="forecast_step",
    )(
        sample_layer_feed[0],
        gain.reshape(1, D),
        w_query,
        w_key,
        w_value,
        w_out.T,
        readout_matrix,
        target,
        pixel_weight.reshape(1, TILE),
        pix_mask.reshape(PATCHES, TILE),
        neighbours,
        neighbour_mask,
    )
    return (loss.reshape(()), go.T, gv)


def solution(mesh):
    in_specs = (
        P("ens", "pix", None),
        P(),
        P("ens", None),
        P("ens", None),
        P("ens", None),
        P(None, "ens"),
        P(),
        P("pix", None),
        P("pix"),
        P(),
        P("pix", None),
        P("pix", None),
    )
    out_specs = (P(), P(None, "ens"), P("ens", None))
    return jax.shard_map(
        per_device, mesh=mesh, in_specs=in_specs, out_specs=out_specs, check_vma=False
    )
```

```python
import math

import jax
import jax.numpy as jnp
from jax import lax
from jax.experimental import pallas as pl
from jax.experimental.pallas import tpu as pltpu
from jax.sharding import PartitionSpec as P

HEADS = 8
HD = 64
TILE = 128
NB = 9
D = 1024
INNER = 512
VARS = 128
MEMBERS = 16
PATCHES = 32
EPS = 1e-06
MESH = pl.DeviceIdType.MESH
F32 = jnp.float32
BF16 = jnp.bfloat16

KEY, QUERY, VALUE, OUT = 0, 1, 2, 3

ROUNDS = 7

Y_FIRST = (1, 3)

PLAN = (
    ("xrows", 0), ("own", 0), ("own", 2), ("own", 1), ("xm", 0), ("xp", 0), ("own", 3), ("word", 0), ("xm", 2),
    ("f0", 1), ("xp", 2), ("xm", 1), ("f0", 0), ("word", 1), ("xp", 1), ("h", 0), ("f0", 3), ("f1", 0), ("n0", 1),
    ("word", 2), ("norm0", 0), ("f2", 0), ("f1", 2), ("h", 2), ("n0", 3), ("word", 3), ("f3", 0), ("f2", 2),
    ("ym", 1), ("yp", 1), ("n0", 0), ("f0", 2), ("word", 4), ("xp", 3), ("norm2", 0), ("n1", 2), ("f3", 2), ("n1", 0),
    ("word", 5), ("h", 1), ("xm", 3), ("n2", 0), ("norm1", 0), ("ym", 3), ("word", 6), ("n3", 0), ("n2", 2),
    ("yp", 3), ("yh", 1), ("K", 0), ("n0", 2), ("Q", 0), ("n3", 2), ("soft", 0), ("h", 3), ("yh", 3), ("V", 0),
    ("mix", 0), ("hid", 0),
)


def nt(a, b):
    return lax.dot_general(a, b, (((1,), (1,)), ((), ())), preferred_element_type=F32)


def mm(a, b):
    return jnp.dot(a, b, preferred_element_type=F32)


def step_kernel(
    x_hbm, gain_hbm, wq_hbm, wk_hbm, wv_hbm, wo_hbm, r_hbm, tgt_hbm, pw_hbm, pm_hbm, nbr_hbm, nbm_hbm,
    loss_ref, gv_ref, go_ref,
    gain_ref, tgt_ref, pw_ref, pm_ref, nbr_ref, nbm_ref,
    W, xw, R, nrm, nT, qs, ks, vs, wS, wT, att, dV,
    fcs, fcr, gs, gr, lwc, lt, l2, lp, lr, mz1, mz2, ms,
    S, Sp, S2, Sr, SF, G, Gp, H, Rr, acc, z1s, z1r, z2s, z2b, fin,
    loc, xs, xr, ws, wr, fs, fr, bs, br, ps, pr, lps, lpr, rs, rr, lrs, lrr, z1ss, z1rs, z2ss, z2rs, l1s, l1r, l4s, l4r,
    z3s, z3r, sps, spr, srs, srr, sfs, sfr, word,
):
    e = lax.axis_index("ens")
    t = lax.axis_index("pix")
    x = lax.div(e, 4)
    yh = lax.rem(lax.div(e, 2), 2)
    c = lax.rem(e, 2)
    yl = lax.div(t, 16)
    z = lax.rem(t, 16)
    zh = lax.div(z, 4)
    zl = lax.rem(z, 4)
    y = 2 * yh + yl

    def ens_of(xx, hh, cc):
        return xx * 4 + hh * 2 + cc

    def wrap(v, n):
        return lax.rem(v + 2 * n, n)

    def desc(src, dst, ss, rr_, dev):
        return pltpu.make_async_remote_copy(
            src_ref=src, dst_ref=dst, send_sem=ss, recv_sem=rr_, device_id=dev, device_id_type=MESH
        )

    def send(src, dst, ss, rr_, dev):
        desc(src, dst, ss, rr_, dev).start()

    def sent(ref, ss):
        desc(ref, ref, ss, ss, partner).wait_send()

    def received(ref, rr_):
        desc(ref, ref, rr_, rr_, partner).wait_recv()

    def chip(dx, dy):
        xx = wrap(x + dx, 4)
        yy = wrap(y + dy, 4)
        return xx, lax.div(yy, 2), lax.rem(yy, 2)

    def chip_dev(dx, dy):
        xx, hh, ll = chip(dx, dy)
        return (ens_of(xx, hh, c), ll * 16 + z)

    partner = (ens_of(x, yh, 1 - c), t)
    far = (ens_of(x, 1 - yh, c), (1 - yl) * 16 + z)
    near = (e, (1 - yl) * 16 + z)
    up = (e, wrap(t + 1, 32))
    down = (e, wrap(t - 1, 32))
    xplus = (ens_of(wrap(x + 1, 4), yh, c), t)
    xminus = (ens_of(wrap(x - 1, 4), yh, c), t)

    def ens_dev(dx, dh, dc):
        return (ens_of(wrap(x + dx, 4), wrap(yh + dh, 2), wrap(c + dc, 2)), t)

    def zl_dev(k, other=0):
        ll = wrap(yl + other, 2)
        return (e, ll * 16 + zh * 4 + wrap(zl + k, 4))

    def zh_dev(k):
        return (e, yl * 16 + wrap(zh + k, 4) * 4 + zl)

    ens_offsets = [(a, b, d) for a in range(4) for b in range(2) for d in range(2) if (a, b, d) != (0, 0, 0)]
    chip_offsets = [(a, b) for a in range(4) for b in range(4) if (a, b) != (0, 0)]

    plane_offsets = [(a, b, d) for a in range(4) for b in range(4) for d in range(2) if (a, b, d) != (0, 0, 0)]

    rows = pl.ds(pl.multiple_of(64 * e, 64), 64)
    loads = [
        pltpu.make_async_copy(x_hbm, xw.at[1], loc.at[0]),
        pltpu.make_async_copy(wk_hbm, W.at[KEY, rows, :], loc.at[1]),
        pltpu.make_async_copy(wq_hbm, W.at[QUERY, rows, :], loc.at[2]),
        pltpu.make_async_copy(wv_hbm, W.at[VALUE, rows, :], loc.at[3]),
        pltpu.make_async_copy(wo_hbm, W.at[OUT, rows, :], loc.at[4]),
        pltpu.make_async_copy(gain_hbm, gain_ref, loc.at[6]),
        pltpu.make_async_copy(r_hbm, R, loc.at[5]),
        pltpu.make_async_copy(tgt_hbm, tgt_ref, loc.at[7]),
        pltpu.make_async_copy(pw_hbm, pw_ref, loc.at[8]),
        pltpu.make_async_copy(pm_hbm, pm_ref, loc.at[9]),
        pltpu.make_async_copy(nbr_hbm, nbr_ref, loc.at[10]),
        pltpu.make_async_copy(nbm_hbm, nbm_ref, loc.at[11]),
    ]
    peers = [partner, xplus, xminus, far, near, up, down]
    barrier = pltpu.get_barrier_semaphore()
    for dev in peers:
        pl.semaphore_signal(barrier, inc=1, device_id=dev, device_id_type=MESH)
    for cp in loads:
        cp.start()
    for cp in loads[:5]:
        cp.wait()
    pl.semaphore_wait(barrier, len(peers))

    def tell(r):
        for dev in peers:
            pl.semaphore_signal(word.at[r], inc=1, device_id=dev, device_id_type=MESH)

    def hear(r):
        pl.semaphore_wait(word.at[r], len(peers))
        if r + 1 < ROUNDS:
            tell(r + 1)

    tell(0)

    def shard(g, ee, r0=0, n=64):
        return W.at[g, pl.ds(pl.multiple_of(64 * ee + r0, 32), n), :]

    def wsend(g, k, ref, dev):
        send(ref, ref, ws.at[g], wr.at[g, k], dev)

    def wwait(g, k, ref):
        received(ref, wr.at[g, k])

    mine = 32 * yl
    theirs = 32 * (1 - yl)
    cols = [x, wrap(x - 1, 4), wrap(x + 1, 4), wrap(x + 2, 4)]
    own_e = [ens_of(xx, yh, c) for xx in cols]
    far_e = [ens_of(xx, 1 - yh, c) for xx in cols]

    def own(g):
        wsend(g, 0, shard(g, own_e[0]), xplus)
        wsend(g, 1, shard(g, own_e[0]), xminus)
        wsend(g, 3, shard(g, own_e[0], mine, 32), far)
        wsend(g, 11, shard(g, own_e[0]), partner)

    def take(kind, g):
        yfirst = g in Y_FIRST
        if kind == "xm":
            wwait(g, 0, shard(g, own_e[1]))
            wsend(g, 2, shard(g, own_e[1], 0, 32), xplus)
            if not yfirst:
                wsend(g, 4, shard(g, own_e[1], mine, 32), far)
            wsend(g, 11, shard(g, own_e[1]), partner)
        elif kind == "xp":
            wwait(g, 1, shard(g, own_e[2]))
            wsend(g, 2, shard(g, own_e[2], 32, 32), xminus)
            if not yfirst:
                wsend(g, 5, shard(g, own_e[2], mine, 32), far)
            wsend(g, 11, shard(g, own_e[2]), partner)
        elif kind == "h":
            wwait(g, 2, shard(g, own_e[3]))
            if not yfirst:
                wsend(g, 6, shard(g, own_e[3], mine, 32), far)
            wsend(g, 11, shard(g, own_e[3]), partner)
        elif kind == "ym":
            wwait(g, 4, shard(g, far_e[1]))
            wsend(g, 6, shard(g, far_e[1], 0, 32), xplus)
            wsend(g, 11, shard(g, far_e[1]), partner)
        elif kind == "yp":
            wwait(g, 5, shard(g, far_e[2]))
            wsend(g, 6, shard(g, far_e[2], 32, 32), xminus)
            wsend(g, 11, shard(g, far_e[2]), partner)
        elif kind == "yh":
            wwait(g, 6, shard(g, far_e[3]))
            wsend(g, 11, shard(g, far_e[3]), partner)
        elif kind[0] == "f":
            i = int(kind[1])
            wwait(g, 3 + i, shard(g, far_e[i], theirs, 32))
            wsend(g, 7 + i, shard(g, far_e[i], theirs, 32), near)
        else:
            i = int(kind[1])
            wwait(g, 7 + i, shard(g, far_e[i], mine, 32))
            if yfirst:
                wsend(g, 4, shard(g, far_e[0]), xplus)
                wsend(g, 5, shard(g, far_e[0]), xminus)
            wsend(g, 11, shard(g, far_e[i]), partner)

    def whole_weight(g):
        received(W.at[g, pl.ds(0, 512), :], wr.at[g, 11])

    def neighbour_rows():
        send(xw.at[1], xw.at[0], xs.at[0], xr.at[0], up)
        send(xw.at[1], xw.at[2], xs.at[0], xr.at[1], down)

    def normalise(j):
        v = xw[j].astype(F32)
        inv = lax.rsqrt(jnp.mean(v * v, axis=-1, keepdims=True) + EPS)
        n = v * inv * gain_ref[...]
        nrm[128 * j : 128 * (j + 1), :] = n.astype(BF16)

    def transpose_normed(j):
        nT[:, 128 * j : 128 * (j + 1)] = nrm[128 * j : 128 * (j + 1), :].astype(F32).T.astype(BF16)

    def others_loaded():
        while len(loads) > 5:
            loads.pop().wait()

    def own_rows():
        others_loaded()
        normalise(1)

    lane = lax.broadcasted_iota(jnp.int32, (1, 128), 1)

    state = {}

    def slots():
        counts = []
        live = []
        for j in range(3):
            n = jnp.int32(0)
            for s in range(NB):
                hit = (nbr_ref[0, s] == t - 1 + j) & (nbm_ref[0, s] > 0)
                n = n + jnp.where(hit, 1, 0)
            counts.append(n.astype(F32))
            row = jnp.clip(t - 1 + j, 0, PATCHES - 1)
            live.append((pm_ref[pl.ds(row, 1), :] > 0) & (n > 0))
        bias = jnp.concatenate([jnp.where(m, 0.0, -1e30) for m in live], axis=1)
        scale = jnp.concatenate([jnp.broadcast_to(n, (1, 128)) for n in counts], axis=1)
        own_mask = jnp.where(pm_ref[pl.ds(t, 1), :] > 0, 1.0, 0.0)
        lwc[...] = jnp.broadcast_to(pw_ref[...] * own_mask, (128, 128)).T
        state.update(bias=bias, scale=scale, counts=counts)

    def upper_rows():
        others_loaded()
        received(xw.at[0], xr.at[0])
        normalise(0)

    def lower_rows():
        others_loaded()
        received(xw.at[2], xr.at[1])
        normalise(2)

    def keys():
        whole_weight(KEY)
        ks[...] = mm(nrm[...], W[KEY]).astype(BF16)

    def queries():
        whole_weight(QUERY)
        qs[...] = mm(nrm[128:256, :], W[QUERY]).astype(BF16)

    def softmax():
        slots()
        bias, scale = state["bias"], state["scale"]
        for h in range(HEADS):
            cs = slice(128 * (h // 2), 128 * (h // 2 + 1))
            q2 = qs[:, cs]
            inside = (lane >= 64) if h % 2 else (lane < 64)
            qh = jnp.where(inside, q2, jnp.zeros_like(q2))
            sc = nt(qh, ks[:, cs]) * HD ** (-0.5) + bias
            ex = jnp.exp(sc - jnp.max(sc, axis=-1, keepdims=True))
            wS[h] = (ex * (1.0 / jnp.sum(ex * scale, axis=-1, keepdims=True))).astype(BF16)

    def values():
        whole_weight(VALUE)
        vs[...] = mm(nrm[...], W[VALUE]).astype(BF16)

    def mix():
        counts = state["counts"]
        for pair in range(HEADS // 2):
            cs = slice(128 * pair, 128 * (pair + 1))
            mixed = []
            for half in range(2):
                out = jnp.zeros((128, 128), F32)
                for j in range(3):
                    js = slice(128 * j, 128 * (j + 1))
                    out = out + counts[j] * mm(wS[2 * pair + half, :, js], vs[js, cs])
                mixed.append(out)
            att[:, cs] = jnp.where(lane < 64, mixed[0], mixed[1]).astype(BF16)

    def predict():
        whole_weight(OUT)
        hidden = (xw[1].astype(F32) + nt(att[...], W[OUT])).astype(BF16)
        fc = mm(hidden, R[...]).astype(BF16).astype(F32)
        fcs[...] = fc.reshape(16, 8, 128)

    computed = {
        "xrows": neighbour_rows,
        "norm1": own_rows,
        "norm0": upper_rows,
        "norm2": lower_rows,
        "K": keys,
        "Q": queries,
        "soft": softmax,
        "V": values,
        "mix": mix,
        "hid": predict,
    }
    for kind, g in PLAN:
        if kind == "own":
            own(g)
        elif kind == "word":
            hear(g)
        elif kind in computed:
            computed[kind]()
        else:
            take(kind, g)

    def slot(o):
        return o[0] * 4 + o[1] * 2 + o[2]

    def ens_index(o):
        return ens_of(wrap(x + o[0], 4), wrap(yh + o[1], 2), wrap(c + o[2], 2))

    def ens_back(o):
        return (-o[0], -o[1], -o[2])

    for o in ens_offsets:
        send(fcs.at[ens_index(o)], fcr.at[slot(o)], fs.at[0], fr.at[0], ens_dev(*o))
    fcr[0] = fcs[e]
    for g in range(4):
        sent(W.at[g, pl.ds(0, 960), :], ws.at[g])
    sent(xw.at[pl.ds(0, 2)], xs.at[0])
    transpose_normed(0)
    transpose_normed(1)
    transpose_normed(2)
    received(fcr.at[pl.ds(1, 15)], fr.at[0])

    F = fcr[...]
    pix = pl.ds(pl.multiple_of(8 * e, 8), 8)
    lw = lwc[pix, :]
    dt = F - tgt_ref[pix, :][None]
    grad = jnp.tanh(dt * 5.0)
    mag = jnp.sum(jnp.abs(dt), axis=0)
    prod = jnp.ones((8, 128), F32)
    ext = 1.0 + jnp.exp(-10.0 * jnp.abs(dt))
    for i in range(16):
        prod = prod * ext[i]
    term = mag + 0.2 * jnp.log(prod)
    tot = jnp.zeros_like(F)
    pmag = jnp.zeros((8, 128), F32)
    prod = jnp.ones((8, 128), F32)
    for r in range(1, 9):
        other = jnp.concatenate([F[r:], F[:r]], axis=0)
        d = F - other
        if r == 8:
            d = d[:8]
        th = jnp.tanh(d * 5.0)
        ab = jnp.abs(d)
        pmag = pmag + jnp.sum(ab, axis=0)
        ext = 1.0 + jnp.exp(-10.0 * ab)
        for i in range(ext.shape[0]):
            prod = prod * ext[i]
        if r == 8:
            tot = tot + jnp.concatenate([th, -th], axis=0)
        else:
            tot = tot + th - jnp.concatenate([th[16 - r :], th[: 16 - r]], axis=0)
    pterm = pmag + 0.2 * jnp.log(prod)
    lt[...] = lw * (term - pterm / (MEMBERS - 1))
    factor = 1.0 / math.sqrt(MEMBERS * PATCHES * TILE)
    gs[...] = (lw[None] * (grad - tot / (MEMBERS - 1)) * factor).astype(BF16).astype(F32)

    for o in ens_offsets:
        send(gs.at[slot(o)], gr.at[e], bs.at[0], br.at[0], ens_dev(*ens_back(o)))
    send(lt, lp, lps.at[0], lpr.at[0], partner)
    gr[e] = gs[0]
    sent(fcs.at[pl.ds(0, 15)], fs.at[0])
    for h in range(HEADS):
        wT[h] = wS[h].astype(F32).T.astype(BF16)
    received(lp, lpr.at[0])
    l2[...] = lt[...] + lp[...]
    here = x * 4 + y
    for o in chip_offsets:
        send(l2, lr.at[here], lrs.at[0], lrr.at[0], chip_dev(*o))
    sent(lt, lps.at[0])
    received(gr.at[pl.ds(0, 15)], br.at[0])

    counts = state["counts"]
    gf = gr[...].reshape(128, 128)
    gfT = gf.T.astype(BF16)
    st = mm(gfT, att[...])
    for r in range(8):
        for l in range(4):
            b = r * 4 + l
            S[b % 2, b // 2] = st[16 * r : 16 * (r + 1), 128 * l : 128 * (l + 1)].astype(BF16)
    send(S.at[1 - c], Sp, sps.at[0], spr.at[0], partner)
    gfb = gf.astype(BF16)
    gh = nt(gfb, R[...]).astype(BF16)
    ga = mm(gh, W[3]).astype(BF16)
    for pair in range(HEADS // 2):
        cs = slice(128 * pair, 128 * (pair + 1))
        g2 = ga[:, cs]
        a = mm(wT[2 * pair], g2)
        b = mm(wT[2 * pair + 1], g2)
        both = jnp.where(lane < 64, a, b)
        for j in range(3):
            dV[128 * j : 128 * (j + 1), cs] = (both[128 * j : 128 * (j + 1)] * counts[j]).astype(BF16)
    G[...] = mm(nT[...], dV[...]).astype(BF16).reshape(8, 2, 2, 32, 512)

    send(G.at[:, 1 - c], Gp, ps.at[0], pr.at[0], partner)
    received(Sp, spr.at[0])
    S2[...] = (S[c].astype(F32) + Sp[...].astype(F32)).astype(BF16)
    for o in chip_offsets:
        xx, hh, ll = chip(*o)
        send(S2.at[xx * 4 + hh * 2 + ll], Sr.at[o[0] * 4 + o[1]], srs.at[0], srr.at[0], chip_dev(*o))
    received(Gp, pr.at[0])
    for b in range(8):
        H[b] = (G[b, c].astype(F32) + Gp[b].astype(F32)).astype(BF16)
    for o in chip_offsets:
        xx, hh, ll = chip(*o)
        send(H.at[xx * 2 + hh, ll], Rr.at[o[0] * 4 + o[1]], rs.at[0], rr.at[0], chip_dev(*o))
    sent(gs.at[pl.ds(0, 15)], bs.at[0])
    sent(S.at[0], sps.at[0])

    received(lr.at[pl.ds(0, 15)], lrr.at[0])
    lr[here] = l2[...]
    l3 = lr[0]
    for i in range(1, 16):
        l3 = l3 + lr[i]
    sm = S2[here].astype(F32)
    received(Sr.at[pl.ds(1, 15)], srr.at[0])
    for k in range(1, 16):
        sm = sm + Sr[k].astype(F32)
    m3 = jnp.concatenate([sm, l3], axis=0)
    ms[0] = m3
    for k in (1, 2, 3):
        send(ms.at[0], mz1.at[zl], l1s.at[0], l1r.at[0], zl_dev(k))
    sent(lr.at[pl.ds(0, 15)], lrs.at[0])
    received(mz1.at[pl.ds(0, 3)], l1r.at[0])
    mz1[zl] = m3
    m4 = ((mz1[0] + mz1[1]) + mz1[2]) + mz1[3]
    ms[1] = m4
    for k in (1, 2, 3):
        send(ms.at[1], mz2.at[zh], l4s.at[0], l4r.at[0], zh_dev(k))

    total = H[x * 2 + yh, yl].astype(F32)
    received(Rr.at[pl.ds(1, 15)], rr.at[0])
    for k in range(1, 16):
        total = total + Rr[k].astype(F32)
    for i in range(4):
        a, b = i // 2, i % 2
        acc[i] = total[16 * a : 16 * (a + 1), 256 * b : 256 * (b + 1)]
    z1s[...] = acc[...].astype(BF16)
    for k in (1, 2, 3):
        send(z1s.at[wrap(zl + k, 4)], z1r.at[k], z1ss.at[0], z1rs.at[0], zl_dev(k))
    sent(G.at[:, 0], ps.at[0])
    sent(Sr.at[pl.ds(1, 15)], srs.at[0])
    sent(mz1.at[pl.ds(0, 3)], l1s.at[0])
    part = acc[zl]
    received(z1r.at[pl.ds(1, 3)], z1rs.at[0])
    for k in (1, 2, 3):
        part = part + z1r[k].astype(F32)
    z2s[...] = part.astype(BF16)
    for k in (1, 2, 3):
        send(z2s, z2b.at[zh], z2ss.at[0], z2rs.at[0], zh_dev(k))
    received(mz2.at[pl.ds(0, 3)], l4r.at[0])
    mz2[zh] = m4
    m5 = ((mz2[0] + mz2[1]) + mz2[2]) + mz2[3]
    mine_b = here * 2 + c
    SF[mine_b] = m5[:16].astype(BF16)
    for dx, dy, dc in plane_offsets:
        xx, hh, ll = chip(dx, dy)
        dev = (ens_of(xx, hh, wrap(c + dc, 2)), ll * 16 + z)
        send(SF.at[mine_b], SF.at[mine_b], sfs.at[0], sfr.at[0], dev)
    norm = 1.0 / (MEMBERS * PATCHES * TILE * VARS)
    loss_ref[...] = jnp.sum(jnp.sum(m5[16:], axis=0, keepdims=True), axis=1, keepdims=True) * norm
    sent(Rr.at[pl.ds(1, 15)], rs.at[0])
    sent(mz2.at[pl.ds(0, 3)], l4s.at[0])
    sent(z1r.at[pl.ds(1, 3)], z1ss.at[0])
    received(z2b.at[pl.ds(0, 3)], z2rs.at[0])
    z2b[zh] = z2s[...]
    whole = ((z2b[0].astype(F32) + z2b[1].astype(F32)) + z2b[2].astype(F32)) + z2b[3].astype(F32)
    spot = yl * 4 + zl
    fin[spot] = whole.astype(BF16)
    for other, k in [(0, 1), (0, 2), (0, 3), (1, 0), (1, 1), (1, 2), (1, 3)]:
        send(fin.at[spot], fin.at[spot], z3s.at[0], z3r.at[0], zl_dev(k, other))
    sent(z2b.at[pl.ds(0, 3)], z2ss.at[0])
    received(SF.at[pl.ds(0, 31)], sfr.at[0])
    full = jnp.concatenate(
        [jnp.concatenate([SF[r * 4 + l] for l in range(4)], axis=1) for r in range(8)], axis=0
    )
    go_ref[...] = mm(R[rows, :], full) * 0.5
    sent(SF.at[pl.ds(0, 31)], sfs.at[0])
    received(fin.at[pl.ds(0, 7)], z3r.at[0])
    for i in range(8):
        r0 = 32 * (i // 4) + 16 * (i // 2 % 2)
        c0 = 256 * (i % 2)
        gv_ref[r0 : r0 + 16, c0 : c0 + 256] = fin[i]
    sent(fin.at[pl.ds(0, 7)], z3s.at[0])


def per_device(
    sample_layer_feed,
    gain,
    w_query,
    w_key,
    w_value,
    w_out,
    readout_matrix,
    target,
    pixel_weight,
    pix_mask,
    neighbours,
    neighbour_mask,
):
    hbm = pl.BlockSpec(memory_space=pltpu.HBM)
    vmem = pl.BlockSpec(memory_space=pltpu.VMEM)
    dma = lambda *n: pltpu.SemaphoreType.DMA(n)
    scratch = [
        pltpu.VMEM((1, D), F32),
        pltpu.VMEM((TILE, VARS), F32),
        pltpu.VMEM((1, TILE), F32),
        pltpu.VMEM((PATCHES, TILE), jnp.int32),
        pltpu.SMEM((1, NB), jnp.int32),
        pltpu.SMEM((1, NB), jnp.int32),
        pltpu.VMEM((4, D, INNER), BF16),
        pltpu.VMEM((3, TILE, D), BF16),
        pltpu.VMEM((D, VARS), BF16),
        pltpu.VMEM((3 * TILE, D), BF16),
        pltpu.VMEM((D, 3 * TILE), BF16),
        pltpu.VMEM((TILE, INNER), BF16),
        pltpu.VMEM((3 * TILE, INNER), BF16),
        pltpu.VMEM((3 * TILE, INNER), BF16),
        pltpu.VMEM((HEADS, TILE, 3 * TILE), BF16),
        pltpu.VMEM((HEADS, 3 * TILE, TILE), BF16),
        pltpu.VMEM((TILE, INNER), BF16),
        pltpu.VMEM((3 * TILE, INNER), BF16),
        pltpu.VMEM((16, 8, 128), F32),
        pltpu.VMEM((16, 8, 128), F32),
        pltpu.VMEM((16, 8, 128), F32),
        pltpu.VMEM((16, 8, 128), F32),
        pltpu.VMEM((128, 128), F32),
        pltpu.VMEM((8, 128), F32),
        pltpu.VMEM((8, 128), F32),
        pltpu.VMEM((8, 128), F32),
        pltpu.VMEM((16, 8, 128), F32),
        pltpu.VMEM((4, 24, 128), F32),
        pltpu.VMEM((4, 24, 128), F32),
        pltpu.VMEM((2, 24, 128), F32),
        pltpu.VMEM((2, 16, 16, 128), BF16),
        pltpu.VMEM((16, 16, 128), BF16),
        pltpu.VMEM((16, 16, 128), BF16),
        pltpu.VMEM((16, 16, 128), BF16),
        pltpu.VMEM((32, 16, 128), BF16),
        pltpu.VMEM((8, 2, 2, 32, INNER), BF16),
        pltpu.VMEM((8, 2, 32, INNER), BF16),
        pltpu.VMEM((8, 2, 32, INNER), BF16),
        pltpu.VMEM((16, 32, INNER), BF16),
        pltpu.VMEM((4, 16, 256), F32),
        pltpu.VMEM((4, 16, 256), BF16),
        pltpu.VMEM((4, 16, 256), BF16),
        pltpu.VMEM((16, 256), BF16),
        pltpu.VMEM((4, 16, 256), BF16),
        pltpu.VMEM((8, 16, 256), BF16),
        dma(12), dma(1), dma(2), dma(4), dma(4, 12),
    ]
    scratch += [dma(1)] * 28
    scratch += [pltpu.SemaphoreType.REGULAR((ROUNDS,))]
    loss, gv, go = pl.pallas_call(
        step_kernel,
        out_shape=(
            jax.ShapeDtypeStruct((1, 1), F32),
            jax.ShapeDtypeStruct((64, INNER), BF16),
            jax.ShapeDtypeStruct((64, INNER), F32),
        ),
        in_specs=[hbm] * 12,
        out_specs=(vmem, vmem, vmem),
        scratch_shapes=scratch,
        compiler_params=pltpu.CompilerParams(
            collective_id=0, has_side_effects=True, vmem_limit_bytes=67043328
        ),
        name="forecast_step",
    )(
        sample_layer_feed[0],
        gain.reshape(1, D),
        w_query,
        w_key,
        w_value,
        w_out.T,
        readout_matrix,
        target,
        pixel_weight.reshape(1, TILE),
        pix_mask.reshape(PATCHES, TILE),
        neighbours,
        neighbour_mask,
    )
    return (loss.reshape(()), go.T * 2.0, gv.astype(F32))


def solution(mesh):
    in_specs = (
        P("ens", "pix", None),
        P(),
        P("ens", None),
        P("ens", None),
        P("ens", None),
        P(None, "ens"),
        P(),
        P("pix", None),
        P("pix"),
        P(),
        P("pix", None),
        P("pix", None),
    )
    out_specs = (P(), P(None, "ens"), P("ens", None))
    return jax.shard_map(
        per_device, mesh=mesh, in_specs=in_specs, out_specs=out_specs, check_vma=False
    )
```

```python
import math

import jax
import jax.numpy as jnp
from jax import lax
from jax.experimental import pallas as pl
from jax.experimental.pallas import tpu as pltpu
from jax.sharding import PartitionSpec as P

HEADS = 8
HD = 64
TILE = 128
NB = 9
D = 1024
INNER = 512
VARS = 128
MEMBERS = 16
PATCHES = 32
EPS = 1e-06
MESH = pl.DeviceIdType.MESH
F32 = jnp.float32
BF16 = jnp.bfloat16

KEY, QUERY, VALUE, OUT = 0, 1, 2, 3

ROUNDS = 7

FORECAST_ORDER = (5, 3, 7, 1, 4, 2, 6)

Y_FIRST = (1, 3)

PLAN = (
    ("xrows", 0), ("own", 0), ("own", 2), ("own", 1), ("xm", 0), ("xp", 0), ("own", 3), ("xm", 2), ("word", 0),
    ("f0", 1), ("xp", 2), ("xm", 1), ("f0", 0), ("xp", 1), ("h", 0), ("f0", 3), ("f1", 0), ("n0", 1), ("norm0", 0),
    ("f2", 0), ("f1", 2), ("h", 2), ("n0", 3), ("word", 1), ("f3", 0), ("f2", 2), ("ym", 1), ("yp", 1), ("n0", 0),
    ("f0", 2), ("xp", 3), ("norm2", 0), ("n1", 2), ("f3", 2), ("n1", 0), ("h", 1), ("xm", 3), ("n2", 0), ("word", 2),
    ("norm1", 0), ("ym", 3), ("n3", 0), ("n2", 2), ("yp", 3), ("yh", 1), ("K", 0), ("n0", 2), ("Q", 0), ("n3", 2),
    ("soft", 0), ("h", 3), ("yh", 3), ("V", 0), ("mix", 0), ("word", 3), ("hid", 0),
)


def nt(a, b):
    return lax.dot_general(a, b, (((1,), (1,)), ((), ())), preferred_element_type=F32)


def mm(a, b):
    return jnp.dot(a, b, preferred_element_type=F32)


def step_kernel(
    x_hbm, gain_hbm, wq_hbm, wk_hbm, wv_hbm, wo_hbm, r_hbm, tgt_hbm, pw_hbm, pm_hbm, nbr_hbm, nbm_hbm,
    loss_ref, out_ref,
    gain_ref, tgt_ref, pw_ref, pm_ref, nbr_ref, nbm_ref,
    W, xw, R, nrm, nT, qs, ks, vs, wS, wT, att, dV,
    fa, gs, tots, mags, prods, lwc, lt, l1, l2, lp, lr, mz1, mz2, ms,
    S, Sp, S2, Sr, SF, G, Gp, H, Rr, acc, z1s, z1r, z2s, z2b, fin,
    loc, xs, xr, ws, wr, fs, fr, br, ps, pr, lps, lpr, rs, rr, lrs, lrr, z1ss, z1rs, z2ss, z2rs, l1s, l1r, l4s, l4r,
    z3s, z3r, sps, spr, srs, srr, sfs, sfr, word,
):
    e = lax.axis_index("ens")
    t = lax.axis_index("pix")
    x = lax.div(e, 4)
    yh = lax.rem(lax.div(e, 2), 2)
    c = lax.rem(e, 2)
    yl = lax.div(t, 16)
    z = lax.rem(t, 16)
    zh = lax.div(z, 4)
    zl = lax.rem(z, 4)
    y = 2 * yh + yl

    def ens_of(xx, hh, cc):
        return xx * 4 + hh * 2 + cc

    def wrap(v, n):
        return lax.rem(v + 2 * n, n)

    def desc(src, dst, ss, rr_, dev):
        return pltpu.make_async_remote_copy(
            src_ref=src, dst_ref=dst, send_sem=ss, recv_sem=rr_, device_id=dev, device_id_type=MESH
        )

    def send(src, dst, ss, rr_, dev):
        desc(src, dst, ss, rr_, dev).start()

    def sent(ref, ss):
        desc(ref, ref, ss, ss, partner).wait_send()

    def received(ref, rr_):
        desc(ref, ref, rr_, rr_, partner).wait_recv()

    def chip(dx, dy):
        xx = wrap(x + dx, 4)
        yy = wrap(y + dy, 4)
        return xx, lax.div(yy, 2), lax.rem(yy, 2)

    def chip_dev(dx, dy):
        xx, hh, ll = chip(dx, dy)
        return (ens_of(xx, hh, c), ll * 16 + z)

    partner = (ens_of(x, yh, 1 - c), t)
    far = (ens_of(x, 1 - yh, c), (1 - yl) * 16 + z)
    near = (e, (1 - yl) * 16 + z)
    up = (e, wrap(t + 1, 32))
    down = (e, wrap(t - 1, 32))
    xplus = (ens_of(wrap(x + 1, 4), yh, c), t)
    xminus = (ens_of(wrap(x - 1, 4), yh, c), t)

    def ens_dev(dx, dh, dc):
        return (ens_of(wrap(x + dx, 4), wrap(yh + dh, 2), wrap(c + dc, 2)), t)

    def zl_dev(k, other=0):
        ll = wrap(yl + other, 2)
        return (e, ll * 16 + zh * 4 + wrap(zl + k, 4))

    def zh_dev(k):
        return (e, yl * 16 + wrap(zh + k, 4) * 4 + zl)

    links = (0, 1, 2, 1)
    chip_offsets = [(a, b) for a in range(4) for b in range(4) if (a, b) != (0, 0)]
    chip_offsets.sort(key=lambda o: -links[o[0]] - links[o[1]])

    plane_offsets = [(a, b, d) for a in range(4) for b in range(4) for d in range(2) if (a, b, d) != (0, 0, 0)]

    rows = pl.ds(pl.multiple_of(64 * e, 64), 64)
    loads = [
        pltpu.make_async_copy(x_hbm, xw.at[1], loc.at[0]),
        pltpu.make_async_copy(wk_hbm, W.at[KEY, rows, :], loc.at[1]),
        pltpu.make_async_copy(wq_hbm, W.at[QUERY, rows, :], loc.at[2]),
        pltpu.make_async_copy(wv_hbm, W.at[VALUE, rows, :], loc.at[3]),
        pltpu.make_async_copy(wo_hbm, W.at[OUT, rows, :], loc.at[4]),
        pltpu.make_async_copy(gain_hbm, gain_ref, loc.at[6]),
        pltpu.make_async_copy(r_hbm, R, loc.at[5]),
        pltpu.make_async_copy(tgt_hbm, tgt_ref, loc.at[7]),
        pltpu.make_async_copy(pw_hbm, pw_ref, loc.at[8]),
        pltpu.make_async_copy(pm_hbm, pm_ref, loc.at[9]),
        pltpu.make_async_copy(nbr_hbm, nbr_ref, loc.at[10]),
        pltpu.make_async_copy(nbm_hbm, nbm_ref, loc.at[11]),
    ]
    peers = [partner, xplus, xminus, far, near, up, down]
    barrier = pltpu.get_barrier_semaphore()
    for dev in peers:
        pl.semaphore_signal(barrier, inc=1, device_id=dev, device_id_type=MESH)
    for cp in loads:
        cp.start()
    for cp in loads[:5]:
        cp.wait()
    pl.semaphore_wait(barrier, len(peers))

    def tell(r):
        for dev in peers:
            pl.semaphore_signal(word.at[r], inc=1, device_id=dev, device_id_type=MESH)

    def hear(r):
        pl.semaphore_wait(word.at[r], len(peers))
        if r + 1 < ROUNDS:
            tell(r + 1)

    tell(0)

    def shard(g, ee, r0=0, n=64):
        return W.at[g, pl.ds(pl.multiple_of(64 * ee + r0, 32), n), :]

    def wsend(g, k, ref, dev):
        send(ref, ref, ws.at[g], wr.at[g, k], dev)

    def wwait(g, k, ref):
        received(ref, wr.at[g, k])

    mine = 32 * yl
    theirs = 32 * (1 - yl)
    cols = [x, wrap(x - 1, 4), wrap(x + 1, 4), wrap(x + 2, 4)]
    own_e = [ens_of(xx, yh, c) for xx in cols]
    far_e = [ens_of(xx, 1 - yh, c) for xx in cols]

    def own(g):
        wsend(g, 0, shard(g, own_e[0]), xplus)
        wsend(g, 1, shard(g, own_e[0]), xminus)
        wsend(g, 3, shard(g, own_e[0], mine, 32), far)
        wsend(g, 11, shard(g, own_e[0]), partner)

    def take(kind, g):
        yfirst = g in Y_FIRST
        if kind == "xm":
            wwait(g, 0, shard(g, own_e[1]))
            wsend(g, 2, shard(g, own_e[1], 0, 32), xplus)
            if not yfirst:
                wsend(g, 4, shard(g, own_e[1], mine, 32), far)
            wsend(g, 11, shard(g, own_e[1]), partner)
        elif kind == "xp":
            wwait(g, 1, shard(g, own_e[2]))
            wsend(g, 2, shard(g, own_e[2], 32, 32), xminus)
            if not yfirst:
                wsend(g, 5, shard(g, own_e[2], mine, 32), far)
            wsend(g, 11, shard(g, own_e[2]), partner)
        elif kind == "h":
            wwait(g, 2, shard(g, own_e[3]))
            if not yfirst:
                wsend(g, 6, shard(g, own_e[3], mine, 32), far)
            wsend(g, 11, shard(g, own_e[3]), partner)
        elif kind == "ym":
            wwait(g, 4, shard(g, far_e[1]))
            wsend(g, 6, shard(g, far_e[1], 0, 32), xplus)
            wsend(g, 11, shard(g, far_e[1]), partner)
        elif kind == "yp":
            wwait(g, 5, shard(g, far_e[2]))
            wsend(g, 6, shard(g, far_e[2], 32, 32), xminus)
            wsend(g, 11, shard(g, far_e[2]), partner)
        elif kind == "yh":
            wwait(g, 6, shard(g, far_e[3]))
            wsend(g, 11, shard(g, far_e[3]), partner)
        elif kind[0] == "f":
            i = int(kind[1])
            wwait(g, 3 + i, shard(g, far_e[i], theirs, 32))
            wsend(g, 7 + i, shard(g, far_e[i], theirs, 32), near)
        else:
            i = int(kind[1])
            wwait(g, 7 + i, shard(g, far_e[i], mine, 32))
            if yfirst:
                wsend(g, 4, shard(g, far_e[0]), xplus)
                wsend(g, 5, shard(g, far_e[0]), xminus)
            wsend(g, 11, shard(g, far_e[i]), partner)

    def whole_weight(g):
        received(W.at[g, pl.ds(0, 512), :], wr.at[g, 11])

    def neighbour_rows():
        send(xw.at[1], xw.at[0], xs.at[0], xr.at[0], up)
        send(xw.at[1], xw.at[2], xs.at[0], xr.at[1], down)

    def normalise(j):
        v = xw[j].astype(F32)
        inv = lax.rsqrt(jnp.mean(v * v, axis=-1, keepdims=True) + EPS)
        n = v * inv * gain_ref[...]
        nrm[128 * j : 128 * (j + 1), :] = n.astype(BF16)

    def transpose_normed(j):
        nT[:, 128 * j : 128 * (j + 1)] = nrm[128 * j : 128 * (j + 1), :].astype(F32).T.astype(BF16)

    def others_loaded():
        while len(loads) > 5:
            loads.pop().wait()

    def own_rows():
        others_loaded()
        normalise(1)

    lane = lax.broadcasted_iota(jnp.int32, (1, 128), 1)

    state = {}

    def slots():
        counts = []
        live = []
        for j in range(3):
            n = jnp.int32(0)
            for s in range(NB):
                hit = (nbr_ref[0, s] == t - 1 + j) & (nbm_ref[0, s] > 0)
                n = n + jnp.where(hit, 1, 0)
            counts.append(n.astype(F32))
            row = jnp.clip(t - 1 + j, 0, PATCHES - 1)
            live.append((pm_ref[pl.ds(row, 1), :] > 0) & (n > 0))
        bias = jnp.concatenate([jnp.where(m, 0.0, -1e30) for m in live], axis=1)
        scale = jnp.concatenate([jnp.broadcast_to(n, (1, 128)) for n in counts], axis=1)
        own_mask = jnp.where(pm_ref[pl.ds(t, 1), :] > 0, 1.0, 0.0)
        lwc[...] = jnp.broadcast_to(pw_ref[...] * own_mask, (128, 128)).T
        state.update(bias=bias, scale=scale, counts=counts)

    def upper_rows():
        others_loaded()
        received(xw.at[0], xr.at[0])
        normalise(0)

    def lower_rows():
        others_loaded()
        received(xw.at[2], xr.at[1])
        normalise(2)

    def keys():
        whole_weight(KEY)
        ks[...] = mm(nrm[...], W[KEY]).astype(BF16)

    def queries():
        whole_weight(QUERY)
        qs[...] = mm(nrm[128:256, :], W[QUERY]).astype(BF16)

    def softmax():
        slots()
        bias, scale = state["bias"], state["scale"]
        for h in range(HEADS):
            cs = slice(128 * (h // 2), 128 * (h // 2 + 1))
            q2 = qs[:, cs]
            inside = (lane >= 64) if h % 2 else (lane < 64)
            qh = jnp.where(inside, q2, jnp.zeros_like(q2))
            sc = nt(qh, ks[:, cs]) * HD ** (-0.5) + bias
            ex = jnp.exp(sc - jnp.max(sc, axis=-1, keepdims=True))
            wS[h] = (ex * (1.0 / jnp.sum(ex * scale, axis=-1, keepdims=True))).astype(BF16)

    def values():
        whole_weight(VALUE)
        vs[...] = mm(nrm[...], W[VALUE]).astype(BF16)

    def mix():
        counts = state["counts"]
        for pair in range(HEADS // 2):
            cs = slice(128 * pair, 128 * (pair + 1))
            mixed = []
            for half in range(2):
                out = jnp.zeros((128, 128), F32)
                for j in range(3):
                    js = slice(128 * j, 128 * (j + 1))
                    out = out + counts[j] * mm(wS[2 * pair + half, :, js], vs[js, cs])
                mixed.append(out)
            att[:, cs] = jnp.where(lane < 64, mixed[0], mixed[1]).astype(BF16)

    def predict():
        whole_weight(OUT)
        hidden = (xw[1].astype(F32) + nt(att[...], W[OUT])).astype(BF16)
        fa[0] = mm(hidden, R[...]).astype(BF16)

    computed = {
        "xrows": neighbour_rows,
        "norm1": own_rows,
        "norm0": upper_rows,
        "norm2": lower_rows,
        "K": keys,
        "Q": queries,
        "soft": softmax,
        "V": values,
        "mix": mix,
        "hid": predict,
    }
    for kind, g in PLAN:
        if kind == "own":
            own(g)
        elif kind == "word":
            hear(g)
        elif kind in computed:
            computed[kind]()
        else:
            take(kind, g)

    send(fa.at[0], fa.at[8], fs.at[0], br.at[0], partner)
    for k in FORECAST_ORDER:
        send(fa.at[0], fa.at[k], fs.at[0], fr.at[k], ens_dev(k // 2, k % 2, 0))

    def hand_over(k):
        received(fa.at[k], fr.at[k])
        send(fa.at[k], fa.at[8 + k], fs.at[0], br.at[0], partner)

    def transpose_weights(h):
        wT[h] = wS[h].astype(F32).T.astype(BF16)

    def pair_terms(first, members):
        for i in range(4):
            rs_ = slice(32 * i, 32 * (i + 1))
            f = fa[0, rs_, :].astype(F32)
            if first:
                d = f - tgt_ref[rs_, :]
                ab = jnp.abs(d)
                gs[rs_, :] = jnp.tanh(d * 5.0)
                lt[rs_, :] = ab + 0.2 * jnp.log(1.0 + jnp.exp(-10.0 * ab))
                tot, mag, prod = jnp.zeros_like(f), jnp.zeros_like(f), jnp.ones_like(f)
            else:
                tot, mag, prod = tots[rs_, :], mags[rs_, :], prods[rs_, :]
            for k in members:
                d = f - fa[k, rs_, :].astype(F32)
                ab = jnp.abs(d)
                tot = tot + jnp.tanh(d * 5.0)
                mag = mag + ab
                prod = prod * (1.0 + jnp.exp(-10.0 * ab))
            tots[rs_, :], mags[rs_, :], prods[rs_, :] = tot, mag, prod

    for g in range(4):
        sent(W.at[g, pl.ds(0, 960), :], ws.at[g])
    sent(xw.at[pl.ds(0, 2)], xs.at[0])
    transpose_normed(0)
    transpose_normed(1)
    for i, k in enumerate(FORECAST_ORDER):
        hand_over(k)
        transpose_weights(i)
        if i == 3:
            hear(4)
    transpose_weights(7)
    transpose_normed(2)
    pair_terms(True, range(1, 8))
    hear(5)
    received(fa.at[pl.ds(0, 8)], br.at[0])
    pair_terms(False, range(8, 16))

    lw = lwc[...]
    mag = mags[...] + 0.2 * jnp.log(prods[...])
    terms = lw * (lt[...] - mag * (0.5 / (MEMBERS - 1)))
    l1[...] = jnp.sum(terms.reshape(16, 8, 128), axis=0)
    factor = 1.0 / math.sqrt(MEMBERS * PATCHES * TILE)
    gs[...] = (lw * (gs[...] - tots[...] / (MEMBERS - 1)) * factor).astype(BF16).astype(F32)
    send(l1, lp, lps.at[0], lpr.at[0], partner)
    here = x * 4 + y

    counts = state["counts"]
    gf = gs[...]
    gfb = gf.astype(BF16)
    gh = nt(gfb, R[...]).astype(BF16)
    ga = mm(gh, W[3]).astype(BF16)
    for pair in range(HEADS // 2):
        cs = slice(128 * pair, 128 * (pair + 1))
        g2 = ga[:, cs]
        a = mm(wT[2 * pair], g2)
        b = mm(wT[2 * pair + 1], g2)
        both = jnp.where(lane < 64, a, b)
        for j in range(3):
            dV[128 * j : 128 * (j + 1), cs] = (both[128 * j : 128 * (j + 1)] * counts[j]).astype(BF16)
    G[...] = mm(nT[...], dV[...]).astype(BF16).reshape(8, 2, 2, 32, 512)

    send(G.at[:, 1 - c], Gp, ps.at[0], pr.at[0], partner)
    gfT = gf.T.astype(BF16)
    st = mm(gfT, att[...])
    for r in range(8):
        for l in range(4):
            b = r * 4 + l
            S[b % 2, b // 2] = st[16 * r : 16 * (r + 1), 128 * l : 128 * (l + 1)].astype(BF16)
    send(S.at[1 - c], Sp, sps.at[0], spr.at[0], partner)
    received(lp, lpr.at[0])
    l2[...] = l1[...] + lp[...]
    for o in chip_offsets:
        send(l2, lr.at[here], lrs.at[0], lrr.at[0], chip_dev(*o))
    received(Sp, spr.at[0])
    S2[...] = (S[c].astype(F32) + Sp[...].astype(F32)).astype(BF16)
    for o in chip_offsets:
        xx, hh, ll = chip(*o)
        send(S2.at[xx * 4 + hh * 2 + ll], Sr.at[o[0] * 4 + o[1]], srs.at[0], srr.at[0], chip_dev(*o))
    received(Gp, pr.at[0])
    for b in range(8):
        H[b] = (G[b, c].astype(F32) + Gp[b].astype(F32)).astype(BF16)
    for o in chip_offsets:
        xx, hh, ll = chip(*o)
        send(H.at[xx * 2 + hh, ll], Rr.at[o[0] * 4 + o[1]], rs.at[0], rr.at[0], chip_dev(*o))
    sent(fa.at[pl.ds(0, 15)], fs.at[0])
    sent(l1, lps.at[0])
    sent(S.at[0], sps.at[0])

    hear(6)

    received(lr.at[pl.ds(0, 15)], lrr.at[0])
    lr[here] = l2[...]
    l3 = lr[0]
    for i in range(1, 16):
        l3 = l3 + lr[i]
    sm = S2[here].astype(F32)
    received(Sr.at[pl.ds(1, 15)], srr.at[0])
    for k in range(1, 16):
        sm = sm + Sr[k].astype(F32)
    m3 = jnp.concatenate([sm, l3], axis=0)
    ms[0] = m3
    for k in (1, 2, 3):
        send(ms.at[0], mz1.at[zl], l1s.at[0], l1r.at[0], zl_dev(k))
    sent(lr.at[pl.ds(0, 15)], lrs.at[0])
    received(mz1.at[pl.ds(0, 3)], l1r.at[0])
    mz1[zl] = m3
    m4 = ((mz1[0] + mz1[1]) + mz1[2]) + mz1[3]
    ms[1] = m4
    for k in (1, 2, 3):
        send(ms.at[1], mz2.at[zh], l4s.at[0], l4r.at[0], zh_dev(k))

    total = H[x * 2 + yh, yl].astype(F32)
    received(Rr.at[pl.ds(1, 15)], rr.at[0])
    for k in range(1, 16):
        total = total + Rr[k].astype(F32)
    for i in range(4):
        a, b = i // 2, i % 2
        acc[i] = total[16 * a : 16 * (a + 1), 256 * b : 256 * (b + 1)]
    z1s[...] = acc[...].astype(BF16)
    for k in (1, 2, 3):
        send(z1s.at[wrap(zl + k, 4)], z1r.at[k], z1ss.at[0], z1rs.at[0], zl_dev(k))
    sent(G.at[:, 0], ps.at[0])
    sent(Sr.at[pl.ds(1, 15)], srs.at[0])
    sent(mz1.at[pl.ds(0, 3)], l1s.at[0])
    part = acc[zl]
    received(z1r.at[pl.ds(1, 3)], z1rs.at[0])
    for k in (1, 2, 3):
        part = part + z1r[k].astype(F32)
    z2s[...] = part.astype(BF16)
    for k in (1, 2, 3):
        send(z2s, z2b.at[zh], z2ss.at[0], z2rs.at[0], zh_dev(k))
    received(mz2.at[pl.ds(0, 3)], l4r.at[0])
    mz2[zh] = m4
    m5 = ((mz2[0] + mz2[1]) + mz2[2]) + mz2[3]
    mine_b = here * 2 + c
    SF[mine_b] = m5[:16].astype(BF16)
    for dx, dy, dc in plane_offsets:
        xx, hh, ll = chip(dx, dy)
        dev = (ens_of(xx, hh, wrap(c + dc, 2)), ll * 16 + z)
        send(SF.at[mine_b], SF.at[mine_b], sfs.at[0], sfr.at[0], dev)
    norm = 1.0 / (MEMBERS * PATCHES * TILE * VARS)
    loss_ref[...] = jnp.sum(jnp.sum(m5[16:], axis=0, keepdims=True), axis=1, keepdims=True) * norm
    sent(Rr.at[pl.ds(1, 15)], rs.at[0])
    sent(mz2.at[pl.ds(0, 3)], l4s.at[0])
    sent(z1r.at[pl.ds(1, 3)], z1ss.at[0])
    received(z2b.at[pl.ds(0, 3)], z2rs.at[0])
    z2b[zh] = z2s[...]
    whole = ((z2b[0].astype(F32) + z2b[1].astype(F32)) + z2b[2].astype(F32)) + z2b[3].astype(F32)
    spot = yl * 4 + zl
    fin[spot] = whole.astype(BF16)
    for other, k in [(0, 1), (0, 2), (0, 3), (1, 0), (1, 1), (1, 2), (1, 3)]:
        send(fin.at[spot], fin.at[spot], z3s.at[0], z3r.at[0], zl_dev(k, other))
    sent(z2b.at[pl.ds(0, 3)], z2ss.at[0])
    received(SF.at[pl.ds(0, 31)], sfr.at[0])
    full = jnp.concatenate(
        [jnp.concatenate([SF[r * 4 + l] for l in range(4)], axis=1) for r in range(8)], axis=0
    )
    out_ref[:, :512] = mm(R[rows, :], full) * 0.5
    sent(SF.at[pl.ds(0, 31)], sfs.at[0])
    received(fin.at[pl.ds(0, 7)], z3r.at[0])
    for i in range(8):
        r0 = 32 * (i // 4) + 16 * (i // 2 % 2)
        c0 = 256 * (i % 2)
        out_ref[r0 : r0 + 16, 512 + c0 : 768 + c0] = fin[i].astype(F32) * 0.5
    sent(fin.at[pl.ds(0, 7)], z3s.at[0])


def per_device(
    sample_layer_feed,
    gain,
    w_query,
    w_key,
    w_value,
    w_out,
    readout_matrix,
    target,
    pixel_weight,
    pix_mask,
    neighbours,
    neighbour_mask,
):
    hbm = pl.BlockSpec(memory_space=pltpu.HBM)
    vmem = pl.BlockSpec(memory_space=pltpu.VMEM)
    dma = lambda *n: pltpu.SemaphoreType.DMA(n)
    scratch = [
        pltpu.VMEM((1, D), F32),
        pltpu.VMEM((TILE, VARS), F32),
        pltpu.VMEM((1, TILE), F32),
        pltpu.VMEM((PATCHES, TILE), jnp.int32),
        pltpu.SMEM((1, NB), jnp.int32),
        pltpu.SMEM((1, NB), jnp.int32),
        pltpu.VMEM((4, D, INNER), BF16),
        pltpu.VMEM((3, TILE, D), BF16),
        pltpu.VMEM((D, VARS), BF16),
        pltpu.VMEM((3 * TILE, D), BF16),
        pltpu.VMEM((D, 3 * TILE), BF16),
        pltpu.VMEM((TILE, INNER), BF16),
        pltpu.VMEM((3 * TILE, INNER), BF16),
        pltpu.VMEM((3 * TILE, INNER), BF16),
        pltpu.VMEM((HEADS, TILE, 3 * TILE), BF16),
        pltpu.VMEM((HEADS, 3 * TILE, TILE), BF16),
        pltpu.VMEM((TILE, INNER), BF16),
        pltpu.VMEM((3 * TILE, INNER), BF16),
        pltpu.VMEM((16, 128, 128), BF16),
        pltpu.VMEM((128, 128), F32),
        pltpu.VMEM((128, 128), F32),
        pltpu.VMEM((128, 128), F32),
        pltpu.VMEM((128, 128), F32),
        pltpu.VMEM((128, 128), F32),
        pltpu.VMEM((128, 128), F32),
        pltpu.VMEM((8, 128), F32),
        pltpu.VMEM((8, 128), F32),
        pltpu.VMEM((8, 128), F32),
        pltpu.VMEM((16, 8, 128), F32),
        pltpu.VMEM((4, 24, 128), F32),
        pltpu.VMEM((4, 24, 128), F32),
        pltpu.VMEM((2, 24, 128), F32),
        pltpu.VMEM((2, 16, 16, 128), BF16),
        pltpu.VMEM((16, 16, 128), BF16),
        pltpu.VMEM((16, 16, 128), BF16),
        pltpu.VMEM((16, 16, 128), BF16),
        pltpu.VMEM((32, 16, 128), BF16),
        pltpu.VMEM((8, 2, 2, 32, INNER), BF16),
        pltpu.VMEM((8, 2, 32, INNER), BF16),
        pltpu.VMEM((8, 2, 32, INNER), BF16),
        pltpu.VMEM((16, 32, INNER), BF16),
        pltpu.VMEM((4, 16, 256), F32),
        pltpu.VMEM((4, 16, 256), BF16),
        pltpu.VMEM((4, 16, 256), BF16),
        pltpu.VMEM((16, 256), BF16),
        pltpu.VMEM((4, 16, 256), BF16),
        pltpu.VMEM((8, 16, 256), BF16),
        dma(12), dma(1), dma(2), dma(4), dma(4, 12),
    ]
    scratch += [dma(1), dma(8)] + [dma(1)] * 25
    scratch += [pltpu.SemaphoreType.REGULAR((ROUNDS,))]
    loss, both = pl.pallas_call(
        step_kernel,
        out_shape=(
            jax.ShapeDtypeStruct((1, 1), F32),
            jax.ShapeDtypeStruct((64, 2 * INNER), F32),
        ),
        in_specs=[hbm] * 12,
        out_specs=(vmem, vmem),
        scratch_shapes=scratch,
        compiler_params=pltpu.CompilerParams(
            collective_id=0, has_side_effects=True, vmem_limit_bytes=67043328
        ),
        name="forecast_step",
    )(
        sample_layer_feed[0],
        gain.reshape(1, D),
        w_query,
        w_key,
        w_value,
        w_out.T,
        readout_matrix,
        target,
        pixel_weight.reshape(1, TILE),
        pix_mask.reshape(PATCHES, TILE),
        neighbours,
        neighbour_mask,
    )
    both = both * 2.0
    return (loss.reshape(()), both[:, :INNER].T, both[:, INNER:])


def solution(mesh):
    in_specs = (
        P("ens", "pix", None),
        P(),
        P("ens", None),
        P("ens", None),
        P("ens", None),
        P(None, "ens"),
        P(),
        P("pix", None),
        P("pix"),
        P(),
        P("pix", None),
        P("pix", None),
    )
    out_specs = (P(), P(None, "ens"), P("ens", None))
    return jax.shard_map(
        per_device, mesh=mesh, in_specs=in_specs, out_specs=out_specs, check_vma=False
    )
```

```python
import math

import jax
import jax.numpy as jnp
from jax import lax
from jax.experimental import pallas as pl
from jax.experimental.pallas import tpu as pltpu
from jax.sharding import PartitionSpec as P

HEADS = 8
HD = 64
TILE = 128
NB = 9
D = 1024
INNER = 512
VARS = 128
MEMBERS = 16
PATCHES = 32
EPS = 1e-06
MESH = pl.DeviceIdType.MESH
F32 = jnp.float32
BF16 = jnp.bfloat16

KEY, QUERY, VALUE, OUT = 0, 1, 2, 3

ROUNDS = 7

FORECAST_ORDER = (5, 3, 7, 1, 4, 2, 6)

Y_FIRST = (1, 3)

PLAN = (
    ("xrows", 0), ("own", 0), ("own", 2), ("own", 1), ("xm", 0), ("xp", 0), ("own", 3), ("xm", 2), ("word", 0),
    ("f0", 1), ("xp", 2), ("xm", 1), ("f0", 0), ("xp", 1), ("h", 0), ("f0", 3), ("f1", 0), ("n0", 1), ("norm0", 0),
    ("f2", 0), ("f1", 2), ("h", 2), ("n0", 3), ("word", 1), ("f3", 0), ("f2", 2), ("ym", 1), ("yp", 1), ("n0", 0),
    ("f0", 2), ("xp", 3), ("norm2", 0), ("n1", 2), ("f3", 2), ("n1", 0), ("h", 1), ("xm", 3), ("n2", 0), ("word", 2),
    ("norm1", 0), ("slots", 0), ("ym", 3), ("n3", 0), ("n2", 2), ("yp", 3), ("yh", 1), ("K", 0), ("n0", 2), ("Q", 0),
    ("n3", 2), ("soft", 0), ("h", 3), ("yh", 3), ("V", 0), ("mix", 0), ("word", 3), ("hid", 0),
)


def nt(a, b):
    return lax.dot_general(a, b, (((1,), (1,)), ((), ())), preferred_element_type=F32)


def mm(a, b):
    return jnp.dot(a, b, preferred_element_type=F32)


def step_kernel(
    x_hbm, gain_hbm, wq_hbm, wk_hbm, wv_hbm, wo_hbm, r_hbm, tgt_hbm, pw_hbm, pm_hbm, nbr_hbm, nbm_hbm,
    loss_ref, out_ref,
    gain_ref, tgt_ref, pw_ref, pm_ref, nbr_ref, nbm_ref,
    W, xw, R, nrm, nT, qs, ks, vs, wS, wT, att, dV,
    fa, gs, tots, mags, prods, lwc, lt, l1, l2, lp, lr, mz1, mz2, ms,
    S, Sp, S2, Sr, SF, Ga, nTp, dVp, H, Rr, acc, z1s, z1r, z2s, z2b, fin,
    loc, xs, xr, ws, wr, fs, fr, br, ps, pr, lps, lpr, rs, rr, lrs, lrr, z1ss, z1rs, z2ss, z2rs, l1s, l1r, l4s, l4r,
    z3s, z3r, sps, spr, srs, srr, sfs, sfr, pds, pdr, word,
):
    e = lax.axis_index("ens")
    t = lax.axis_index("pix")
    x = lax.div(e, 4)
    yh = lax.rem(lax.div(e, 2), 2)
    c = lax.rem(e, 2)
    yl = lax.div(t, 16)
    z = lax.rem(t, 16)
    zh = lax.div(z, 4)
    zl = lax.rem(z, 4)
    y = 2 * yh + yl

    def ens_of(xx, hh, cc):
        return xx * 4 + hh * 2 + cc

    def wrap(v, n):
        return lax.rem(v + 2 * n, n)

    def desc(src, dst, ss, rr_, dev):
        return pltpu.make_async_remote_copy(
            src_ref=src, dst_ref=dst, send_sem=ss, recv_sem=rr_, device_id=dev, device_id_type=MESH
        )

    def send(src, dst, ss, rr_, dev):
        desc(src, dst, ss, rr_, dev).start()

    def sent(ref, ss):
        desc(ref, ref, ss, ss, partner).wait_send()

    def received(ref, rr_):
        desc(ref, ref, rr_, rr_, partner).wait_recv()

    def chip(dx, dy):
        xx = wrap(x + dx, 4)
        yy = wrap(y + dy, 4)
        return xx, lax.div(yy, 2), lax.rem(yy, 2)

    def chip_dev(dx, dy):
        xx, hh, ll = chip(dx, dy)
        return (ens_of(xx, hh, c), ll * 16 + z)

    partner = (ens_of(x, yh, 1 - c), t)
    far = (ens_of(x, 1 - yh, c), (1 - yl) * 16 + z)
    near = (e, (1 - yl) * 16 + z)
    up = (e, wrap(t + 1, 32))
    down = (e, wrap(t - 1, 32))
    xplus = (ens_of(wrap(x + 1, 4), yh, c), t)
    xminus = (ens_of(wrap(x - 1, 4), yh, c), t)

    def ens_dev(dx, dh, dc):
        return (ens_of(wrap(x + dx, 4), wrap(yh + dh, 2), wrap(c + dc, 2)), t)

    def zl_dev(k, other=0):
        ll = wrap(yl + other, 2)
        return (e, ll * 16 + zh * 4 + wrap(zl + k, 4))

    def zh_dev(k):
        return (e, yl * 16 + wrap(zh + k, 4) * 4 + zl)

    links = (0, 1, 2, 1)
    chip_offsets = [(a, b) for a in range(4) for b in range(4) if (a, b) != (0, 0)]
    chip_offsets.sort(key=lambda o: -links[o[0]] - links[o[1]])

    plane_offsets = [(a, b, d) for a in range(4) for b in range(4) for d in range(2) if (a, b, d) != (0, 0, 0)]

    rows = pl.ds(pl.multiple_of(64 * e, 64), 64)
    loads = [
        pltpu.make_async_copy(x_hbm, xw.at[1], loc.at[0]),
        pltpu.make_async_copy(wk_hbm, W.at[KEY, rows, :], loc.at[1]),
        pltpu.make_async_copy(wq_hbm, W.at[QUERY, rows, :], loc.at[2]),
        pltpu.make_async_copy(wv_hbm, W.at[VALUE, rows, :], loc.at[3]),
        pltpu.make_async_copy(wo_hbm, W.at[OUT, rows, :], loc.at[4]),
        pltpu.make_async_copy(gain_hbm, gain_ref, loc.at[6]),
        pltpu.make_async_copy(r_hbm, R, loc.at[5]),
        pltpu.make_async_copy(tgt_hbm, tgt_ref, loc.at[7]),
        pltpu.make_async_copy(pw_hbm, pw_ref, loc.at[8]),
        pltpu.make_async_copy(pm_hbm, pm_ref, loc.at[9]),
        pltpu.make_async_copy(nbr_hbm, nbr_ref, loc.at[10]),
        pltpu.make_async_copy(nbm_hbm, nbm_ref, loc.at[11]),
    ]
    peers = [partner, xplus, xminus, far, near, up, down]
    barrier = pltpu.get_barrier_semaphore()
    for dev in peers:
        pl.semaphore_signal(barrier, inc=1, device_id=dev, device_id_type=MESH)
    for cp in loads:
        cp.start()
    for cp in loads[:5]:
        cp.wait()
    pl.semaphore_wait(barrier, len(peers))

    def tell(r):
        for dev in peers:
            pl.semaphore_signal(word.at[r], inc=1, device_id=dev, device_id_type=MESH)

    def hear(r):
        pl.semaphore_wait(word.at[r], len(peers))
        if r + 1 < ROUNDS:
            tell(r + 1)

    tell(0)

    def shard(g, ee, r0=0, n=64):
        return W.at[g, pl.ds(pl.multiple_of(64 * ee + r0, 32), n), :]

    def wsend(g, k, ref, dev):
        send(ref, ref, ws.at[g], wr.at[g, k], dev)

    def wwait(g, k, ref):
        received(ref, wr.at[g, k])

    mine = 32 * yl
    theirs = 32 * (1 - yl)
    cols = [x, wrap(x - 1, 4), wrap(x + 1, 4), wrap(x + 2, 4)]
    own_e = [ens_of(xx, yh, c) for xx in cols]
    far_e = [ens_of(xx, 1 - yh, c) for xx in cols]

    def own(g):
        wsend(g, 0, shard(g, own_e[0]), xplus)
        wsend(g, 1, shard(g, own_e[0]), xminus)
        wsend(g, 3, shard(g, own_e[0], mine, 32), far)
        wsend(g, 11, shard(g, own_e[0]), partner)

    def take(kind, g):
        yfirst = g in Y_FIRST
        if kind == "xm":
            wwait(g, 0, shard(g, own_e[1]))
            wsend(g, 2, shard(g, own_e[1], 0, 32), xplus)
            if not yfirst:
                wsend(g, 4, shard(g, own_e[1], mine, 32), far)
            wsend(g, 11, shard(g, own_e[1]), partner)
        elif kind == "xp":
            wwait(g, 1, shard(g, own_e[2]))
            wsend(g, 2, shard(g, own_e[2], 32, 32), xminus)
            if not yfirst:
                wsend(g, 5, shard(g, own_e[2], mine, 32), far)
            wsend(g, 11, shard(g, own_e[2]), partner)
        elif kind == "h":
            wwait(g, 2, shard(g, own_e[3]))
            if not yfirst:
                wsend(g, 6, shard(g, own_e[3], mine, 32), far)
            wsend(g, 11, shard(g, own_e[3]), partner)
        elif kind == "ym":
            wwait(g, 4, shard(g, far_e[1]))
            wsend(g, 6, shard(g, far_e[1], 0, 32), xplus)
            wsend(g, 11, shard(g, far_e[1]), partner)
        elif kind == "yp":
            wwait(g, 5, shard(g, far_e[2]))
            wsend(g, 6, shard(g, far_e[2], 32, 32), xminus)
            wsend(g, 11, shard(g, far_e[2]), partner)
        elif kind == "yh":
            wwait(g, 6, shard(g, far_e[3]))
            wsend(g, 11, shard(g, far_e[3]), partner)
        elif kind[0] == "f":
            i = int(kind[1])
            wwait(g, 3 + i, shard(g, far_e[i], theirs, 32))
            wsend(g, 7 + i, shard(g, far_e[i], theirs, 32), near)
        else:
            i = int(kind[1])
            wwait(g, 7 + i, shard(g, far_e[i], mine, 32))
            if yfirst:
                wsend(g, 4, shard(g, far_e[0]), xplus)
                wsend(g, 5, shard(g, far_e[0]), xminus)
            wsend(g, 11, shard(g, far_e[i]), partner)

    def whole_weight(g):
        received(W.at[g, pl.ds(0, 512), :], wr.at[g, 11])

    def neighbour_rows():
        send(xw.at[1], xw.at[0], xs.at[0], xr.at[0], up)
        send(xw.at[1], xw.at[2], xs.at[0], xr.at[1], down)

    def normalise(j):
        v = xw[j].astype(F32)
        inv = lax.rsqrt(jnp.mean(v * v, axis=-1, keepdims=True) + EPS)
        n = v * inv * gain_ref[...]
        nrm[128 * j : 128 * (j + 1), :] = n.astype(BF16)

    def transpose_normed(j):
        rows_t = nrm[128 * j : 128 * (j + 1), :].astype(F32).T.astype(BF16)
        nT[:, :, :, 128 * j : 128 * (j + 1)] = rows_t.reshape(8, 2, 64, 128)

    def own_rows():
        others_loaded()
        normalise(1)

    lane = lax.broadcasted_iota(jnp.int32, (1, 128), 1)

    def others_loaded():
        while len(loads) > 5:
            loads.pop().wait()

    state = {}

    def slots():
        others_loaded()
        counts = []
        live = []
        for j in range(3):
            n = jnp.int32(0)
            for s in range(NB):
                hit = (nbr_ref[0, s] == t - 1 + j) & (nbm_ref[0, s] > 0)
                n = n + jnp.where(hit, 1, 0)
            counts.append(n.astype(F32))
            row = jnp.clip(t - 1 + j, 0, PATCHES - 1)
            live.append((pm_ref[pl.ds(row, 1), :] > 0) & (n > 0))
        bias = jnp.concatenate([jnp.where(m, 0.0, -1e30) for m in live], axis=1)
        scale = jnp.concatenate([jnp.broadcast_to(n, (1, 128)) for n in counts], axis=1)
        own_mask = jnp.where(pm_ref[pl.ds(t, 1), :] > 0, 1.0, 0.0)
        lwc[...] = jnp.broadcast_to(pw_ref[...] * own_mask, (128, 128)).T
        state.update(bias=bias, scale=scale, counts=counts)

    def upper_rows():
        others_loaded()
        received(xw.at[0], xr.at[0])
        normalise(0)

    def lower_rows():
        others_loaded()
        received(xw.at[2], xr.at[1])
        normalise(2)

    def keys():
        whole_weight(KEY)
        ks[...] = mm(nrm[...], W[KEY]).astype(BF16)

    def queries():
        whole_weight(QUERY)
        qs[...] = mm(nrm[128:256, :], W[QUERY]).astype(BF16)

    def softmax():
        bias, scale = state["bias"], state["scale"]
        for h in range(HEADS):
            cs = slice(128 * (h // 2), 128 * (h // 2 + 1))
            q2 = qs[:, cs]
            inside = (lane >= 64) if h % 2 else (lane < 64)
            qh = jnp.where(inside, q2, jnp.zeros_like(q2))
            sc = nt(qh, ks[:, cs]) * HD ** (-0.5) + bias
            ex = jnp.exp(sc - jnp.max(sc, axis=-1, keepdims=True))
            wS[h] = (ex * (1.0 / jnp.sum(ex * scale, axis=-1, keepdims=True))).astype(BF16)

    def values():
        whole_weight(VALUE)
        vs[...] = mm(nrm[...], W[VALUE]).astype(BF16)

    def mix():
        counts = state["counts"]
        for pair in range(HEADS // 2):
            cs = slice(128 * pair, 128 * (pair + 1))
            mixed = []
            for half in range(2):
                out = jnp.zeros((128, 128), F32)
                for j in range(3):
                    js = slice(128 * j, 128 * (j + 1))
                    out = out + counts[j] * mm(wS[2 * pair + half, :, js], vs[js, cs])
                mixed.append(out)
            att[:, cs] = jnp.where(lane < 64, mixed[0], mixed[1]).astype(BF16)

    def predict():
        whole_weight(OUT)
        hidden = (xw[1].astype(F32) + nt(att[...], W[OUT])).astype(BF16)
        fa[0] = mm(hidden, R[...]).astype(BF16)

    computed = {
        "xrows": neighbour_rows,
        "norm1": own_rows,
        "slots": slots,
        "norm0": upper_rows,
        "norm2": lower_rows,
        "K": keys,
        "Q": queries,
        "soft": softmax,
        "V": values,
        "mix": mix,
        "hid": predict,
    }
    for kind, g in PLAN:
        if kind == "own":
            own(g)
        elif kind == "word":
            hear(g)
        elif kind in computed:
            computed[kind]()
        else:
            take(kind, g)

    send(fa.at[0], fa.at[8], fs.at[0], br.at[0], partner)
    for k in FORECAST_ORDER:
        send(fa.at[0], fa.at[k], fs.at[0], fr.at[k], ens_dev(k // 2, k % 2, 0))

    def hand_over(k):
        received(fa.at[k], fr.at[k])
        send(fa.at[k], fa.at[8 + k], fs.at[0], br.at[0], partner)

    def transpose_weights(h):
        wT[h] = wS[h].astype(F32).T.astype(BF16)

    def pair_terms(first, members):
        for i in range(4):
            rs_ = slice(32 * i, 32 * (i + 1))
            f = fa[0, rs_, :].astype(F32)
            if first:
                d = f - tgt_ref[rs_, :]
                ab = jnp.abs(d)
                gs[rs_, :] = jnp.tanh(d * 5.0)
                lt[rs_, :] = ab + 0.2 * jnp.log(1.0 + jnp.exp(-10.0 * ab))
                tot, mag, prod = jnp.zeros_like(f), jnp.zeros_like(f), jnp.ones_like(f)
            else:
                tot, mag, prod = tots[rs_, :], mags[rs_, :], prods[rs_, :]
            for k in members:
                d = f - fa[k, rs_, :].astype(F32)
                ab = jnp.abs(d)
                tot = tot + jnp.tanh(d * 5.0)
                mag = mag + ab
                prod = prod * (1.0 + jnp.exp(-10.0 * ab))
            tots[rs_, :], mags[rs_, :], prods[rs_, :] = tot, mag, prod

    for g in range(4):
        sent(W.at[g, pl.ds(0, 960), :], ws.at[g])
    sent(xw.at[pl.ds(0, 2)], xs.at[0])
    for j in range(3):
        transpose_normed(j)
    send(nT.at[:, 1 - c], nTp, ps.at[0], pr.at[0], partner)
    for i, k in enumerate(FORECAST_ORDER):
        hand_over(k)
        transpose_weights(i)
        if i == 3:
            hear(4)
    transpose_weights(7)
    pair_terms(True, range(1, 8))
    received(fa.at[pl.ds(0, 8)], br.at[0])
    pair_terms(False, range(8, 16))

    lw = lwc[...]
    mag = mags[...] + 0.2 * jnp.log(prods[...])
    terms = lw * (lt[...] - mag * (0.5 / (MEMBERS - 1)))
    l1[...] = jnp.sum(terms, axis=0, keepdims=True)
    factor = 1.0 / math.sqrt(MEMBERS * PATCHES * TILE)
    gs[...] = (lw * (gs[...] - tots[...] / (MEMBERS - 1)) * factor).astype(BF16).astype(F32)
    send(l1, lp, lps.at[0], lpr.at[0], partner)
    here = x * 4 + y

    counts = state["counts"]
    gf = gs[...]
    gfb = gf.astype(BF16)
    gh = nt(gfb, R[...]).astype(BF16)
    ga = mm(gh, W[3]).astype(BF16)
    for pair in range(HEADS // 2):
        cs = slice(128 * pair, 128 * (pair + 1))
        g2 = ga[:, cs]
        a = mm(wT[2 * pair], g2)
        b = mm(wT[2 * pair + 1], g2)
        mixed = jnp.where(lane < 64, a, b)
        for j in range(3):
            dV[128 * j : 128 * (j + 1), cs] = (mixed[128 * j : 128 * (j + 1)] * counts[j]).astype(BF16)
    send(dV, dVp, pds.at[0], pdr.at[0], partner)
    gfT = gf.T.astype(BF16)
    st = mm(gfT, att[...])
    for r in range(8):
        for l in range(4):
            b = r * 4 + l
            S[b % 2, b // 2] = st[16 * r : 16 * (r + 1), 128 * l : 128 * (l + 1)].astype(BF16)
    send(S.at[1 - c], Sp, sps.at[0], spr.at[0], partner)

    Ga[...] = mm(nT[:, c].reshape(512, 384), dV[...])
    hear(5)
    received(lp, lpr.at[0])
    l2[...] = l1[...] + lp[...]
    for o in chip_offsets:
        send(l2, lr.at[here], lrs.at[0], lrr.at[0], chip_dev(*o))
    received(Sp, spr.at[0])
    S2[...] = (S[c].astype(F32) + Sp[...].astype(F32)).astype(BF16)
    for o in chip_offsets:
        xx, hh, ll = chip(*o)
        send(S2.at[xx * 4 + hh * 2 + ll], Sr.at[o[0] * 4 + o[1]], srs.at[0], srr.at[0], chip_dev(*o))
    received(nTp, pr.at[0])
    received(dVp, pdr.at[0])
    both = Ga[...] + mm(nTp[...].reshape(512, 384), dVp[...])
    H[...] = both.astype(BF16).reshape(8, 2, 32, 512)
    for o in chip_offsets:
        xx, hh, ll = chip(*o)
        send(H.at[xx * 2 + hh, ll], Rr.at[o[0] * 4 + o[1]], rs.at[0], rr.at[0], chip_dev(*o))
    sent(fa.at[pl.ds(0, 15)], fs.at[0])
    sent(l1, lps.at[0])
    sent(S.at[0], sps.at[0])

    received(lr.at[pl.ds(0, 15)], lrr.at[0])
    lr[here] = l2[...]
    l3 = lr[0]
    for i in range(1, 16):
        l3 = l3 + lr[i]
    sm = S2[here].astype(F32)
    received(Sr.at[pl.ds(1, 15)], srr.at[0])
    for k in range(1, 16):
        sm = sm + Sr[k].astype(F32)
    m3 = jnp.concatenate([sm, l3, jnp.zeros((7, 128), F32)], axis=0)
    ms[0] = m3
    for k in (1, 2, 3):
        send(ms.at[0], mz1.at[zl], l1s.at[0], l1r.at[0], zl_dev(k))
    sent(lr.at[pl.ds(0, 15)], lrs.at[0])
    received(mz1.at[pl.ds(0, 3)], l1r.at[0])
    mz1[zl] = m3
    m4 = ((mz1[0] + mz1[1]) + mz1[2]) + mz1[3]
    ms[1] = m4
    hear(6)
    for k in (1, 2, 3):
        send(ms.at[1], mz2.at[zh], l4s.at[0], l4r.at[0], zh_dev(k))

    total = H[x * 2 + yh, yl].astype(F32)
    received(Rr.at[pl.ds(1, 15)], rr.at[0])
    for k in range(1, 16):
        total = total + Rr[k].astype(F32)
    for i in range(4):
        a, b = i // 2, i % 2
        acc[i] = total[16 * a : 16 * (a + 1), 256 * b : 256 * (b + 1)]
    z1s[...] = acc[...].astype(BF16)
    for k in (1, 2, 3):
        send(z1s.at[wrap(zl + k, 4)], z1r.at[k], z1ss.at[0], z1rs.at[0], zl_dev(k))
    sent(nTp, ps.at[0])
    sent(dVp, pds.at[0])
    sent(Sr.at[pl.ds(1, 15)], srs.at[0])
    sent(mz1.at[pl.ds(0, 3)], l1s.at[0])
    part = acc[zl]
    received(z1r.at[pl.ds(1, 3)], z1rs.at[0])
    for k in (1, 2, 3):
        part = part + z1r[k].astype(F32)
    z2s[...] = part.astype(BF16)
    for k in (1, 2, 3):
        send(z2s, z2b.at[zh], z2ss.at[0], z2rs.at[0], zh_dev(k))
    received(mz2.at[pl.ds(0, 3)], l4r.at[0])
    mz2[zh] = m4
    m5 = ((mz2[0] + mz2[1]) + mz2[2]) + mz2[3]
    mine_b = here * 2 + c
    SF[mine_b] = m5[:16].astype(BF16)
    for dx, dy, dc in plane_offsets:
        xx, hh, ll = chip(dx, dy)
        dev = (ens_of(xx, hh, wrap(c + dc, 2)), ll * 16 + z)
        send(SF.at[mine_b], SF.at[mine_b], sfs.at[0], sfr.at[0], dev)
    norm = 1.0 / (MEMBERS * PATCHES * TILE * VARS)
    loss_ref[...] = jnp.sum(jnp.sum(m5[16:], axis=0, keepdims=True), axis=1, keepdims=True) * norm
    sent(Rr.at[pl.ds(1, 15)], rs.at[0])
    sent(mz2.at[pl.ds(0, 3)], l4s.at[0])
    sent(z1r.at[pl.ds(1, 3)], z1ss.at[0])
    received(z2b.at[pl.ds(0, 3)], z2rs.at[0])
    z2b[zh] = z2s[...]
    whole = ((z2b[0].astype(F32) + z2b[1].astype(F32)) + z2b[2].astype(F32)) + z2b[3].astype(F32)
    spot = yl * 4 + zl
    fin[spot] = whole.astype(BF16)
    for other, k in [(0, 1), (0, 2), (0, 3), (1, 0), (1, 1), (1, 2), (1, 3)]:
        send(fin.at[spot], fin.at[spot], z3s.at[0], z3r.at[0], zl_dev(k, other))
    sent(z2b.at[pl.ds(0, 3)], z2ss.at[0])
    received(SF.at[pl.ds(0, 31)], sfr.at[0])
    full = jnp.concatenate(
        [jnp.concatenate([SF[r * 4 + l] for l in range(4)], axis=1) for r in range(8)], axis=0
    )
    out_ref[:, :512] = mm(R[rows, :], full) * 0.5
    sent(SF.at[pl.ds(0, 31)], sfs.at[0])
    received(fin.at[pl.ds(0, 7)], z3r.at[0])
    for i in range(8):
        r0 = 32 * (i // 4) + 16 * (i // 2 % 2)
        c0 = 256 * (i % 2)
        out_ref[r0 : r0 + 16, 512 + c0 : 768 + c0] = fin[i].astype(F32) * 0.5
    sent(fin.at[pl.ds(0, 7)], z3s.at[0])


def per_device(
    sample_layer_feed,
    gain,
    w_query,
    w_key,
    w_value,
    w_out,
    readout_matrix,
    target,
    pixel_weight,
    pix_mask,
    neighbours,
    neighbour_mask,
):
    hbm = pl.BlockSpec(memory_space=pltpu.HBM)
    vmem = pl.BlockSpec(memory_space=pltpu.VMEM)
    dma = lambda *n: pltpu.SemaphoreType.DMA(n)
    scratch = [
        pltpu.VMEM((1, D), F32),
        pltpu.VMEM((TILE, VARS), F32),
        pltpu.VMEM((1, TILE), F32),
        pltpu.VMEM((PATCHES, TILE), jnp.int32),
        pltpu.SMEM((1, NB), jnp.int32),
        pltpu.SMEM((1, NB), jnp.int32),
        pltpu.VMEM((4, D, INNER), BF16),
        pltpu.VMEM((3, TILE, D), BF16),
        pltpu.VMEM((D, VARS), BF16),
        pltpu.VMEM((3 * TILE, D), BF16),
        pltpu.VMEM((8, 2, 64, 3 * TILE), BF16),
        pltpu.VMEM((TILE, INNER), BF16),
        pltpu.VMEM((3 * TILE, INNER), BF16),
        pltpu.VMEM((3 * TILE, INNER), BF16),
        pltpu.VMEM((HEADS, TILE, 3 * TILE), BF16),
        pltpu.VMEM((HEADS, 3 * TILE, TILE), BF16),
        pltpu.VMEM((TILE, INNER), BF16),
        pltpu.VMEM((3 * TILE, INNER), BF16),
        pltpu.VMEM((16, 128, 128), BF16),
        pltpu.VMEM((128, 128), F32),
        pltpu.VMEM((128, 128), F32),
        pltpu.VMEM((128, 128), F32),
        pltpu.VMEM((128, 128), F32),
        pltpu.VMEM((128, 128), F32),
        pltpu.VMEM((128, 128), F32),
        pltpu.VMEM((1, 128), F32),
        pltpu.VMEM((1, 128), F32),
        pltpu.VMEM((1, 128), F32),
        pltpu.VMEM((16, 1, 128), F32),
        pltpu.VMEM((4, 24, 128), F32),
        pltpu.VMEM((4, 24, 128), F32),
        pltpu.VMEM((2, 24, 128), F32),
        pltpu.VMEM((2, 16, 16, 128), BF16),
        pltpu.VMEM((16, 16, 128), BF16),
        pltpu.VMEM((16, 16, 128), BF16),
        pltpu.VMEM((16, 16, 128), BF16),
        pltpu.VMEM((32, 16, 128), BF16),
        pltpu.VMEM((INNER, INNER), F32),
        pltpu.VMEM((8, 64, 3 * TILE), BF16),
        pltpu.VMEM((3 * TILE, INNER), BF16),
        pltpu.VMEM((8, 2, 32, INNER), BF16),
        pltpu.VMEM((16, 32, INNER), BF16),
        pltpu.VMEM((4, 16, 256), F32),
        pltpu.VMEM((4, 16, 256), BF16),
        pltpu.VMEM((4, 16, 256), BF16),
        pltpu.VMEM((16, 256), BF16),
        pltpu.VMEM((4, 16, 256), BF16),
        pltpu.VMEM((8, 16, 256), BF16),
        dma(12), dma(1), dma(2), dma(4), dma(4, 12),
    ]
    scratch += [dma(1), dma(8)] + [dma(1)] * 27
    scratch += [pltpu.SemaphoreType.REGULAR((ROUNDS,))]
    loss, both = pl.pallas_call(
        step_kernel,
        out_shape=(
            jax.ShapeDtypeStruct((1, 1), F32),
            jax.ShapeDtypeStruct((64, 2 * INNER), F32),
        ),
        in_specs=[hbm] * 12,
        out_specs=(vmem, vmem),
        scratch_shapes=scratch,
        compiler_params=pltpu.CompilerParams(
            collective_id=0, has_side_effects=True, vmem_limit_bytes=67043328
        ),
        name="forecast_step",
    )(
        sample_layer_feed[0],
        gain.reshape(1, D),
        w_query,
        w_key,
        w_value,
        w_out.T,
        readout_matrix,
        target,
        pixel_weight.reshape(1, TILE),
        pix_mask.reshape(PATCHES, TILE),
        neighbours,
        neighbour_mask,
    )
    both = both * 2.0
    return (loss.reshape(()), both[:, :INNER].T, both[:, INNER:])


def solution(mesh):
    in_specs = (
        P("ens", "pix", None),
        P(),
        P("ens", None),
        P("ens", None),
        P("ens", None),
        P(None, "ens"),
        P(),
        P("pix", None),
        P("pix"),
        P(),
        P("pix", None),
        P("pix", None),
    )
    out_specs = (P(), P(None, "ens"), P("ens", None))
    return jax.shard_map(
        per_device, mesh=mesh, in_specs=in_specs, out_specs=out_specs, check_vma=False
    )
```

```python
import math

import jax
import jax.numpy as jnp
from jax import lax
from jax.experimental import pallas as pl
from jax.experimental.pallas import tpu as pltpu
from jax.sharding import PartitionSpec as P

HEADS = 8
HD = 64
TILE = 128
NB = 9
D = 1024
INNER = 512
VARS = 128
MEMBERS = 16
PATCHES = 32
EPS = 1e-06
MESH = pl.DeviceIdType.MESH
F32 = jnp.float32
BF16 = jnp.bfloat16

KEY, QUERY, VALUE, OUT = 0, 1, 2, 3

ROUNDS = 7

FORECAST_ORDER = (5, 3, 7, 1, 4, 2, 6)

Y_FIRST = (1, 3)

PLAN = (
    ("xrows", 0), ("own", 0), ("own", 2), ("own", 1), ("xm", 0), ("xp", 0), ("own", 3), ("xm", 2), ("word", 0),
    ("f0", 1), ("xp", 2), ("xm", 1), ("f0", 0), ("xp", 1), ("h", 0), ("f0", 3), ("f1", 0), ("n0", 1), ("norm0", 0),
    ("f2", 0), ("f1", 2), ("h", 2), ("n0", 3), ("word", 1), ("f3", 0), ("f2", 2), ("ym", 1), ("yp", 1), ("n0", 0),
    ("f0", 2), ("xp", 3), ("norm2", 0), ("n1", 2), ("f3", 2), ("n1", 0), ("h", 1), ("xm", 3), ("n2", 0), ("norm1", 0),
    ("slots", 0), ("ym", 3), ("n3", 0), ("n2", 2), ("yp", 3), ("yh", 1), ("K", 0), ("n0", 2), ("Q", 0), ("word", 2),
    ("n3", 2), ("soft", 0), ("h", 3), ("yh", 3), ("V", 0), ("mix", 0), ("word", 3), ("hid", 0),
)


def nt(a, b):
    return lax.dot_general(a, b, (((1,), (1,)), ((), ())), preferred_element_type=F32)


def mm(a, b):
    return jnp.dot(a, b, preferred_element_type=F32)


def step_kernel(
    x_hbm, gain_hbm, wq_hbm, wk_hbm, wv_hbm, wo_hbm, r_hbm, tgt_hbm, pw_hbm, pm_hbm, nbr_hbm, nbm_hbm,
    loss_ref, out_ref,
    gain_ref, tgt_ref, pw_ref, pm_ref, nbr_ref, nbm_ref,
    W, xw, R, nrm, nT, qs, ks, vs, wS, wT, att, dV,
    fa, gs, tots, mags, prods, lwc, lt, l1, lr, mz1, mz2, ms,
    S, Sr, SF, Ga, nTp, dVp, H, Rr, acc, z1s, z1r, z2s, z2b, fin,
    loc, xs, xr, ws, wr, fs, fr, br, ps, pr, rs, rr, lrs, lrr, z1ss, z1rs, z2ss, z2rs, l1s, l1r, l4s, l4r,
    z3s, z3r, srs, srr, sfs, sfr, pds, pdr, word,
):
    e = lax.axis_index("ens")
    t = lax.axis_index("pix")
    x = lax.div(e, 4)
    yh = lax.rem(lax.div(e, 2), 2)
    c = lax.rem(e, 2)
    yl = lax.div(t, 16)
    z = lax.rem(t, 16)
    zh = lax.div(z, 4)
    zl = lax.rem(z, 4)
    y = 2 * yh + yl

    def ens_of(xx, hh, cc):
        return xx * 4 + hh * 2 + cc

    def wrap(v, n):
        return lax.rem(v + 2 * n, n)

    def desc(src, dst, ss, rr_, dev):
        return pltpu.make_async_remote_copy(
            src_ref=src, dst_ref=dst, send_sem=ss, recv_sem=rr_, device_id=dev, device_id_type=MESH
        )

    def send(src, dst, ss, rr_, dev):
        desc(src, dst, ss, rr_, dev).start()

    def sent(ref, ss):
        desc(ref, ref, ss, ss, partner).wait_send()

    def received(ref, rr_):
        desc(ref, ref, rr_, rr_, partner).wait_recv()

    def chip(dx, dy):
        xx = wrap(x + dx, 4)
        yy = wrap(y + dy, 4)
        return xx, lax.div(yy, 2), lax.rem(yy, 2)

    def chip_dev(dx, dy):
        xx, hh, ll = chip(dx, dy)
        return (ens_of(xx, hh, c), ll * 16 + z)

    partner = (ens_of(x, yh, 1 - c), t)
    far = (ens_of(x, 1 - yh, c), (1 - yl) * 16 + z)
    near = (e, (1 - yl) * 16 + z)
    up = (e, wrap(t + 1, 32))
    down = (e, wrap(t - 1, 32))
    xplus = (ens_of(wrap(x + 1, 4), yh, c), t)
    xminus = (ens_of(wrap(x - 1, 4), yh, c), t)

    def ens_dev(dx, dh, dc):
        return (ens_of(wrap(x + dx, 4), wrap(yh + dh, 2), wrap(c + dc, 2)), t)

    def zl_dev(k, other=0):
        ll = wrap(yl + other, 2)
        return (e, ll * 16 + zh * 4 + wrap(zl + k, 4))

    def zh_dev(k):
        return (e, yl * 16 + wrap(zh + k, 4) * 4 + zl)

    links = (0, 1, 2, 1)
    chip_offsets = [(a, b) for a in range(4) for b in range(4) if (a, b) != (0, 0)]
    chip_offsets.sort(key=lambda o: -links[o[0]] - links[o[1]])

    plane_offsets = [(a, b, d) for a in range(4) for b in range(4) for d in range(2) if (a, b, d) != (0, 0, 0)]
    plane_offsets.sort(key=lambda o: -links[o[0]] - links[o[1]])

    def plane_dev(o):
        xx, hh, ll = chip(o[0], o[1])
        return (ens_of(xx, hh, wrap(c + o[2], 2)), ll * 16 + z)

    rows = pl.ds(pl.multiple_of(64 * e, 64), 64)
    loads = [
        pltpu.make_async_copy(x_hbm, xw.at[1], loc.at[0]),
        pltpu.make_async_copy(wk_hbm, W.at[KEY, rows, :], loc.at[1]),
        pltpu.make_async_copy(wq_hbm, W.at[QUERY, rows, :], loc.at[2]),
        pltpu.make_async_copy(wv_hbm, W.at[VALUE, rows, :], loc.at[3]),
        pltpu.make_async_copy(wo_hbm, W.at[OUT, rows, :], loc.at[4]),
        pltpu.make_async_copy(gain_hbm, gain_ref, loc.at[6]),
        pltpu.make_async_copy(r_hbm, R, loc.at[5]),
        pltpu.make_async_copy(tgt_hbm, tgt_ref, loc.at[7]),
        pltpu.make_async_copy(pw_hbm, pw_ref, loc.at[8]),
        pltpu.make_async_copy(pm_hbm, pm_ref, loc.at[9]),
        pltpu.make_async_copy(nbr_hbm, nbr_ref, loc.at[10]),
        pltpu.make_async_copy(nbm_hbm, nbm_ref, loc.at[11]),
    ]
    peers = [partner, xplus, xminus, far, near, up, down]
    barrier = pltpu.get_barrier_semaphore()
    for dev in peers:
        pl.semaphore_signal(barrier, inc=1, device_id=dev, device_id_type=MESH)
    for cp in loads:
        cp.start()
    for cp in loads[:5]:
        cp.wait()
    pl.semaphore_wait(barrier, len(peers))

    def tell(r):
        for dev in peers:
            pl.semaphore_signal(word.at[r], inc=1, device_id=dev, device_id_type=MESH)

    def hear(r):
        pl.semaphore_wait(word.at[r], len(peers))
        if r + 1 < ROUNDS:
            tell(r + 1)

    tell(0)

    def shard(g, ee, r0=0, n=64):
        return W.at[g, pl.ds(pl.multiple_of(64 * ee + r0, 32), n), :]

    def wsend(g, k, ref, dev):
        send(ref, ref, ws.at[g], wr.at[g, k], dev)

    def wwait(g, k, ref):
        received(ref, wr.at[g, k])

    mine = 32 * yl
    theirs = 32 * (1 - yl)
    cols = [x, wrap(x - 1, 4), wrap(x + 1, 4), wrap(x + 2, 4)]
    own_e = [ens_of(xx, yh, c) for xx in cols]
    far_e = [ens_of(xx, 1 - yh, c) for xx in cols]

    def own(g):
        wsend(g, 0, shard(g, own_e[0]), xplus)
        wsend(g, 1, shard(g, own_e[0]), xminus)
        wsend(g, 3, shard(g, own_e[0], mine, 32), far)
        wsend(g, 11, shard(g, own_e[0]), partner)

    def take(kind, g):
        yfirst = g in Y_FIRST
        if kind == "xm":
            wwait(g, 0, shard(g, own_e[1]))
            wsend(g, 2, shard(g, own_e[1], 0, 32), xplus)
            if not yfirst:
                wsend(g, 4, shard(g, own_e[1], mine, 32), far)
            wsend(g, 11, shard(g, own_e[1]), partner)
        elif kind == "xp":
            wwait(g, 1, shard(g, own_e[2]))
            wsend(g, 2, shard(g, own_e[2], 32, 32), xminus)
            if not yfirst:
                wsend(g, 5, shard(g, own_e[2], mine, 32), far)
            wsend(g, 11, shard(g, own_e[2]), partner)
        elif kind == "h":
            wwait(g, 2, shard(g, own_e[3]))
            if not yfirst:
                wsend(g, 6, shard(g, own_e[3], mine, 32), far)
            wsend(g, 11, shard(g, own_e[3]), partner)
        elif kind == "ym":
            wwait(g, 4, shard(g, far_e[1]))
            wsend(g, 6, shard(g, far_e[1], 0, 32), xplus)
            wsend(g, 11, shard(g, far_e[1]), partner)
        elif kind == "yp":
            wwait(g, 5, shard(g, far_e[2]))
            wsend(g, 6, shard(g, far_e[2], 32, 32), xminus)
            wsend(g, 11, shard(g, far_e[2]), partner)
        elif kind == "yh":
            wwait(g, 6, shard(g, far_e[3]))
            wsend(g, 11, shard(g, far_e[3]), partner)
        elif kind[0] == "f":
            i = int(kind[1])
            wwait(g, 3 + i, shard(g, far_e[i], theirs, 32))
            wsend(g, 7 + i, shard(g, far_e[i], theirs, 32), near)
        else:
            i = int(kind[1])
            wwait(g, 7 + i, shard(g, far_e[i], mine, 32))
            if yfirst:
                wsend(g, 4, shard(g, far_e[0]), xplus)
                wsend(g, 5, shard(g, far_e[0]), xminus)
            wsend(g, 11, shard(g, far_e[i]), partner)

    def whole_weight(g):
        received(W.at[g, pl.ds(0, 512), :], wr.at[g, 11])

    def neighbour_rows():
        send(xw.at[1], xw.at[0], xs.at[0], xr.at[0], up)
        send(xw.at[1], xw.at[2], xs.at[0], xr.at[1], down)

    def normalise(j):
        v = xw[j].astype(F32)
        inv = lax.rsqrt(jnp.mean(v * v, axis=-1, keepdims=True) + EPS)
        n = v * inv * gain_ref[...]
        nrm[128 * j : 128 * (j + 1), :] = n.astype(BF16)

    def transpose_normed(j):
        rows_t = nrm[128 * j : 128 * (j + 1), :].astype(F32).T.astype(BF16)
        nT[:, :, :, 128 * j : 128 * (j + 1)] = rows_t.reshape(8, 2, 64, 128)

    def own_rows():
        others_loaded()
        normalise(1)

    lane = lax.broadcasted_iota(jnp.int32, (1, 128), 1)

    def others_loaded():
        while len(loads) > 5:
            loads.pop().wait()

    state = {}

    def slots():
        others_loaded()
        counts = []
        live = []
        for j in range(3):
            n = jnp.int32(0)
            for s in range(NB):
                hit = (nbr_ref[0, s] == t - 1 + j) & (nbm_ref[0, s] > 0)
                n = n + jnp.where(hit, 1, 0)
            counts.append(n.astype(F32))
            row = jnp.clip(t - 1 + j, 0, PATCHES - 1)
            live.append((pm_ref[pl.ds(row, 1), :] > 0) & (n > 0))
        bias = jnp.concatenate([jnp.where(m, 0.0, -1e30) for m in live], axis=1)
        scale = jnp.concatenate([jnp.broadcast_to(n, (1, 128)) for n in counts], axis=1)
        own_mask = jnp.where(pm_ref[pl.ds(t, 1), :] > 0, 1.0, 0.0)
        lwc[...] = jnp.broadcast_to(pw_ref[...] * own_mask, (128, 128)).T
        state.update(bias=bias, scale=scale, counts=counts)

    def upper_rows():
        others_loaded()
        received(xw.at[0], xr.at[0])
        normalise(0)

    def lower_rows():
        others_loaded()
        received(xw.at[2], xr.at[1])
        normalise(2)

    def keys():
        whole_weight(KEY)
        ks[...] = mm(nrm[...], W[KEY]).astype(BF16)

    def queries():
        whole_weight(QUERY)
        qs[...] = mm(nrm[128:256, :], W[QUERY]).astype(BF16)

    def softmax():
        bias, scale = state["bias"], state["scale"]
        for h in range(HEADS):
            cs = slice(128 * (h // 2), 128 * (h // 2 + 1))
            q2 = qs[:, cs]
            inside = (lane >= 64) if h % 2 else (lane < 64)
            qh = jnp.where(inside, q2, jnp.zeros_like(q2))
            sc = nt(qh, ks[:, cs]) * HD ** (-0.5) + bias
            ex = jnp.exp(sc - jnp.max(sc, axis=-1, keepdims=True))
            wS[h] = (ex * (1.0 / jnp.sum(ex * scale, axis=-1, keepdims=True))).astype(BF16)

    def values():
        whole_weight(VALUE)
        vs[...] = mm(nrm[...], W[VALUE]).astype(BF16)

    def mix():
        counts = state["counts"]
        for pair in range(HEADS // 2):
            cs = slice(128 * pair, 128 * (pair + 1))
            mixed = []
            for half in range(2):
                out = jnp.zeros((128, 128), F32)
                for j in range(3):
                    js = slice(128 * j, 128 * (j + 1))
                    out = out + counts[j] * mm(wS[2 * pair + half, :, js], vs[js, cs])
                mixed.append(out)
            att[:, cs] = jnp.where(lane < 64, mixed[0], mixed[1]).astype(BF16)

    def predict():
        whole_weight(OUT)
        hidden = (xw[1].astype(F32) + nt(att[...], W[OUT])).astype(BF16)
        fa[0] = mm(hidden, R[...]).astype(BF16)

    computed = {
        "xrows": neighbour_rows,
        "norm1": own_rows,
        "slots": slots,
        "norm0": upper_rows,
        "norm2": lower_rows,
        "K": keys,
        "Q": queries,
        "soft": softmax,
        "V": values,
        "mix": mix,
        "hid": predict,
    }
    for kind, g in PLAN:
        if kind == "own":
            own(g)
        elif kind == "word":
            hear(g)
        elif kind in computed:
            computed[kind]()
        else:
            take(kind, g)

    send(fa.at[0], fa.at[8], fs.at[0], br.at[0], partner)
    for k in FORECAST_ORDER:
        send(fa.at[0], fa.at[k], fs.at[0], fr.at[k], ens_dev(k // 2, k % 2, 0))

    def hand_over(k):
        received(fa.at[k], fr.at[k])
        send(fa.at[k], fa.at[8 + k], fs.at[0], br.at[0], partner)

    def transpose_weights(h):
        wT[h] = wS[h].astype(F32).T.astype(BF16)

    def pair_terms(first, members):
        for i in range(4):
            rs_ = slice(32 * i, 32 * (i + 1))
            f = fa[0, rs_, :].astype(F32)
            if first:
                d = f - tgt_ref[rs_, :]
                ab = jnp.abs(d)
                gs[rs_, :] = jnp.tanh(d * 5.0)
                lt[rs_, :] = ab + 0.2 * jnp.log(1.0 + jnp.exp(-10.0 * ab))
                tot, mag, prod = jnp.zeros_like(f), jnp.zeros_like(f), jnp.ones_like(f)
            else:
                tot, mag, prod = tots[rs_, :], mags[rs_, :], prods[rs_, :]
            for k in members:
                d = f - fa[k, rs_, :].astype(F32)
                ab = jnp.abs(d)
                tot = tot + jnp.tanh(d * 5.0)
                mag = mag + ab
                prod = prod * (1.0 + jnp.exp(-10.0 * ab))
            tots[rs_, :], mags[rs_, :], prods[rs_, :] = tot, mag, prod

    for g in range(4):
        sent(W.at[g, pl.ds(0, 960), :], ws.at[g])
    sent(xw.at[pl.ds(0, 2)], xs.at[0])
    for j in range(3):
        transpose_normed(j)
    send(nT.at[:, 1 - c], nTp, ps.at[0], pr.at[0], partner)
    for i, k in enumerate(FORECAST_ORDER):
        hand_over(k)
        transpose_weights(i)
        if i == 3:
            hear(4)
    transpose_weights(7)
    pair_terms(True, range(1, 8))
    received(fa.at[pl.ds(0, 8)], br.at[0])
    pair_terms(False, range(8, 16))

    lw = lwc[...]
    mag = mags[...] + 0.2 * jnp.log(prods[...])
    terms = lw * (lt[...] - mag * (0.5 / (MEMBERS - 1)))
    l1[...] = jnp.sum(terms, axis=0, keepdims=True)
    factor = 1.0 / math.sqrt(MEMBERS * PATCHES * TILE)
    gs[...] = (lw * (gs[...] - tots[...] / (MEMBERS - 1)) * factor).astype(BF16).astype(F32)
    here = x * 4 + y
    mine_b = here * 2 + c
    for o in plane_offsets:
        send(l1, lr.at[mine_b], lrs.at[0], lrr.at[0], plane_dev(o))

    counts = state["counts"]
    gf = gs[...]
    gfb = gf.astype(BF16)
    gh = nt(gfb, R[...]).astype(BF16)
    ga = mm(gh, W[3]).astype(BF16)
    for pair in range(HEADS // 2):
        cs = slice(128 * pair, 128 * (pair + 1))
        g2 = ga[:, cs]
        a = mm(wT[2 * pair], g2)
        b = mm(wT[2 * pair + 1], g2)
        mixed = jnp.where(lane < 64, a, b)
        for j in range(3):
            dV[128 * j : 128 * (j + 1), cs] = (mixed[128 * j : 128 * (j + 1)] * counts[j]).astype(BF16)
    send(dV, dVp, pds.at[0], pdr.at[0], partner)
    gfT = gf.T.astype(BF16)
    st = mm(gfT, att[...])
    for r in range(8):
        for l in range(4):
            b = r * 4 + l
            S[b % 2, b // 2] = st[16 * r : 16 * (r + 1), 128 * l : 128 * (l + 1)].astype(BF16)
    for o in plane_offsets:
        xx, hh, ll = chip(o[0], o[1])
        part_s = S.at[wrap(c + o[2], 2), xx * 4 + hh * 2 + ll]
        send(part_s, Sr.at[o[0] * 8 + o[1] * 2 + o[2]], srs.at[0], srr.at[0], plane_dev(o))

    Ga[...] = mm(nT[:, c].reshape(512, 384), dV[...])
    hear(5)
    received(nTp, pr.at[0])
    received(dVp, pdr.at[0])
    both = Ga[...] + mm(nTp[...].reshape(512, 384), dVp[...])
    H[...] = both.astype(BF16).reshape(8, 2, 32, 512)
    for o in chip_offsets:
        xx, hh, ll = chip(*o)
        send(H.at[xx * 2 + hh, ll], Rr.at[o[0] * 4 + o[1]], rs.at[0], rr.at[0], chip_dev(*o))
    sent(fa.at[pl.ds(0, 15)], fs.at[0])

    received(lr.at[pl.ds(0, 31)], lrr.at[0])
    lr[mine_b] = l1[...]
    l3 = lr[0]
    for i in range(1, 32):
        l3 = l3 + lr[i]
    sm = S[c, here].astype(F32)
    received(Sr.at[pl.ds(1, 31)], srr.at[0])
    for k in range(1, 32):
        sm = sm + Sr[k].astype(F32)
    m3 = jnp.concatenate([sm, l3, jnp.zeros((7, 128), F32)], axis=0)
    ms[0] = m3
    for k in (1, 2, 3):
        send(ms.at[0], mz1.at[zl], l1s.at[0], l1r.at[0], zl_dev(k))
    sent(lr.at[pl.ds(0, 31)], lrs.at[0])
    received(mz1.at[pl.ds(0, 3)], l1r.at[0])
    mz1[zl] = m3
    m4 = ((mz1[0] + mz1[1]) + mz1[2]) + mz1[3]
    ms[1] = m4
    hear(6)
    for k in (1, 2, 3):
        send(ms.at[1], mz2.at[zh], l4s.at[0], l4r.at[0], zh_dev(k))

    total = H[x * 2 + yh, yl].astype(F32)
    received(Rr.at[pl.ds(1, 15)], rr.at[0])
    for k in range(1, 16):
        total = total + Rr[k].astype(F32)
    for i in range(4):
        a, b = i // 2, i % 2
        acc[i] = total[16 * a : 16 * (a + 1), 256 * b : 256 * (b + 1)]
    z1s[...] = acc[...].astype(BF16)
    for k in (1, 2, 3):
        send(z1s.at[wrap(zl + k, 4)], z1r.at[k], z1ss.at[0], z1rs.at[0], zl_dev(k))
    sent(nTp, ps.at[0])
    sent(dVp, pds.at[0])
    sent(Sr.at[pl.ds(1, 31)], srs.at[0])
    sent(mz1.at[pl.ds(0, 3)], l1s.at[0])
    part = acc[zl]
    received(z1r.at[pl.ds(1, 3)], z1rs.at[0])
    for k in (1, 2, 3):
        part = part + z1r[k].astype(F32)
    z2s[...] = part.astype(BF16)
    for k in (1, 2, 3):
        send(z2s, z2b.at[zh], z2ss.at[0], z2rs.at[0], zh_dev(k))
    received(mz2.at[pl.ds(0, 3)], l4r.at[0])
    mz2[zh] = m4
    m5 = ((mz2[0] + mz2[1]) + mz2[2]) + mz2[3]
    SF[mine_b] = m5[:16].astype(BF16)
    for o in plane_offsets:
        send(SF.at[mine_b], SF.at[mine_b], sfs.at[0], sfr.at[0], plane_dev(o))
    norm = 1.0 / (MEMBERS * PATCHES * TILE * VARS)
    loss_ref[...] = jnp.sum(jnp.sum(m5[16:], axis=0, keepdims=True), axis=1, keepdims=True) * norm
    sent(Rr.at[pl.ds(1, 15)], rs.at[0])
    sent(mz2.at[pl.ds(0, 3)], l4s.at[0])
    sent(z1r.at[pl.ds(1, 3)], z1ss.at[0])
    received(z2b.at[pl.ds(0, 3)], z2rs.at[0])
    z2b[zh] = z2s[...]
    whole = ((z2b[0].astype(F32) + z2b[1].astype(F32)) + z2b[2].astype(F32)) + z2b[3].astype(F32)
    spot = yl * 4 + zl
    fin[spot] = whole.astype(BF16)
    for other, k in [(0, 1), (0, 2), (0, 3), (1, 0), (1, 1), (1, 2), (1, 3)]:
        send(fin.at[spot], fin.at[spot], z3s.at[0], z3r.at[0], zl_dev(k, other))
    sent(z2b.at[pl.ds(0, 3)], z2ss.at[0])
    received(SF.at[pl.ds(0, 31)], sfr.at[0])
    full = jnp.concatenate(
        [jnp.concatenate([SF[r * 4 + l] for l in range(4)], axis=1) for r in range(8)], axis=0
    )
    out_ref[:, :512] = mm(R[rows, :], full) * 0.5
    sent(SF.at[pl.ds(0, 31)], sfs.at[0])
    received(fin.at[pl.ds(0, 7)], z3r.at[0])
    for i in range(8):
        r0 = 32 * (i // 4) + 16 * (i // 2 % 2)
        c0 = 256 * (i % 2)
        out_ref[r0 : r0 + 16, 512 + c0 : 768 + c0] = fin[i].astype(F32) * 0.5
    sent(fin.at[pl.ds(0, 7)], z3s.at[0])


def per_device(
    sample_layer_feed,
    gain,
    w_query,
    w_key,
    w_value,
    w_out,
    readout_matrix,
    target,
    pixel_weight,
    pix_mask,
    neighbours,
    neighbour_mask,
):
    hbm = pl.BlockSpec(memory_space=pltpu.HBM)
    vmem = pl.BlockSpec(memory_space=pltpu.VMEM)
    dma = lambda *n: pltpu.SemaphoreType.DMA(n)
    scratch = [
        pltpu.VMEM((1, D), F32),
        pltpu.VMEM((TILE, VARS), F32),
        pltpu.VMEM((1, TILE), F32),
        pltpu.VMEM((PATCHES, TILE), jnp.int32),
        pltpu.SMEM((1, NB), jnp.int32),
        pltpu.SMEM((1, NB), jnp.int32),
        pltpu.VMEM((4, D, INNER), BF16),
        pltpu.VMEM((3, TILE, D), BF16),
        pltpu.VMEM((D, VARS), BF16),
        pltpu.VMEM((3 * TILE, D), BF16),
        pltpu.VMEM((8, 2, 64, 3 * TILE), BF16),
        pltpu.VMEM((TILE, INNER), BF16),
        pltpu.VMEM((3 * TILE, INNER), BF16),
        pltpu.VMEM((3 * TILE, INNER), BF16),
        pltpu.VMEM((HEADS, TILE, 3 * TILE), BF16),
        pltpu.VMEM((HEADS, 3 * TILE, TILE), BF16),
        pltpu.VMEM((TILE, INNER), BF16),
        pltpu.VMEM((3 * TILE, INNER), BF16),
        pltpu.VMEM((16, 128, 128), BF16),
        pltpu.VMEM((128, 128), F32),
        pltpu.VMEM((128, 128), F32),
        pltpu.VMEM((128, 128), F32),
        pltpu.VMEM((128, 128), F32),
        pltpu.VMEM((128, 128), F32),
        pltpu.VMEM((128, 128), F32),
        pltpu.VMEM((1, 128), F32),
        pltpu.VMEM((32, 1, 128), F32),
        pltpu.VMEM((4, 24, 128), F32),
        pltpu.VMEM((4, 24, 128), F32),
        pltpu.VMEM((2, 24, 128), F32),
        pltpu.VMEM((2, 16, 16, 128), BF16),
        pltpu.VMEM((32, 16, 128), BF16),
        pltpu.VMEM((32, 16, 128), BF16),
        pltpu.VMEM((INNER, INNER), F32),
        pltpu.VMEM((8, 64, 3 * TILE), BF16),
        pltpu.VMEM((3 * TILE, INNER), BF16),
        pltpu.VMEM((8, 2, 32, INNER), BF16),
        pltpu.VMEM((16, 32, INNER), BF16),
        pltpu.VMEM((4, 16, 256), F32),
        pltpu.VMEM((4, 16, 256), BF16),
        pltpu.VMEM((4, 16, 256), BF16),
        pltpu.VMEM((16, 256), BF16),
        pltpu.VMEM((4, 16, 256), BF16),
        pltpu.VMEM((8, 16, 256), BF16),
        dma(12), dma(1), dma(2), dma(4), dma(4, 12),
    ]
    scratch += [dma(1), dma(8)] + [dma(1)] * 23
    scratch += [pltpu.SemaphoreType.REGULAR((ROUNDS,))]
    loss, both = pl.pallas_call(
        step_kernel,
        out_shape=(
            jax.ShapeDtypeStruct((1, 1), F32),
            jax.ShapeDtypeStruct((64, 2 * INNER), F32),
        ),
        in_specs=[hbm] * 12,
        out_specs=(vmem, vmem),
        scratch_shapes=scratch,
        compiler_params=pltpu.CompilerParams(
            collective_id=0, has_side_effects=True, vmem_limit_bytes=67043328
        ),
        name="forecast_step",
    )(
        sample_layer_feed[0],
        gain.reshape(1, D),
        w_query,
        w_key,
        w_value,
        w_out.T,
        readout_matrix,
        target,
        pixel_weight.reshape(1, TILE),
        pix_mask.reshape(PATCHES, TILE),
        neighbours,
        neighbour_mask,
    )
    both = both * 2.0
    return (loss.reshape(()), both[:, :INNER].T, both[:, INNER:])


def solution(mesh):
    in_specs = (
        P("ens", "pix", None),
        P(),
        P("ens", None),
        P("ens", None),
        P("ens", None),
        P(None, "ens"),
        P(),
        P("pix", None),
        P("pix"),
        P(),
        P("pix", None),
        P("pix", None),
    )
    out_specs = (P(), P(None, "ens"), P("ens", None))
    return jax.shard_map(
        per_device, mesh=mesh, in_specs=in_specs, out_specs=out_specs, check_vma=False
    )
```

```python
import math

import jax
import jax.numpy as jnp
from jax import lax
from jax.experimental import pallas as pl
from jax.experimental.pallas import tpu as pltpu
from jax.sharding import PartitionSpec as P

HEADS = 8
HD = 64
TILE = 128
NB = 9
D = 1024
INNER = 512
VARS = 128
MEMBERS = 16
PATCHES = 32
EPS = 1e-06
MESH = pl.DeviceIdType.MESH
F32 = jnp.float32
BF16 = jnp.bfloat16

KEY, QUERY, VALUE, OUT = 0, 1, 2, 3

ROUNDS = 7

FORECAST_ORDER = (5, 3, 7, 1, 4, 2, 6)

Y_FIRST = (0, 3,)

PLAN = (
    ("xrows", 0), ("own", 1), ("own", 2), ("own", 0), ("own", 3), ("xm", 1), ("f0", 0), ("xp", 1), ("xp", 2),
    ("word", 0), ("xm", 2), ("f1", 1), ("xm", 0), ("f0", 3), ("norm1", 0), ("slots", 0), ("xp", 0), ("f0", 1),
    ("n0", 0), ("f2", 1), ("h", 1), ("f2", 2), ("h", 2), ("f0", 2), ("norm2", 0), ("word", 1), ("n1", 1), ("n0", 3),
    ("f3", 1), ("n2", 1), ("norm0", 0), ("yp", 0), ("ym", 0), ("xm", 3), ("f1", 2), ("f3", 2), ("n0", 1), ("xp", 3),
    ("h", 0), ("ym", 3), ("yp", 3), ("n3", 1), ("yh", 0), ("n1", 2), ("n2", 2), ("n0", 2), ("Q", 0), ("n3", 2),
    ("h", 3), ("K", 0), ("yh", 3), ("word", 2), ("soft", 0), ("V", 0), ("mix", 0), ("word", 3), ("hid", 0),
)


def nt(a, b):
    return lax.dot_general(a, b, (((1,), (1,)), ((), ())), preferred_element_type=F32)


def mm(a, b):
    return jnp.dot(a, b, preferred_element_type=F32)


def step_kernel(
    x_hbm, gain_hbm, wq_hbm, wk_hbm, wv_hbm, wo_hbm, r_hbm, tgt_hbm, pw_hbm, pm_hbm, nbr_hbm, nbm_hbm,
    loss_ref, out_ref,
    gain_ref, tgt_ref, pw_ref, pm_ref, nbr_ref, nbm_ref,
    W, xw, R, nrm, nT, qs, ks, vs, wS, wT, att, dV,
    fa, gs, tots, mags, prods, lwc, lt, l1, lr, mz1, mz2, ms,
    S, Sr, SF, Ga, nTp, dVp, H, Rr, acc, z1s, z1r, z2s, z2b, fin,
    loc, xs, xr, ws, wr, fs, fr, br, ps, pr, rs, rr, lrs, lrr, z1ss, z1rs, z2ss, z2rs, l1s, l1r, l4s, l4r,
    z3s, z3r, srs, srr, sfs, sfr, pds, pdr, word,
):
    e = lax.axis_index("ens")
    t = lax.axis_index("pix")
    x = lax.div(e, 4)
    yh = lax.rem(lax.div(e, 2), 2)
    c = lax.rem(e, 2)
    yl = lax.div(t, 16)
    z = lax.rem(t, 16)
    zh = lax.div(z, 4)
    zl = lax.rem(z, 4)
    y = 2 * yh + yl

    def ens_of(xx, hh, cc):
        return xx * 4 + hh * 2 + cc

    def wrap(v, n):
        return lax.rem(v + 2 * n, n)

    def desc(src, dst, ss, rr_, dev):
        return pltpu.make_async_remote_copy(
            src_ref=src, dst_ref=dst, send_sem=ss, recv_sem=rr_, device_id=dev, device_id_type=MESH
        )

    def send(src, dst, ss, rr_, dev):
        desc(src, dst, ss, rr_, dev).start()

    def sent(ref, ss):
        desc(ref, ref, ss, ss, partner).wait_send()

    def received(ref, rr_):
        desc(ref, ref, rr_, rr_, partner).wait_recv()

    def chip(dx, dy):
        xx = wrap(x + dx, 4)
        yy = wrap(y + dy, 4)
        return xx, lax.div(yy, 2), lax.rem(yy, 2)

    def chip_dev(dx, dy):
        xx, hh, ll = chip(dx, dy)
        return (ens_of(xx, hh, c), ll * 16 + z)

    partner = (ens_of(x, yh, 1 - c), t)
    far = (ens_of(x, 1 - yh, c), (1 - yl) * 16 + z)
    near = (e, (1 - yl) * 16 + z)
    up = (e, wrap(t + 1, 32))
    down = (e, wrap(t - 1, 32))
    xplus = (ens_of(wrap(x + 1, 4), yh, c), t)
    xminus = (ens_of(wrap(x - 1, 4), yh, c), t)

    def ens_dev(dx, dh, dc):
        return (ens_of(wrap(x + dx, 4), wrap(yh + dh, 2), wrap(c + dc, 2)), t)

    def zl_dev(k, other=0):
        ll = wrap(yl + other, 2)
        return (e, ll * 16 + zh * 4 + wrap(zl + k, 4))

    def zh_dev(k):
        return (e, yl * 16 + wrap(zh + k, 4) * 4 + zl)

    links = (0, 1, 2, 1)
    chip_offsets = [(a, b) for a in range(4) for b in range(4) if (a, b) != (0, 0)]
    chip_offsets.sort(key=lambda o: -links[o[0]] - links[o[1]])

    plane_offsets = [(a, b, d) for a in range(4) for b in range(4) for d in range(2) if (a, b, d) != (0, 0, 0)]
    plane_offsets.sort(key=lambda o: -links[o[0]] - links[o[1]])

    def plane_dev(o):
        xx, hh, ll = chip(o[0], o[1])
        return (ens_of(xx, hh, wrap(c + o[2], 2)), ll * 16 + z)

    rows = pl.ds(pl.multiple_of(64 * e, 64), 64)
    loads = [
        pltpu.make_async_copy(x_hbm, xw.at[1], loc.at[0]),
        pltpu.make_async_copy(wk_hbm, W.at[KEY, rows, :], loc.at[1]),
        pltpu.make_async_copy(wq_hbm, W.at[QUERY, rows, :], loc.at[2]),
        pltpu.make_async_copy(wv_hbm, W.at[VALUE, rows, :], loc.at[3]),
        pltpu.make_async_copy(wo_hbm, W.at[OUT, rows, :], loc.at[4]),
        pltpu.make_async_copy(gain_hbm, gain_ref, loc.at[6]),
        pltpu.make_async_copy(r_hbm, R, loc.at[5]),
        pltpu.make_async_copy(tgt_hbm, tgt_ref, loc.at[7]),
        pltpu.make_async_copy(pw_hbm, pw_ref, loc.at[8]),
        pltpu.make_async_copy(pm_hbm, pm_ref, loc.at[9]),
        pltpu.make_async_copy(nbr_hbm, nbr_ref, loc.at[10]),
        pltpu.make_async_copy(nbm_hbm, nbm_ref, loc.at[11]),
    ]
    peers = [partner, xplus, xminus, far, near, up, down]
    barrier = pltpu.get_barrier_semaphore()
    for dev in peers:
        pl.semaphore_signal(barrier, inc=1, device_id=dev, device_id_type=MESH)
    for cp in loads:
        cp.start()
    for cp in loads[:5]:
        cp.wait()
    pl.semaphore_wait(barrier, len(peers))

    def tell(r):
        for dev in peers:
            pl.semaphore_signal(word.at[r], inc=1, device_id=dev, device_id_type=MESH)

    def hear(r):
        pl.semaphore_wait(word.at[r], len(peers))
        if r + 1 < ROUNDS:
            tell(r + 1)

    tell(0)

    def shard(g, ee, r0=0, n=64):
        return W.at[g, pl.ds(pl.multiple_of(64 * ee + r0, 32), n), :]

    def wsend(g, k, ref, dev):
        send(ref, ref, ws.at[g], wr.at[g, k], dev)

    def wwait(g, k, ref):
        received(ref, wr.at[g, k])

    mine = 32 * yl
    theirs = 32 * (1 - yl)
    cols = [x, wrap(x - 1, 4), wrap(x + 1, 4), wrap(x + 2, 4)]
    own_e = [ens_of(xx, yh, c) for xx in cols]
    far_e = [ens_of(xx, 1 - yh, c) for xx in cols]

    def own(g):
        wsend(g, 0, shard(g, own_e[0]), xplus)
        wsend(g, 1, shard(g, own_e[0]), xminus)
        wsend(g, 3, shard(g, own_e[0], mine, 32), far)
        wsend(g, 11, shard(g, own_e[0]), partner)

    def take(kind, g):
        yfirst = g in Y_FIRST
        if kind == "xm":
            wwait(g, 0, shard(g, own_e[1]))
            wsend(g, 2, shard(g, own_e[1], 0, 32), xplus)
            if not yfirst:
                wsend(g, 4, shard(g, own_e[1], mine, 32), far)
            wsend(g, 11, shard(g, own_e[1]), partner)
        elif kind == "xp":
            wwait(g, 1, shard(g, own_e[2]))
            wsend(g, 2, shard(g, own_e[2], 32, 32), xminus)
            if not yfirst:
                wsend(g, 5, shard(g, own_e[2], mine, 32), far)
            wsend(g, 11, shard(g, own_e[2]), partner)
        elif kind == "h":
            wwait(g, 2, shard(g, own_e[3]))
            if not yfirst:
                wsend(g, 6, shard(g, own_e[3], mine, 32), far)
            wsend(g, 11, shard(g, own_e[3]), partner)
        elif kind == "ym":
            wwait(g, 4, shard(g, far_e[1]))
            wsend(g, 6, shard(g, far_e[1], 0, 32), xplus)
            wsend(g, 11, shard(g, far_e[1]), partner)
        elif kind == "yp":
            wwait(g, 5, shard(g, far_e[2]))
            wsend(g, 6, shard(g, far_e[2], 32, 32), xminus)
            wsend(g, 11, shard(g, far_e[2]), partner)
        elif kind == "yh":
            wwait(g, 6, shard(g, far_e[3]))
            wsend(g, 11, shard(g, far_e[3]), partner)
        elif kind[0] == "f":
            i = int(kind[1])
            wwait(g, 3 + i, shard(g, far_e[i], theirs, 32))
            wsend(g, 7 + i, shard(g, far_e[i], theirs, 32), near)
        else:
            i = int(kind[1])
            wwait(g, 7 + i, shard(g, far_e[i], mine, 32))
            if yfirst:
                wsend(g, 4, shard(g, far_e[0]), xplus)
                wsend(g, 5, shard(g, far_e[0]), xminus)
            wsend(g, 11, shard(g, far_e[i]), partner)

    def whole_weight(g):
        received(W.at[g, pl.ds(0, 512), :], wr.at[g, 11])

    def neighbour_rows():
        send(xw.at[1], xw.at[0], xs.at[0], xr.at[0], up)
        send(xw.at[1], xw.at[2], xs.at[0], xr.at[1], down)

    def normalise(j):
        v = xw[j].astype(F32)
        inv = lax.rsqrt(jnp.mean(v * v, axis=-1, keepdims=True) + EPS)
        n = v * inv * gain_ref[...]
        nrm[128 * j : 128 * (j + 1), :] = n.astype(BF16)

    def transpose_normed(j):
        rows_t = nrm[128 * j : 128 * (j + 1), :].astype(F32).T.astype(BF16)
        nT[:, :, :, 128 * j : 128 * (j + 1)] = rows_t.reshape(8, 2, 64, 128)

    def own_rows():
        others_loaded()
        normalise(1)

    lane = lax.broadcasted_iota(jnp.int32, (1, 128), 1)

    def others_loaded():
        while len(loads) > 5:
            loads.pop().wait()

    state = {}

    def slots():
        others_loaded()
        counts = []
        live = []
        for j in range(3):
            n = jnp.int32(0)
            for s in range(NB):
                hit = (nbr_ref[0, s] == t - 1 + j) & (nbm_ref[0, s] > 0)
                n = n + jnp.where(hit, 1, 0)
            counts.append(n.astype(F32))
            row = jnp.clip(t - 1 + j, 0, PATCHES - 1)
            live.append((pm_ref[pl.ds(row, 1), :] > 0) & (n > 0))
        bias = jnp.concatenate([jnp.where(m, 0.0, -1e30) for m in live], axis=1)
        scale = jnp.concatenate([jnp.broadcast_to(n, (1, 128)) for n in counts], axis=1)
        own_mask = jnp.where(pm_ref[pl.ds(t, 1), :] > 0, 1.0, 0.0)
        lwc[...] = jnp.broadcast_to(pw_ref[...] * own_mask, (128, 128)).T
        state.update(bias=bias, scale=scale, counts=counts)

    def upper_rows():
        others_loaded()
        received(xw.at[0], xr.at[0])
        normalise(0)

    def lower_rows():
        others_loaded()
        received(xw.at[2], xr.at[1])
        normalise(2)

    def keys():
        whole_weight(KEY)
        ks[...] = mm(nrm[...], W[KEY]).astype(BF16)

    def queries():
        whole_weight(QUERY)
        qs[...] = mm(nrm[128:256, :], W[QUERY]).astype(BF16)

    def softmax():
        bias, scale = state["bias"], state["scale"]
        for h in range(HEADS):
            cs = slice(128 * (h // 2), 128 * (h // 2 + 1))
            q2 = qs[:, cs]
            inside = (lane >= 64) if h % 2 else (lane < 64)
            qh = jnp.where(inside, q2, jnp.zeros_like(q2))
            sc = nt(qh, ks[:, cs]) * HD ** (-0.5) + bias
            ex = jnp.exp(sc - jnp.max(sc, axis=-1, keepdims=True))
            wS[h] = (ex * (1.0 / jnp.sum(ex * scale, axis=-1, keepdims=True))).astype(BF16)

    def values():
        whole_weight(VALUE)
        vs[...] = mm(nrm[...], W[VALUE]).astype(BF16)

    def mix():
        counts = state["counts"]
        for pair in range(HEADS // 2):
            cs = slice(128 * pair, 128 * (pair + 1))
            mixed = []
            for half in range(2):
                out = jnp.zeros((128, 128), F32)
                for j in range(3):
                    js = slice(128 * j, 128 * (j + 1))
                    out = out + counts[j] * mm(wS[2 * pair + half, :, js], vs[js, cs])
                mixed.append(out)
            att[:, cs] = jnp.where(lane < 64, mixed[0], mixed[1]).astype(BF16)

    def predict():
        whole_weight(OUT)
        hidden = (xw[1].astype(F32) + nt(att[...], W[OUT])).astype(BF16)
        fa[0] = mm(hidden, R[...]).astype(BF16)

    computed = {
        "xrows": neighbour_rows,
        "norm1": own_rows,
        "slots": slots,
        "norm0": upper_rows,
        "norm2": lower_rows,
        "K": keys,
        "Q": queries,
        "soft": softmax,
        "V": values,
        "mix": mix,
        "hid": predict,
    }
    for kind, g in PLAN:
        if kind == "own":
            own(g)
        elif kind == "word":
            hear(g)
        elif kind in computed:
            computed[kind]()
        else:
            take(kind, g)

    send(fa.at[0], fa.at[8], fs.at[0], br.at[0], partner)
    for k in FORECAST_ORDER:
        send(fa.at[0], fa.at[k], fs.at[0], fr.at[k], ens_dev(k // 2, k % 2, 0))

    def hand_over(k):
        received(fa.at[k], fr.at[k])
        send(fa.at[k], fa.at[8 + k], fs.at[0], br.at[0], partner)

    def transpose_weights(h):
        wT[h] = wS[h].astype(F32).T.astype(BF16)

    def pair_terms(first, members):
        for i in range(4):
            rs_ = slice(32 * i, 32 * (i + 1))
            f = fa[0, rs_, :].astype(F32)
            if first:
                d = f - tgt_ref[rs_, :]
                ab = jnp.abs(d)
                gs[rs_, :] = jnp.tanh(d * 5.0)
                lt[rs_, :] = ab + 0.2 * jnp.log(1.0 + jnp.exp(-10.0 * ab))
                tot, mag, prod = jnp.zeros_like(f), jnp.zeros_like(f), jnp.ones_like(f)
            else:
                tot, mag, prod = tots[rs_, :], mags[rs_, :], prods[rs_, :]
            for k in members:
                d = f - fa[k, rs_, :].astype(F32)
                ab = jnp.abs(d)
                tot = tot + jnp.tanh(d * 5.0)
                mag = mag + ab
                prod = prod * (1.0 + jnp.exp(-10.0 * ab))
            tots[rs_, :], mags[rs_, :], prods[rs_, :] = tot, mag, prod

    for g in range(4):
        sent(W.at[g, pl.ds(0, 960), :], ws.at[g])
    sent(xw.at[pl.ds(0, 2)], xs.at[0])
    for j in range(3):
        transpose_normed(j)
    send(nT.at[:, 1 - c], nTp, ps.at[0], pr.at[0], partner)
    for i, k in enumerate(FORECAST_ORDER):
        hand_over(k)
        transpose_weights(i)
        if i == 3:
            hear(4)
    transpose_weights(7)
    pair_terms(True, range(1, 8))
    received(fa.at[pl.ds(0, 8)], br.at[0])
    pair_terms(False, range(8, 16))

    lw = lwc[...]
    mag = mags[...] + 0.2 * jnp.log(prods[...])
    terms = lw * (lt[...] - mag * (0.5 / (MEMBERS - 1)))
    l1[...] = jnp.sum(terms, axis=0, keepdims=True)
    factor = 1.0 / math.sqrt(MEMBERS * PATCHES * TILE)
    gs[...] = (lw * (gs[...] - tots[...] / (MEMBERS - 1)) * factor).astype(BF16).astype(F32)
    here = x * 4 + y
    mine_b = here * 2 + c
    for o in plane_offsets:
        send(l1, lr.at[mine_b], lrs.at[0], lrr.at[0], plane_dev(o))

    counts = state["counts"]
    gf = gs[...]
    gfb = gf.astype(BF16)
    gh = nt(gfb, R[...]).astype(BF16)
    ga = mm(gh, W[3]).astype(BF16)
    for pair in range(HEADS // 2):
        cs = slice(128 * pair, 128 * (pair + 1))
        g2 = ga[:, cs]
        a = mm(wT[2 * pair], g2)
        b = mm(wT[2 * pair + 1], g2)
        mixed = jnp.where(lane < 64, a, b)
        for j in range(3):
            dV[128 * j : 128 * (j + 1), cs] = (mixed[128 * j : 128 * (j + 1)] * counts[j]).astype(BF16)
    send(dV, dVp, pds.at[0], pdr.at[0], partner)
    gfT = gf.T.astype(BF16)
    st = mm(gfT, att[...])
    for r in range(8):
        for l in range(4):
            b = r * 4 + l
            S[b % 2, b // 2] = st[16 * r : 16 * (r + 1), 128 * l : 128 * (l + 1)].astype(BF16)
    for o in plane_offsets:
        xx, hh, ll = chip(o[0], o[1])
        part_s = S.at[wrap(c + o[2], 2), xx * 4 + hh * 2 + ll]
        send(part_s, Sr.at[o[0] * 8 + o[1] * 2 + o[2]], srs.at[0], srr.at[0], plane_dev(o))

    Ga[...] = mm(nT[:, c].reshape(512, 384), dV[...])
    hear(5)
    received(nTp, pr.at[0])
    received(dVp, pdr.at[0])
    both = Ga[...] + mm(nTp[...].reshape(512, 384), dVp[...])
    H[...] = both.astype(BF16).reshape(8, 2, 32, 512)
    for o in chip_offsets:
        xx, hh, ll = chip(*o)
        send(H.at[xx * 2 + hh, ll], Rr.at[o[0] * 4 + o[1]], rs.at[0], rr.at[0], chip_dev(*o))
    sent(fa.at[pl.ds(0, 15)], fs.at[0])

    received(lr.at[pl.ds(0, 31)], lrr.at[0])
    lr[mine_b] = l1[...]
    l3 = lr[0]
    for i in range(1, 32):
        l3 = l3 + lr[i]
    sm = S[c, here].astype(F32)
    received(Sr.at[pl.ds(1, 31)], srr.at[0])
    for k in range(1, 32):
        sm = sm + Sr[k].astype(F32)
    m3 = jnp.concatenate([sm, l3, jnp.zeros((7, 128), F32)], axis=0)
    ms[0] = m3
    for k in (1, 2, 3):
        send(ms.at[0], mz1.at[zl], l1s.at[0], l1r.at[0], zl_dev(k))
    sent(lr.at[pl.ds(0, 31)], lrs.at[0])
    received(mz1.at[pl.ds(0, 3)], l1r.at[0])
    mz1[zl] = m3
    m4 = ((mz1[0] + mz1[1]) + mz1[2]) + mz1[3]
    ms[1] = m4
    hear(6)
    for k in (1, 2, 3):
        send(ms.at[1], mz2.at[zh], l4s.at[0], l4r.at[0], zh_dev(k))

    total = H[x * 2 + yh, yl].astype(F32)
    received(Rr.at[pl.ds(1, 15)], rr.at[0])
    for k in range(1, 16):
        total = total + Rr[k].astype(F32)
    for i in range(4):
        a, b = i // 2, i % 2
        acc[i] = total[16 * a : 16 * (a + 1), 256 * b : 256 * (b + 1)]
    z1s[...] = acc[...].astype(BF16)
    for k in (1, 2, 3):
        send(z1s.at[wrap(zl + k, 4)], z1r.at[k], z1ss.at[0], z1rs.at[0], zl_dev(k))
    sent(nTp, ps.at[0])
    sent(dVp, pds.at[0])
    sent(Sr.at[pl.ds(1, 31)], srs.at[0])
    sent(mz1.at[pl.ds(0, 3)], l1s.at[0])
    part = acc[zl]
    received(z1r.at[pl.ds(1, 3)], z1rs.at[0])
    for k in (1, 2, 3):
        part = part + z1r[k].astype(F32)
    z2s[...] = part.astype(BF16)
    for k in (1, 2, 3):
        send(z2s, z2b.at[zh], z2ss.at[0], z2rs.at[0], zh_dev(k))
    received(mz2.at[pl.ds(0, 3)], l4r.at[0])
    mz2[zh] = m4
    m5 = ((mz2[0] + mz2[1]) + mz2[2]) + mz2[3]
    SF[mine_b] = m5[:16].astype(BF16)
    for o in plane_offsets:
        send(SF.at[mine_b], SF.at[mine_b], sfs.at[0], sfr.at[0], plane_dev(o))
    norm = 1.0 / (MEMBERS * PATCHES * TILE * VARS)
    loss_ref[...] = jnp.sum(jnp.sum(m5[16:], axis=0, keepdims=True), axis=1, keepdims=True) * norm
    sent(Rr.at[pl.ds(1, 15)], rs.at[0])
    sent(mz2.at[pl.ds(0, 3)], l4s.at[0])
    sent(z1r.at[pl.ds(1, 3)], z1ss.at[0])
    received(z2b.at[pl.ds(0, 3)], z2rs.at[0])
    z2b[zh] = z2s[...]
    whole = ((z2b[0].astype(F32) + z2b[1].astype(F32)) + z2b[2].astype(F32)) + z2b[3].astype(F32)
    spot = yl * 4 + zl
    fin[spot] = whole.astype(BF16)
    for other, k in [(0, 1), (0, 2), (0, 3), (1, 0), (1, 1), (1, 2), (1, 3)]:
        send(fin.at[spot], fin.at[spot], z3s.at[0], z3r.at[0], zl_dev(k, other))
    sent(z2b.at[pl.ds(0, 3)], z2ss.at[0])
    received(SF.at[pl.ds(0, 31)], sfr.at[0])
    full = jnp.concatenate(
        [jnp.concatenate([SF[r * 4 + l] for l in range(4)], axis=1) for r in range(8)], axis=0
    )
    out_ref[:, :512] = mm(R[rows, :], full) * 0.5
    sent(SF.at[pl.ds(0, 31)], sfs.at[0])
    received(fin.at[pl.ds(0, 7)], z3r.at[0])
    for i in range(8):
        r0 = 32 * (i // 4) + 16 * (i // 2 % 2)
        c0 = 256 * (i % 2)
        out_ref[r0 : r0 + 16, 512 + c0 : 768 + c0] = fin[i].astype(F32) * 0.5
    sent(fin.at[pl.ds(0, 7)], z3s.at[0])


def per_device(
    sample_layer_feed,
    gain,
    w_query,
    w_key,
    w_value,
    w_out,
    readout_matrix,
    target,
    pixel_weight,
    pix_mask,
    neighbours,
    neighbour_mask,
):
    hbm = pl.BlockSpec(memory_space=pltpu.HBM)
    vmem = pl.BlockSpec(memory_space=pltpu.VMEM)
    dma = lambda *n: pltpu.SemaphoreType.DMA(n)
    scratch = [
        pltpu.VMEM((1, D), F32),
        pltpu.VMEM((TILE, VARS), F32),
        pltpu.VMEM((1, TILE), F32),
        pltpu.VMEM((PATCHES, TILE), jnp.int32),
        pltpu.SMEM((1, NB), jnp.int32),
        pltpu.SMEM((1, NB), jnp.int32),
        pltpu.VMEM((4, D, INNER), BF16),
        pltpu.VMEM((3, TILE, D), BF16),
        pltpu.VMEM((D, VARS), BF16),
        pltpu.VMEM((3 * TILE, D), BF16),
        pltpu.VMEM((8, 2, 64, 3 * TILE), BF16),
        pltpu.VMEM((TILE, INNER), BF16),
        pltpu.VMEM((3 * TILE, INNER), BF16),
        pltpu.VMEM((3 * TILE, INNER), BF16),
        pltpu.VMEM((HEADS, TILE, 3 * TILE), BF16),
        pltpu.VMEM((HEADS, 3 * TILE, TILE), BF16),
        pltpu.VMEM((TILE, INNER), BF16),
        pltpu.VMEM((3 * TILE, INNER), BF16),
        pltpu.VMEM((16, 128, 128), BF16),
        pltpu.VMEM((128, 128), F32),
        pltpu.VMEM((128, 128), F32),
        pltpu.VMEM((128, 128), F32),
        pltpu.VMEM((128, 128), F32),
        pltpu.VMEM((128, 128), F32),
        pltpu.VMEM((128, 128), F32),
        pltpu.VMEM((1, 128), F32),
        pltpu.VMEM((32, 1, 128), F32),
        pltpu.VMEM((4, 24, 128), F32),
        pltpu.VMEM((4, 24, 128), F32),
        pltpu.VMEM((2, 24, 128), F32),
        pltpu.VMEM((2, 16, 16, 128), BF16),
        pltpu.VMEM((32, 16, 128), BF16),
        pltpu.VMEM((32, 16, 128), BF16),
        pltpu.VMEM((INNER, INNER), F32),
        pltpu.VMEM((8, 64, 3 * TILE), BF16),
        pltpu.VMEM((3 * TILE, INNER), BF16),
        pltpu.VMEM((8, 2, 32, INNER), BF16),
        pltpu.VMEM((16, 32, INNER), BF16),
        pltpu.VMEM((4, 16, 256), F32),
        pltpu.VMEM((4, 16, 256), BF16),
        pltpu.VMEM((4, 16, 256), BF16),
        pltpu.VMEM((16, 256), BF16),
        pltpu.VMEM((4, 16, 256), BF16),
        pltpu.VMEM((8, 16, 256), BF16),
        dma(12), dma(1), dma(2), dma(4), dma(4, 12),
    ]
    scratch += [dma(1), dma(8)] + [dma(1)] * 23
    scratch += [pltpu.SemaphoreType.REGULAR((ROUNDS,))]
    loss, both = pl.pallas_call(
        step_kernel,
        out_shape=(
            jax.ShapeDtypeStruct((1, 1), F32),
            jax.ShapeDtypeStruct((64, 2 * INNER), F32),
        ),
        in_specs=[hbm] * 12,
        out_specs=(vmem, vmem),
        scratch_shapes=scratch,
        compiler_params=pltpu.CompilerParams(
            collective_id=0, has_side_effects=True, vmem_limit_bytes=67043328
        ),
        name="forecast_step",
    )(
        sample_layer_feed[0],
        gain.reshape(1, D),
        w_query,
        w_key,
        w_value,
        w_out.T,
        readout_matrix,
        target,
        pixel_weight.reshape(1, TILE),
        pix_mask.reshape(PATCHES, TILE),
        neighbours,
        neighbour_mask,
    )
    both = both * 2.0
    return (loss.reshape(()), both[:, :INNER].T, both[:, INNER:])


def solution(mesh):
    in_specs = (
        P("ens", "pix", None),
        P(),
        P("ens", None),
        P("ens", None),
        P("ens", None),
        P(None, "ens"),
        P(),
        P("pix", None),
        P("pix"),
        P(),
        P("pix", None),
        P("pix", None),
    )
    out_specs = (P(), P(None, "ens"), P("ens", None))
    return jax.shard_map(
        per_device, mesh=mesh, in_specs=in_specs, out_specs=out_specs, check_vma=False
    )
```

```python
import math

import jax
import jax.numpy as jnp
from jax import lax
from jax.experimental import pallas as pl
from jax.experimental.pallas import tpu as pltpu
from jax.sharding import PartitionSpec as P

HEADS = 8
HD = 64
TILE = 128
NB = 9
D = 1024
INNER = 512
VARS = 128
MEMBERS = 16
PATCHES = 32
EPS = 1e-06
MESH = pl.DeviceIdType.MESH
F32 = jnp.float32
BF16 = jnp.bfloat16

KEY, QUERY, VALUE, OUT = 0, 1, 2, 3

ROUNDS = 7

FORECAST_ORDER = (5, 3, 7, 1, 4, 2, 6)

Y_FIRST = (0, 3,)

PLAN = (
    ("xrows", 0), ("own", 1), ("own", 2), ("own", 0), ("own", 3), ("xm", 1), ("f0", 0), ("xp", 1), ("xp", 2),
    ("word", 0), ("xm", 2), ("f1", 1), ("xm", 0), ("f0", 3), ("norm1", 0), ("slots", 0), ("xp", 0), ("f0", 1),
    ("n0", 0), ("f2", 1), ("h", 1), ("f2", 2), ("h", 2), ("f0", 2), ("norm2", 0), ("word", 1), ("n1", 1), ("n0", 3),
    ("f3", 1), ("n2", 1), ("norm0", 0), ("yp", 0), ("ym", 0), ("xm", 3), ("f1", 2), ("f3", 2), ("n0", 1), ("xp", 3),
    ("h", 0), ("ym", 3), ("yp", 3), ("n3", 1), ("yh", 0), ("n1", 2), ("n2", 2), ("n0", 2), ("Q", 0), ("n3", 2),
    ("h", 3), ("K", 0), ("yh", 3), ("word", 2), ("soft", 0), ("V", 0), ("mix", 0), ("word", 3), ("hid", 0),
)


def nt(a, b):
    return lax.dot_general(a, b, (((1,), (1,)), ((), ())), preferred_element_type=F32)


def mm(a, b):
    return jnp.dot(a, b, preferred_element_type=F32)


def step_kernel(
    x_hbm, gain_hbm, wq_hbm, wk_hbm, wv_hbm, wo_hbm, r_hbm, tgt_hbm, pw_hbm, pm_hbm, nbr_hbm, nbm_hbm,
    loss_ref, out_ref,
    gain_ref, tgt_ref, pw_ref, pm_ref, nbr_ref, nbm_ref,
    W, xw, R, nrm, nT, qs, ks, vs, wS, wT, att, dV,
    fa, gs, tots, mags, prods, lwc, lt, l1, lr, mz1, mz2, ms,
    S, Sr, SF, Ga, nTp, dVp, H, Rr, acc, z1s, z1r, z2s, z2b, fin,
    loc, xs, xr, ws, wr, fs, fr, br, ps, pr, rs, rr, lrs, lrr, z1ss, z1rs, z2ss, z2rs, l1s, l1r, l4s, l4r,
    z3s, z3r, srs, srr, sfs, sfr, pds, pdr, word,
):
    e = lax.axis_index("ens")
    t = lax.axis_index("pix")
    x = lax.div(e, 4)
    yh = lax.rem(lax.div(e, 2), 2)
    c = lax.rem(e, 2)
    yl = lax.div(t, 16)
    z = lax.rem(t, 16)
    zh = lax.div(z, 4)
    zl = lax.rem(z, 4)
    y = 2 * yh + yl

    def ens_of(xx, hh, cc):
        return xx * 4 + hh * 2 + cc

    def wrap(v, n):
        return lax.rem(v + 2 * n, n)

    def desc(src, dst, ss, rr_, dev):
        return pltpu.make_async_remote_copy(
            src_ref=src, dst_ref=dst, send_sem=ss, recv_sem=rr_, device_id=dev, device_id_type=MESH
        )

    def send(src, dst, ss, rr_, dev):
        desc(src, dst, ss, rr_, dev).start()

    def sent(ref, ss):
        desc(ref, ref, ss, ss, partner).wait_send()

    def received(ref, rr_):
        desc(ref, ref, rr_, rr_, partner).wait_recv()

    def chip(dx, dy):
        xx = wrap(x + dx, 4)
        yy = wrap(y + dy, 4)
        return xx, lax.div(yy, 2), lax.rem(yy, 2)

    def chip_dev(dx, dy):
        xx, hh, ll = chip(dx, dy)
        return (ens_of(xx, hh, c), ll * 16 + z)

    partner = (ens_of(x, yh, 1 - c), t)
    far = (ens_of(x, 1 - yh, c), (1 - yl) * 16 + z)
    near = (e, (1 - yl) * 16 + z)
    up = (e, wrap(t + 1, 32))
    down = (e, wrap(t - 1, 32))
    xplus = (ens_of(wrap(x + 1, 4), yh, c), t)
    xminus = (ens_of(wrap(x - 1, 4), yh, c), t)

    def ens_dev(dx, dh, dc):
        return (ens_of(wrap(x + dx, 4), wrap(yh + dh, 2), wrap(c + dc, 2)), t)

    def zl_dev(k, other=0):
        ll = wrap(yl + other, 2)
        return (e, ll * 16 + zh * 4 + wrap(zl + k, 4))

    def zh_dev(k):
        return (e, yl * 16 + wrap(zh + k, 4) * 4 + zl)

    links = (0, 1, 2, 1)
    chip_offsets = [(a, b) for a in range(4) for b in range(4) if (a, b) != (0, 0)]
    chip_offsets.sort(key=lambda o: -links[o[0]] - links[o[1]])

    plane_offsets = [(a, b, d) for a in range(4) for b in range(4) for d in range(2) if (a, b, d) != (0, 0, 0)]
    plane_offsets.sort(key=lambda o: -links[o[0]] - links[o[1]])

    def plane_dev(o):
        xx, hh, ll = chip(o[0], o[1])
        return (ens_of(xx, hh, wrap(c + o[2], 2)), ll * 16 + z)

    rows = pl.ds(pl.multiple_of(64 * e, 64), 64)
    loads = [
        pltpu.make_async_copy(x_hbm, xw.at[1], loc.at[0]),
        pltpu.make_async_copy(wk_hbm, W.at[KEY, rows, :], loc.at[1]),
        pltpu.make_async_copy(wq_hbm, W.at[QUERY, rows, :], loc.at[2]),
        pltpu.make_async_copy(wv_hbm, W.at[VALUE, rows, :], loc.at[3]),
        pltpu.make_async_copy(wo_hbm, W.at[OUT, rows, :], loc.at[4]),
        pltpu.make_async_copy(gain_hbm, gain_ref, loc.at[6]),
        pltpu.make_async_copy(r_hbm, R, loc.at[5]),
        pltpu.make_async_copy(tgt_hbm, tgt_ref, loc.at[7]),
        pltpu.make_async_copy(pw_hbm, pw_ref, loc.at[8]),
        pltpu.make_async_copy(pm_hbm, pm_ref, loc.at[9]),
        pltpu.make_async_copy(nbr_hbm, nbr_ref, loc.at[10]),
        pltpu.make_async_copy(nbm_hbm, nbm_ref, loc.at[11]),
    ]
    peers = [partner, xplus, xminus, far, near, up, down]
    barrier = pltpu.get_barrier_semaphore()
    for dev in peers:
        pl.semaphore_signal(barrier, inc=1, device_id=dev, device_id_type=MESH)
    for cp in loads:
        cp.start()
    for cp in loads[:5]:
        cp.wait()
    pl.semaphore_wait(barrier, len(peers))

    def tell(r):
        for dev in peers:
            pl.semaphore_signal(word.at[r], inc=1, device_id=dev, device_id_type=MESH)

    def hear(r):
        pl.semaphore_wait(word.at[r], len(peers))
        if r + 1 < ROUNDS:
            tell(r + 1)

    tell(0)

    def shard(g, ee, r0=0, n=64):
        return W.at[g, pl.ds(pl.multiple_of(64 * ee + r0, 32), n), :]

    def wsend(g, k, ref, dev):
        send(ref, ref, ws.at[g], wr.at[g, k], dev)

    def wwait(g, k, ref):
        received(ref, wr.at[g, k])

    mine = 32 * yl
    theirs = 32 * (1 - yl)
    cols = [x, wrap(x - 1, 4), wrap(x + 1, 4), wrap(x + 2, 4)]
    own_e = [ens_of(xx, yh, c) for xx in cols]
    far_e = [ens_of(xx, 1 - yh, c) for xx in cols]

    def own(g):
        wsend(g, 0, shard(g, own_e[0]), xplus)
        wsend(g, 1, shard(g, own_e[0]), xminus)
        wsend(g, 3, shard(g, own_e[0], mine, 32), far)
        wsend(g, 11, shard(g, own_e[0]), partner)

    def take(kind, g):
        yfirst = g in Y_FIRST
        if kind == "xm":
            wwait(g, 0, shard(g, own_e[1]))
            wsend(g, 2, shard(g, own_e[1], 0, 32), xplus)
            if not yfirst:
                wsend(g, 4, shard(g, own_e[1], mine, 32), far)
            wsend(g, 11, shard(g, own_e[1]), partner)
        elif kind == "xp":
            wwait(g, 1, shard(g, own_e[2]))
            wsend(g, 2, shard(g, own_e[2], 32, 32), xminus)
            if not yfirst:
                wsend(g, 5, shard(g, own_e[2], mine, 32), far)
            wsend(g, 11, shard(g, own_e[2]), partner)
        elif kind == "h":
            wwait(g, 2, shard(g, own_e[3]))
            if not yfirst:
                wsend(g, 6, shard(g, own_e[3], mine, 32), far)
            wsend(g, 11, shard(g, own_e[3]), partner)
        elif kind == "ym":
            wwait(g, 4, shard(g, far_e[1]))
            wsend(g, 6, shard(g, far_e[1], 0, 32), xplus)
            wsend(g, 11, shard(g, far_e[1]), partner)
        elif kind == "yp":
            wwait(g, 5, shard(g, far_e[2]))
            wsend(g, 6, shard(g, far_e[2], 32, 32), xminus)
            wsend(g, 11, shard(g, far_e[2]), partner)
        elif kind == "yh":
            wwait(g, 6, shard(g, far_e[3]))
            wsend(g, 11, shard(g, far_e[3]), partner)
        elif kind[0] == "f":
            i = int(kind[1])
            wwait(g, 3 + i, shard(g, far_e[i], theirs, 32))
            wsend(g, 7 + i, shard(g, far_e[i], theirs, 32), near)
        else:
            i = int(kind[1])
            wwait(g, 7 + i, shard(g, far_e[i], mine, 32))
            if yfirst:
                wsend(g, 4, shard(g, far_e[0]), xplus)
                wsend(g, 5, shard(g, far_e[0]), xminus)
            wsend(g, 11, shard(g, far_e[i]), partner)

    def whole_weight(g):
        received(W.at[g, pl.ds(0, 512), :], wr.at[g, 11])

    def neighbour_rows():
        @pl.when(t < PATCHES - 1)
        def _():
            send(xw.at[1], xw.at[0], xs.at[0], xr.at[0], up)

        @pl.when(t > 0)
        def _():
            send(xw.at[1], xw.at[2], xs.at[0], xr.at[1], down)

    def normalise(j):
        v = xw[j].astype(F32)
        inv = lax.rsqrt(jnp.mean(v * v, axis=-1, keepdims=True) + EPS)
        n = v * inv * gain_ref[...]
        nrm[128 * j : 128 * (j + 1), :] = n.astype(BF16)

    def transpose_normed(j):
        rows_t = nrm[128 * j : 128 * (j + 1), :].astype(F32).T.astype(BF16)
        nT[:, :, :, 128 * j : 128 * (j + 1)] = rows_t.reshape(8, 2, 64, 128)

    def own_rows():
        others_loaded()
        normalise(1)

    lane = lax.broadcasted_iota(jnp.int32, (1, 128), 1)

    def others_loaded():
        while len(loads) > 5:
            loads.pop().wait()

    state = {}

    def slots():
        others_loaded()
        counts = []
        live = []
        for j in range(3):
            n = jnp.int32(0)
            for s in range(NB):
                hit = (nbr_ref[0, s] == t - 1 + j) & (nbm_ref[0, s] > 0)
                n = n + jnp.where(hit, 1, 0)
            counts.append(n.astype(F32))
            row = jnp.clip(t - 1 + j, 0, PATCHES - 1)
            live.append((pm_ref[pl.ds(row, 1), :] > 0) & (n > 0))
        bias = jnp.concatenate([jnp.where(m, 0.0, -1e30) for m in live], axis=1)
        scale = jnp.concatenate([jnp.broadcast_to(n, (1, 128)) for n in counts], axis=1)
        own_mask = jnp.where(pm_ref[pl.ds(t, 1), :] > 0, 1.0, 0.0)
        lwc[...] = jnp.broadcast_to(pw_ref[...] * own_mask, (128, 128)).T
        state.update(bias=bias, scale=scale, counts=counts)

    def upper_rows():
        others_loaded()
        @pl.when(t > 0)
        def _():
            received(xw.at[0], xr.at[0])

        @pl.when(t == 0)
        def _():
            xw[0] = xw[1]

        normalise(0)

    def lower_rows():
        others_loaded()
        @pl.when(t < PATCHES - 1)
        def _():
            received(xw.at[2], xr.at[1])

        @pl.when(t == PATCHES - 1)
        def _():
            xw[2] = xw[1]

        normalise(2)

    def keys():
        whole_weight(KEY)
        ks[...] = mm(nrm[...], W[KEY]).astype(BF16)

    def queries():
        whole_weight(QUERY)
        qs[...] = mm(nrm[128:256, :], W[QUERY]).astype(BF16)

    def softmax():
        bias, scale = state["bias"], state["scale"]
        for h in range(HEADS):
            cs = slice(128 * (h // 2), 128 * (h // 2 + 1))
            q2 = qs[:, cs]
            inside = (lane >= 64) if h % 2 else (lane < 64)
            qh = jnp.where(inside, q2, jnp.zeros_like(q2))
            sc = nt(qh, ks[:, cs]) * HD ** (-0.5) + bias
            ex = jnp.exp(sc - jnp.max(sc, axis=-1, keepdims=True))
            wS[h] = (ex * (1.0 / jnp.sum(ex * scale, axis=-1, keepdims=True))).astype(BF16)

    def values():
        whole_weight(VALUE)
        vs[...] = mm(nrm[...], W[VALUE]).astype(BF16)

    def mix():
        counts = state["counts"]
        for pair in range(HEADS // 2):
            cs = slice(128 * pair, 128 * (pair + 1))
            mixed = []
            for half in range(2):
                out = jnp.zeros((128, 128), F32)
                for j in range(3):
                    js = slice(128 * j, 128 * (j + 1))
                    out = out + counts[j] * mm(wS[2 * pair + half, :, js], vs[js, cs])
                mixed.append(out)
            att[:, cs] = jnp.where(lane < 64, mixed[0], mixed[1]).astype(BF16)

    def predict():
        whole_weight(OUT)
        hidden = (xw[1].astype(F32) + nt(att[...], W[OUT])).astype(BF16)
        fa[0] = mm(hidden, R[...]).astype(BF16)

    computed = {
        "xrows": neighbour_rows,
        "norm1": own_rows,
        "slots": slots,
        "norm0": upper_rows,
        "norm2": lower_rows,
        "K": keys,
        "Q": queries,
        "soft": softmax,
        "V": values,
        "mix": mix,
        "hid": predict,
    }
    for kind, g in PLAN:
        if kind == "own":
            own(g)
        elif kind == "word":
            hear(g)
        elif kind in computed:
            computed[kind]()
        else:
            take(kind, g)

    send(fa.at[0], fa.at[8], fs.at[0], br.at[0], partner)
    for k in FORECAST_ORDER:
        send(fa.at[0], fa.at[k], fs.at[0], fr.at[k], ens_dev(k // 2, k % 2, 0))

    def hand_over(k):
        received(fa.at[k], fr.at[k])
        send(fa.at[k], fa.at[8 + k], fs.at[0], br.at[0], partner)

    def transpose_weights(h):
        wT[h] = wS[h].astype(F32).T.astype(BF16)

    def pair_terms(first, members):
        for i in range(4):
            rs_ = slice(32 * i, 32 * (i + 1))
            f = fa[0, rs_, :].astype(F32)
            if first:
                d = f - tgt_ref[rs_, :]
                ab = jnp.abs(d)
                gs[rs_, :] = jnp.tanh(d * 5.0)
                lt[rs_, :] = ab + 0.2 * jnp.log(1.0 + jnp.exp(-10.0 * ab))
                tot, mag, prod = jnp.zeros_like(f), jnp.zeros_like(f), jnp.ones_like(f)
            else:
                tot, mag, prod = tots[rs_, :], mags[rs_, :], prods[rs_, :]
            for k in members:
                d = f - fa[k, rs_, :].astype(F32)
                ab = jnp.abs(d)
                tot = tot + jnp.tanh(d * 5.0)
                mag = mag + ab
                prod = prod * (1.0 + jnp.exp(-10.0 * ab))
            tots[rs_, :], mags[rs_, :], prods[rs_, :] = tot, mag, prod

    for g in range(4):
        sent(W.at[g, pl.ds(0, 960), :], ws.at[g])
    inner = (t > 0) & (t < PATCHES - 1)

    @pl.when(inner)
    def _():
        sent(xw.at[pl.ds(0, 2)], xs.at[0])

    @pl.when(jnp.logical_not(inner))
    def _():
        sent(xw.at[0], xs.at[0])

    for j in range(3):
        transpose_normed(j)
    send(nT.at[:, 1 - c], nTp, ps.at[0], pr.at[0], partner)
    for i, k in enumerate(FORECAST_ORDER):
        hand_over(k)
        transpose_weights(i)
        if i == 3:
            hear(4)
    transpose_weights(7)
    pair_terms(True, range(1, 8))
    received(fa.at[pl.ds(0, 8)], br.at[0])
    pair_terms(False, range(8, 16))

    lw = lwc[...]
    mag = mags[...] + 0.2 * jnp.log(prods[...])
    terms = lw * (lt[...] - mag * (0.5 / (MEMBERS - 1)))
    l1[...] = jnp.sum(terms, axis=0, keepdims=True)
    factor = 1.0 / math.sqrt(MEMBERS * PATCHES * TILE)
    gs[...] = (lw * (gs[...] - tots[...] / (MEMBERS - 1)) * factor).astype(BF16).astype(F32)
    here = x * 4 + y
    mine_b = here * 2 + c
    for o in plane_offsets:
        send(l1, lr.at[mine_b], lrs.at[0], lrr.at[0], plane_dev(o))

    counts = state["counts"]
    gf = gs[...]
    gfb = gf.astype(BF16)
    gh = nt(gfb, R[...]).astype(BF16)
    ga = mm(gh, W[3]).astype(BF16)
    for pair in range(HEADS // 2):
        cs = slice(128 * pair, 128 * (pair + 1))
        g2 = ga[:, cs]
        a = mm(wT[2 * pair], g2)
        b = mm(wT[2 * pair + 1], g2)
        mixed = jnp.where(lane < 64, a, b)
        for j in range(3):
            dV[128 * j : 128 * (j + 1), cs] = (mixed[128 * j : 128 * (j + 1)] * counts[j]).astype(BF16)
    send(dV, dVp, pds.at[0], pdr.at[0], partner)
    gfT = gf.T.astype(BF16)
    st = mm(gfT, att[...])
    for r in range(8):
        for l in range(4):
            b = r * 4 + l
            S[b % 2, b // 2] = st[16 * r : 16 * (r + 1), 128 * l : 128 * (l + 1)].astype(BF16)
    for o in plane_offsets:
        xx, hh, ll = chip(o[0], o[1])
        part_s = S.at[wrap(c + o[2], 2), xx * 4 + hh * 2 + ll]
        send(part_s, Sr.at[o[0] * 8 + o[1] * 2 + o[2]], srs.at[0], srr.at[0], plane_dev(o))

    Ga[...] = mm(nT[:, c].reshape(512, 384), dV[...])
    hear(5)
    received(nTp, pr.at[0])
    received(dVp, pdr.at[0])
    both = Ga[...] + mm(nTp[...].reshape(512, 384), dVp[...])
    H[...] = both.astype(BF16).reshape(8, 2, 32, 512)
    for o in chip_offsets:
        xx, hh, ll = chip(*o)
        send(H.at[xx * 2 + hh, ll], Rr.at[o[0] * 4 + o[1]], rs.at[0], rr.at[0], chip_dev(*o))
    sent(fa.at[pl.ds(0, 15)], fs.at[0])

    received(lr.at[pl.ds(0, 31)], lrr.at[0])
    lr[mine_b] = l1[...]
    l3 = lr[0]
    for i in range(1, 32):
        l3 = l3 + lr[i]
    sm = S[c, here].astype(F32)
    received(Sr.at[pl.ds(1, 31)], srr.at[0])
    for k in range(1, 32):
        sm = sm + Sr[k].astype(F32)
    m3 = jnp.concatenate([sm, l3, jnp.zeros((7, 128), F32)], axis=0)
    ms[0] = m3
    for k in (1, 2, 3):
        send(ms.at[0], mz1.at[zl], l1s.at[0], l1r.at[0], zl_dev(k))
    sent(lr.at[pl.ds(0, 31)], lrs.at[0])
    received(mz1.at[pl.ds(0, 3)], l1r.at[0])
    mz1[zl] = m3
    m4 = ((mz1[0] + mz1[1]) + mz1[2]) + mz1[3]
    ms[1] = m4
    hear(6)
    for k in (1, 2, 3):
        send(ms.at[1], mz2.at[zh], l4s.at[0], l4r.at[0], zh_dev(k))

    total = H[x * 2 + yh, yl].astype(F32)
    received(Rr.at[pl.ds(1, 15)], rr.at[0])
    for k in range(1, 16):
        total = total + Rr[k].astype(F32)
    for i in range(4):
        a, b = i // 2, i % 2
        acc[i] = total[16 * a : 16 * (a + 1), 256 * b : 256 * (b + 1)]
    z1s[...] = acc[...].astype(BF16)
    for k in (1, 2, 3):
        send(z1s.at[wrap(zl + k, 4)], z1r.at[k], z1ss.at[0], z1rs.at[0], zl_dev(k))
    sent(nTp, ps.at[0])
    sent(dVp, pds.at[0])
    sent(Sr.at[pl.ds(1, 31)], srs.at[0])
    sent(mz1.at[pl.ds(0, 3)], l1s.at[0])
    part = acc[zl]
    received(z1r.at[pl.ds(1, 3)], z1rs.at[0])
    for k in (1, 2, 3):
        part = part + z1r[k].astype(F32)
    z2s[...] = part.astype(BF16)
    for k in (1, 2, 3):
        send(z2s, z2b.at[zh], z2ss.at[0], z2rs.at[0], zh_dev(k))
    received(mz2.at[pl.ds(0, 3)], l4r.at[0])
    mz2[zh] = m4
    m5 = ((mz2[0] + mz2[1]) + mz2[2]) + mz2[3]
    SF[mine_b] = m5[:16].astype(BF16)
    for o in plane_offsets:
        send(SF.at[mine_b], SF.at[mine_b], sfs.at[0], sfr.at[0], plane_dev(o))
    norm = 1.0 / (MEMBERS * PATCHES * TILE * VARS)
    loss_ref[...] = jnp.sum(jnp.sum(m5[16:], axis=0, keepdims=True), axis=1, keepdims=True) * norm
    sent(Rr.at[pl.ds(1, 15)], rs.at[0])
    sent(mz2.at[pl.ds(0, 3)], l4s.at[0])
    sent(z1r.at[pl.ds(1, 3)], z1ss.at[0])
    received(z2b.at[pl.ds(0, 3)], z2rs.at[0])
    z2b[zh] = z2s[...]
    whole = ((z2b[0].astype(F32) + z2b[1].astype(F32)) + z2b[2].astype(F32)) + z2b[3].astype(F32)
    spot = yl * 4 + zl
    fin[spot] = whole.astype(BF16)
    for other, k in [(0, 1), (0, 2), (0, 3), (1, 0), (1, 1), (1, 2), (1, 3)]:
        send(fin.at[spot], fin.at[spot], z3s.at[0], z3r.at[0], zl_dev(k, other))
    sent(z2b.at[pl.ds(0, 3)], z2ss.at[0])
    received(SF.at[pl.ds(0, 31)], sfr.at[0])
    full = jnp.concatenate(
        [jnp.concatenate([SF[r * 4 + l] for l in range(4)], axis=1) for r in range(8)], axis=0
    )
    out_ref[:, :512] = mm(R[rows, :], full) * 0.5
    sent(SF.at[pl.ds(0, 31)], sfs.at[0])
    received(fin.at[pl.ds(0, 7)], z3r.at[0])
    for i in range(8):
        r0 = 32 * (i // 4) + 16 * (i // 2 % 2)
        c0 = 256 * (i % 2)
        out_ref[r0 : r0 + 16, 512 + c0 : 768 + c0] = fin[i].astype(F32) * 0.5
    sent(fin.at[pl.ds(0, 7)], z3s.at[0])


def per_device(
    sample_layer_feed,
    gain,
    w_query,
    w_key,
    w_value,
    w_out,
    readout_matrix,
    target,
    pixel_weight,
    pix_mask,
    neighbours,
    neighbour_mask,
):
    hbm = pl.BlockSpec(memory_space=pltpu.HBM)
    vmem = pl.BlockSpec(memory_space=pltpu.VMEM)
    dma = lambda *n: pltpu.SemaphoreType.DMA(n)
    scratch = [
        pltpu.VMEM((1, D), F32),
        pltpu.VMEM((TILE, VARS), F32),
        pltpu.VMEM((1, TILE), F32),
        pltpu.VMEM((PATCHES, TILE), jnp.int32),
        pltpu.SMEM((1, NB), jnp.int32),
        pltpu.SMEM((1, NB), jnp.int32),
        pltpu.VMEM((4, D, INNER), BF16),
        pltpu.VMEM((3, TILE, D), BF16),
        pltpu.VMEM((D, VARS), BF16),
        pltpu.VMEM((3 * TILE, D), BF16),
        pltpu.VMEM((8, 2, 64, 3 * TILE), BF16),
        pltpu.VMEM((TILE, INNER), BF16),
        pltpu.VMEM((3 * TILE, INNER), BF16),
        pltpu.VMEM((3 * TILE, INNER), BF16),
        pltpu.VMEM((HEADS, TILE, 3 * TILE), BF16),
        pltpu.VMEM((HEADS, 3 * TILE, TILE), BF16),
        pltpu.VMEM((TILE, INNER), BF16),
        pltpu.VMEM((3 * TILE, INNER), BF16),
        pltpu.VMEM((16, 128, 128), BF16),
        pltpu.VMEM((128, 128), F32),
        pltpu.VMEM((128, 128), F32),
        pltpu.VMEM((128, 128), F32),
        pltpu.VMEM((128, 128), F32),
        pltpu.VMEM((128, 128), F32),
        pltpu.VMEM((128, 128), F32),
        pltpu.VMEM((1, 128), F32),
        pltpu.VMEM((32, 1, 128), F32),
        pltpu.VMEM((4, 24, 128), F32),
        pltpu.VMEM((4, 24, 128), F32),
        pltpu.VMEM((2, 24, 128), F32),
        pltpu.VMEM((2, 16, 16, 128), BF16),
        pltpu.VMEM((32, 16, 128), BF16),
        pltpu.VMEM((32, 16, 128), BF16),
        pltpu.VMEM((INNER, INNER), F32),
        pltpu.VMEM((8, 64, 3 * TILE), BF16),
        pltpu.VMEM((3 * TILE, INNER), BF16),
        pltpu.VMEM((8, 2, 32, INNER), BF16),
        pltpu.VMEM((16, 32, INNER), BF16),
        pltpu.VMEM((4, 16, 256), F32),
        pltpu.VMEM((4, 16, 256), BF16),
        pltpu.VMEM((4, 16, 256), BF16),
        pltpu.VMEM((16, 256), BF16),
        pltpu.VMEM((4, 16, 256), BF16),
        pltpu.VMEM((8, 16, 256), BF16),
        dma(12), dma(1), dma(2), dma(4), dma(4, 12),
    ]
    scratch += [dma(1), dma(8)] + [dma(1)] * 23
    scratch += [pltpu.SemaphoreType.REGULAR((ROUNDS,))]
    loss, both = pl.pallas_call(
        step_kernel,
        out_shape=(
            jax.ShapeDtypeStruct((1, 1), F32),
            jax.ShapeDtypeStruct((64, 2 * INNER), F32),
        ),
        in_specs=[hbm] * 12,
        out_specs=(vmem, vmem),
        scratch_shapes=scratch,
        compiler_params=pltpu.CompilerParams(
            collective_id=0, has_side_effects=True, vmem_limit_bytes=67043328
        ),
        name="forecast_step",
    )(
        sample_layer_feed[0],
        gain.reshape(1, D),
        w_query,
        w_key,
        w_value,
        w_out.T,
        readout_matrix,
        target,
        pixel_weight.reshape(1, TILE),
        pix_mask.reshape(PATCHES, TILE),
        neighbours,
        neighbour_mask,
    )
    both = both * 2.0
    return (loss.reshape(()), both[:, :INNER].T, both[:, INNER:])


def solution(mesh):
    in_specs = (
        P("ens", "pix", None),
        P(),
        P("ens", None),
        P("ens", None),
        P("ens", None),
        P(None, "ens"),
        P(),
        P("pix", None),
        P("pix"),
        P(),
        P("pix", None),
        P("pix", None),
    )
    out_specs = (P(), P(None, "ens"), P("ens", None))
    return jax.shard_map(
        per_device, mesh=mesh, in_specs=in_specs, out_specs=out_specs, check_vma=False
    )
```
